256 devices in a mesh: rows: 8 (over z), cols: 32 (over y, x, core).
Axes of the slice: x: 4, y: 4, z: 8, core: 2. Of those that a mesh axis runs over, the one named last changes fastest.
Arguments:
- whitened: float32 [3, 1048576], P(None, ('rows', 'cols')), may hold values from -6 to 6
- cotangent: bfloat16 [64, 1048576], P(None, ('rows', 'cols')), may hold values from -6 to 6
- lift_weight: float32 [64, 3], replicated, may hold values from -3.5 to 3.5
- conv_now: bfloat16 [3, 128, 64], replicated, may hold values from -0.5 to 0.5
- conv_past: bfloat16 [3, 128, 64], replicated, may hold values from -0.5 to 0.5
- mix_weight: bfloat16 [3, 64, 64], replicated, may hold values from -0.75 to 0.75
- dilations: int32 [3], replicated, may hold values from 64 to 256, as said below
- psd_bin: int32 [4096, 32, 8], P(None, 'cols', 'rows'), may hold values from 0 to 1023, as said below
- psd_weight: float32 [2, 1024], replicated, may hold values from 0.2 to 5
Outputs:
- data_grad: float32 [3, 1048576], P(None, ('rows', 'cols'))
- grad_now: float32 [3, 128, 64], replicated
- grad_past: float32 [3, 128, 64], replicated
- grad_mix: float32 [3, 64, 64], replicated
- grad_lift: float32 [64, 3], replicated
The draws below stay inside these ranges and needn't reach their ends.
Inputs may be any that keep to these rules, and one draw needn't show every extreme that they name: `dilations`: multiples of 4; one layer has 64, one has 256. `psd_bin`: frequencies k and 1048576 - k have the same bin.
All inputs are finite; a program needn't handle non-finite values.
Results may differ from the reference program's by a relative error of at most 0.0068.
Values may be sent and summed in bfloat16 or wider, within the bound.
No kernel may reach another device: no remote copies, remote signals or barrier semaphores. Data moves between devices by JAX's collectives and lax.ppermute only.
A program may use at most 64 MiB of HBM per device.

```python
import math
import jax
import jax.numpy as jnp
from jax import lax

C = 64
LAYERS = 3
DMAX = 256
NBINS = 1024
SEG = 4096
ROW_BLOCKS = 8
COL_BLOCKS = 32
LEN = 1048576


def draw_dilations(key, part):
    middle_key = jax.random.fold_in(key, 11)
    order_key = jax.random.fold_in(key, 23)
    middle = 4 * jax.random.randint(middle_key, (), DMAX // 16, DMAX // 4 + 1, dtype=jnp.int32)
    levels = jnp.stack([jnp.int32(DMAX // 4), middle, jnp.int32(DMAX)]).astype(jnp.int32)
    return jax.random.permutation(order_key, levels)


def draw_psd_bin(key, part):
    length_all = SEG * ROW_BLOCKS * COL_BLOCKS
    raw_bins = jax.random.randint(key, (length_all,), 0, NBINS, dtype=jnp.int32)
    raw_bins = raw_bins.at[1].set(NBINS - 1).at[2].set(0)
    position = jnp.arange(length_all, dtype=jnp.int32)
    mirror = jnp.minimum(position, (length_all - position) % length_all)
    return raw_bins[mirror].reshape(SEG, COL_BLOCKS, ROW_BLOCKS)


def steps_of(key, extent, cuts, low, top_value):
    def one(axis_at, parts):
        draws = jax.random.uniform(jax.random.fold_in(jax.random.fold_in(key, 6), axis_at), (parts,), jnp.float32, low / len(cuts), top_value / len(cuts))
        return jnp.repeat(jnp.exp(draws), extent[axis_at] // parts).reshape((-1,) + (1,) * (len(extent) - axis_at - 1))

    gain = one(*cuts[0])
    for cut in cuts[1:]:
        gain = gain * one(*cut)
    return gain


def scatter_about(key, dims, scale, limit, split=(), held_as=jnp.bfloat16):
    level = steps_of(key, dims, split, -0.22, 0.18) if split else 1.0
    values = jax.random.normal(key, dims, jnp.float32) * scale * level
    return jnp.minimum(jnp.maximum(values, -limit), limit).astype(held_as)


def setup_inputs(seed: int = 0) -> dict:
    seeds = jax.random.split(jax.random.key(seed), 10)
    whitened = scatter_about(seeds[0], (3, LEN), 1.0, 6.0, ((1, 256),), jnp.float32)
    cotangent = scatter_about(seeds[1], (C, LEN), 1.0, 6.0, ((1, 256),))
    lift_weight = scatter_about(seeds[2], (C, 3), 3 ** -0.5, 3.5, (), jnp.float32)
    conv_now = scatter_about(seeds[3], (LAYERS, 2 * C, C), (2 * C) ** -0.5, 0.5)
    conv_past = scatter_about(seeds[4], (LAYERS, 2 * C, C), (2 * C) ** -0.5, 0.5)
    mix_weight = scatter_about(seeds[5], (LAYERS, C, C), C ** -0.5, 0.75)
    dilations = draw_dilations(jax.random.fold_in(seeds[9], 71), 0)
    psd_bin = draw_psd_bin(jax.random.fold_in(seeds[9], 71), 0)
    psd_weight = jnp.clip(jnp.exp(jax.random.uniform(seeds[8], (2, NBINS), jnp.float32, math.log(0.2), math.log(5.0))), 0.2, 5.0)
    return dict(whitened=whitened, cotangent=cotangent, lift_weight=lift_weight, conv_now=conv_now, conv_past=conv_past, mix_weight=mix_weight, dilations=dilations, psd_bin=psd_bin, psd_weight=psd_weight)


def lifted(lift_weight, inputs):
    return lift_weight[:, 0:1] * inputs[0:1] + lift_weight[:, 1:2] * inputs[1:2] + lift_weight[:, 2:3] * inputs[2:3]

def delayed(field_b, delay):
    joined = jnp.concatenate([jnp.zeros((field_b.shape[0], DMAX), field_b.dtype), field_b], axis=1)
    return lax.dynamic_slice_in_dim(joined, (DMAX - delay).astype(jnp.int32), field_b.shape[1], 1)

def advanced(values, delay, head_rim):
    joined = jnp.concatenate([values, head_rim], axis=1)
    return lax.dynamic_slice_in_dim(joined, delay.astype(jnp.int32), values.shape[1], 1)

def block_grads(window, cot_block, heads, lift_weight, conv_now, conv_past, mix_weight, dilations):
    channel_count = mix_weight.shape[1]
    margin = 3 * DMAX
    field_now = lifted(lift_weight, window)
    saved = []
    for layer_id in range(LAYERS):
        field_b = field_now.astype(jnp.bfloat16)
        past_b = delayed(field_b, dilations[layer_id])
        pre_act = jnp.dot(conv_now[layer_id], field_b, preferred_element_type=jnp.float32) + jnp.dot(conv_past[layer_id], past_b, preferred_element_type=jnp.float32)
        tanh_part = jnp.tanh(pre_act[:channel_count])
        sigm_part = jax.nn.sigmoid(pre_act[channel_count:])
        gate_b = (tanh_part * sigm_part).astype(jnp.bfloat16)
        saved.append((field_b[:, margin:], past_b[:, margin:], tanh_part[:, margin:], sigm_part[:, margin:], gate_b[:, margin:]))
        field_now = field_now + jnp.dot(mix_weight[layer_id], gate_b, preferred_element_type=jnp.float32)
    grad_field = cot_block.astype(jnp.float32)
    grads_now = [None] * LAYERS
    grads_past = [None] * LAYERS
    grads_mix = [None] * LAYERS
    new_heads = [None] * LAYERS
    for layer_id in reversed(range(LAYERS)):
        field_b, past_b, tanh_part, sigm_part, gate_b = saved[layer_id]
        grad_field_b = grad_field.astype(jnp.bfloat16)
        grad_gate = jnp.dot(mix_weight[layer_id].T, grad_field_b, preferred_element_type=jnp.float32)
        grads_mix[layer_id] = jnp.dot(grad_field_b, gate_b.T, preferred_element_type=jnp.float32)
        grad_pre = jnp.concatenate([grad_gate * sigm_part * (1.0 - tanh_part * tanh_part), grad_gate * tanh_part * sigm_part * (1.0 - sigm_part)], axis=0).astype(jnp.bfloat16)
        grads_now[layer_id] = jnp.dot(grad_pre, field_b.T, preferred_element_type=jnp.float32)
        grads_past[layer_id] = jnp.dot(grad_pre, past_b.T, preferred_element_type=jnp.float32)
        ahead_term = jnp.dot(conv_past[layer_id].T, grad_pre, preferred_element_type=jnp.float32)
        new_heads[layer_id] = ahead_term[:, :DMAX]
        grad_field = grad_field + jnp.dot(conv_now[layer_id].T, grad_pre, preferred_element_type=jnp.float32) + advanced(ahead_term, dilations[layer_id], heads[layer_id])
    own_input = window[:, margin:]
    input_grad = jnp.dot(lift_weight.T, grad_field, precision=lax.Precision.HIGHEST)
    lift_part = jnp.dot(grad_field, own_input.T, precision=lax.Precision.HIGHEST)
    return (input_grad, jnp.stack(grads_now), jnp.stack(grads_past), jnp.stack(grads_mix), lift_part, tuple(new_heads))

def reference(whitened, cotangent, lift_weight, conv_now, conv_past, mix_weight, dilations, psd_bin, psd_weight):
    channel_count = mix_weight.shape[1]
    block_count = LEN // SEG
    margin = 3 * DMAX
    padded = jnp.concatenate([jnp.zeros((3, margin), whitened.dtype), whitened], axis=1)

    def step_block(carry, block_id):
        heads, sum_now, sum_past, sum_mix, sum_lift = carry
        start_at = (block_id * SEG).astype(jnp.int32)
        window = lax.dynamic_slice_in_dim(padded, start_at, margin + SEG, 1)
        cot_block = lax.dynamic_slice_in_dim(cotangent, start_at, SEG, 1)
        input_grad, part_now, part_past, part_mix, part_lift, new_heads = block_grads(window, cot_block, heads, lift_weight, conv_now, conv_past, mix_weight, dilations)
        return ((new_heads, sum_now + part_now, sum_past + part_past, sum_mix + part_mix, sum_lift + part_lift), input_grad)
    start_heads = tuple((jnp.zeros((channel_count, DMAX), jnp.float32) for layer_id in range(LAYERS)))
    start_carry = (start_heads, jnp.zeros((LAYERS, 2 * channel_count, channel_count), jnp.float32), jnp.zeros((LAYERS, 2 * channel_count, channel_count), jnp.float32), jnp.zeros((LAYERS, channel_count, channel_count), jnp.float32), jnp.zeros((channel_count, 3), jnp.float32))
    final_carry, pieces = lax.scan(step_block, start_carry, jnp.arange(block_count, dtype=jnp.int32), reverse=True)
    input_grad = jnp.transpose(pieces, (1, 0, 2)).reshape(3, LEN)
    scaling = 1.0 / jnp.sqrt(jnp.float32(LEN))
    bins_flat = psd_bin.reshape(-1)
    weights = psd_weight[:, bins_flat]
    factors = jnp.stack([weights[0], weights[0], weights[1]])
    spectrum = jnp.fft.fft(input_grad, axis=1)
    data_grad = jnp.real(jnp.fft.ifft(spectrum * factors, axis=1)).astype(jnp.float32)
    return (data_grad, final_carry[1] * scaling, final_carry[2] * scaling, final_carry[3] * scaling, final_carry[4] * scaling)
```

```python
import functools
import math

import jax
import jax.numpy as jnp
import numpy as np
from jax import lax
from jax.experimental import pallas as pl
from jax.experimental.pallas import tpu as pltpu
from jax.sharding import PartitionSpec as P

F32 = jnp.float32
BF16 = jnp.bfloat16
BOTH = ("rows", "cols")
RIM = 640
BASE = 1024
SEG = 4096
WIDE = BASE + SEG + 1024
STEP = 512
LANES = 128


def lane_ids(rows):
    return lax.broadcasted_iota(jnp.int32, (rows, LANES), 1)


def dot32(a, b):
    return jnp.dot(a, b, preferred_element_type=F32)


def dot_nt(a, b, precision=None):
    return lax.dot_general(
        a, b, (((1,), (1,)), ((), ())), preferred_element_type=F32, precision=precision
    )


def columns(start, width):
    return pl.ds(pl.multiple_of(start, LANES), width)


def conv_kernel(
    dil, wh, wh_left, wh_right, cot, cot_right, lift, lift_rows, w_cat, w_cat_t, mix, mix_t,
    sent, late, f0, f1, f2, x1, x2, fl1, fl2, sg1, sg2, gt1, gt2, ah, ah2, dp, dp2,
    g_conv, g_mix, g_lift, x_t,
):
    lane = lane_ids(64)

    def split(layer):
        d = dil[layer]
        return pl.multiple_of((d // LANES) * LANES, LANES), d % LANES

    def behind(ref, start, width, layer):
        whole, rest = split(layer)
        first = start - whole - LANES
        turned = [
            pltpu.roll(ref[:, columns(first + LANES * k, LANES)], rest, 1)
            for k in range(width // LANES + 1)
        ]
        keep = lane < rest
        return jnp.concatenate(
            [jnp.where(keep, turned[k], turned[k + 1]) for k in range(width // LANES)], axis=1
        )

    def beyond(ref, start, width, layer):
        whole, rest = split(layer)
        first = start + whole
        back = (LANES - rest) % LANES
        turned = [
            pltpu.roll(ref[:, columns(first + LANES * k, LANES)], back, 1)
            for k in range(width // LANES + 1)
        ]
        keep = lane < LANES - rest
        return jnp.concatenate(
            [jnp.where(keep, turned[k], turned[k + 1]) for k in range(width // LANES)], axis=1
        )

    lift_cols = [jnp.broadcast_to(lift[:, i : i + 1], (64, LANES)) for i in range(3)]

    def lift_tile(src, at, dst_at):
        tile = src[:, columns(at, LANES)]
        f0[:, columns(dst_at, LANES)] = (
            lift_cols[0] * tile[0:1] + lift_cols[1] * tile[1:2] + lift_cols[2] * tile[2:3]
        )

    zero_tile = jnp.zeros((64, LANES), F32)
    for k in range(3):
        f0[:, k * LANES : (k + 1) * LANES] = zero_tile
    f1[:, 384:512] = zero_tile
    f2[:, 640:768] = zero_tile
    for k in range(RIM // LANES):
        lift_tile(wh_left, k * LANES, BASE - RIM + k * LANES)
        lift_tile(wh_right, k * LANES, BASE + SEG + k * LANES)

    def lift_step(i, carry):
        for k in range(4):
            lift_tile(wh, (i * 4 + k) * LANES, BASE + (i * 4 + k) * LANES)
        return carry

    lax.fori_loop(0, SEG // (4 * LANES), lift_step, 0)
    for k in range(3):
        at = BASE + SEG + RIM + k * LANES
        ah[:, at : at + LANES] = zero_tile
        ah2[:, at : at + LANES] = zero_tile
        ah2[:, at - LANES : at] = zero_tile

    def gates(layer, field, start, width):
        now = field[:, columns(start, width)]
        both = jnp.concatenate(
            [now.astype(BF16), behind(field, start, width, layer).astype(BF16)], axis=0
        )
        pre = dot32(w_cat[layer], both)
        filt = jnp.tanh(pre[:64])
        sig = 0.5 * jnp.tanh(0.5 * pre[64:]) + 0.5
        gate = (filt * sig).astype(BF16)
        return now, both, filt, sig, gate

    def forward(layer, field, field_next, x, fl, sg, gt, start, width):
        now, both, filt, sig, gate = gates(layer, field, start, width)
        at = columns(start, width)
        x[:, at] = both
        fl[:, at] = filt
        sg[:, at] = sig
        gt[:, at] = gate
        field_next[:, at] = now + dot32(mix[layer], gate)

    def run_forward(layer, field, field_next, x, fl, sg, gt, left):
        forward(layer, field, field_next, x, fl, sg, gt, BASE - left, left)

        def step(i, carry):
            forward(layer, field, field_next, x, fl, sg, gt, BASE + i * STEP, STEP)
            return carry

        lax.fori_loop(0, SEG // STEP, step, 0)
        forward(layer, field, field_next, x, fl, sg, gt, BASE + SEG, RIM)

    run_forward(0, f0, f1, x1, fl1, sg1, gt1, 512)
    run_forward(1, f1, f2, x2, fl2, sg2, gt2, 256)

    g_conv[...] = jnp.zeros_like(g_conv)
    g_mix[...] = jnp.zeros_like(g_mix)

    def backward(layer, dfield, dfield_b, both, filt, sig, gate, ah_out, dp_out, start, width, own):
        d_gate = dot32(mix_t[layer], dfield_b)
        d_pre = jnp.concatenate(
            [d_gate * sig * (1.0 - filt * filt), d_gate * filt * sig * (1.0 - sig)], axis=0
        ).astype(BF16)
        back = dot32(w_cat_t[layer], d_pre)
        at = columns(start, width)
        dp_out[:, at] = dfield + back[:64]
        ah_out[:, at] = back[64:]
        if own:
            g_conv[layer] += dot_nt(d_pre, both)
            g_mix[layer] += dot_nt(
                dfield_b, jnp.concatenate([jnp.zeros((64, width), BF16), gate], axis=0)
            )

    def last_layer(start, width, cot_ref, cot_at, own):
        now, both, filt, sig, gate = gates(2, f2, start, width)
        dfield_b = cot_ref[:, columns(cot_at, width)]
        backward(2, dfield_b.astype(F32), dfield_b, both, filt, sig, gate, ah, dp, start, width, own)

    def step3(i, carry):
        last_layer(BASE + i * STEP, STEP, cot, i * STEP, True)
        return carry

    lax.fori_loop(0, SEG // STEP, step3, 0)
    last_layer(BASE + SEG, RIM, cot_right, 0, False)

    def saved_layer(layer, x, fl, sg, gt, ah_in, dp_in, ah_out, dp_out, start, width, own):
        at = columns(start, width)
        dfield = dp_in[:, at] + beyond(ah_in, start, width, layer + 1)
        backward(
            layer, dfield, dfield.astype(BF16), x[:, at], fl[:, at], sg[:, at], gt[:, at],
            ah_out, dp_out, start, width, own,
        )

    def step2(i, carry):
        saved_layer(1, x2, fl2, sg2, gt2, ah, dp, ah2, dp2, BASE + i * STEP, STEP, True)
        return carry

    lax.fori_loop(0, SEG // STEP, step2, 0)
    saved_layer(1, x2, fl2, sg2, gt2, ah, dp, ah2, dp2, BASE + SEG, 512, False)

    def step1(i, carry):
        saved_layer(0, x1, fl1, sg1, gt1, ah2, dp2, ah, dp, BASE + i * STEP, STEP, True)
        return carry

    lax.fori_loop(0, SEG // STEP, step1, 0)
    saved_layer(0, x1, fl1, sg1, gt1, ah2, dp2, ah, dp, BASE + SEG, 256, False)

    x_t[...] = jnp.zeros_like(x_t)
    g_lift[...] = jnp.zeros_like(g_lift)
    row_of = lax.broadcasted_iota(jnp.int32, (64, 64), 0) % 16
    rows_all = lift_rows[...]

    def step0(i, carry):
        start = BASE + i * 256
        dfield = dp[:, columns(start, 256)] + beyond(ah, start, 256, 0)
        placed = jnp.where(row_of == i, rows_all, 0.0)
        x_t[0:64] += lax.dot(
            placed, dfield, precision=lax.Precision.HIGHEST, preferred_element_type=F32
        )
        seen = jnp.concatenate(
            [jnp.zeros((64, 256), F32), wh[:, columns(i * 256, 256)], jnp.zeros((56, 256), F32)],
            axis=0,
        )
        g_lift[...] += dot_nt(dfield, seen, lax.Precision.HIGHEST)
        return carry

    lax.fori_loop(0, 16, step0, 0)

    low = lane_ids(256) < 64
    early = jnp.concatenate([g_conv[2], g_mix[1], g_lift[...]], axis=0)
    sent[:, 0, 0:128] = jnp.where(low, x_t[...].T, early)
    sent[:, 0, 128:256] = jnp.concatenate([g_conv[0], g_conv[1]], axis=0)
    late[...] = jnp.concatenate([pltpu.roll(g_conv[2], 64, 1), g_mix[0], g_mix[2]], axis=0)


def swap(x):
    first = (lane_ids(x.shape[0]) // 16) % 2 == 0
    return jnp.where(first, pltpu.roll(x, LANES - 16, 1), -pltpu.roll(x, 16, 1))


def wide_dot(table, x, sign):
    low = lane_ids(256) < 64
    parts = []
    for value in (x, sign * swap(x)):
        high = value.astype(BF16)
        rest = value - high.astype(F32)
        parts.append((high, jnp.where(low, high.astype(F32), pltpu.roll(rest, 64, 1)).astype(BF16)))
    mixed = dot32(table[0], jnp.concatenate([parts[0][1], parts[1][1]], axis=0))
    small = dot32(table[1], jnp.concatenate([parts[0][0], parts[1][0]], axis=0))
    return mixed + pltpu.roll(mixed, 64, 1) + small


def first_kernel(got, late, table, twist_cos, twist_sin, inner, sent, sums):
    data = got[:, 0, 0:128]
    rest = got[:, 0, 128:256]
    low = lane_ids(256) < 64
    x = jnp.where(low, data, 0.0)
    sums[:, 0:128] = jnp.broadcast_to(jnp.sum(data, axis=0, keepdims=True), (8, 128))
    sums[:, 128:256] = jnp.broadcast_to(jnp.sum(rest, axis=0, keepdims=True), (8, 128))
    y = wide_dot(table, x, 1.0)
    y = y * twist_cos[...] + swap(y) * twist_sin[...]
    y = lax.dot(y, inner[...], precision=lax.Precision.HIGHEST, preferred_element_type=F32)
    sent[:, 0, :] = jnp.where(low, y, late[...])


def middle_kernel(got, sums, weights, table, sent, sums_late):
    data = got[:, 0, :]
    low = lane_ids(256) < 64
    x = jnp.where(low, data, 0.0)
    sums_late[...] = jnp.broadcast_to(jnp.sum(data, axis=0, keepdims=True), (8, 128))
    y = wide_dot(table, x, 1.0)
    y = jnp.where(low, y * weights[...], 0.0)
    y = wide_dot(table, y, -1.0)
    sent[:, 0, 0:128] = jnp.where(low, y, jnp.broadcast_to(sums[0:1, 0:128], (256, 128)))
    sent[:, 0, 128:256] = jnp.broadcast_to(sums[0:1, 128:256], (256, 128))


def third_kernel(got, sums_late, table, twist_cos, twist_sin, inner, sent):
    low = lane_ids(256) < 64
    x = jnp.where(low, got[:, 0, 0:128], 0.0)
    y = dot_nt(x, inner[...], lax.Precision.HIGHEST)
    y = y * twist_cos[...] - swap(y) * twist_sin[...]
    y = wide_dot(table, y, -1.0)
    sent[:, 0, :] = jnp.where(low, y, jnp.broadcast_to(sums_late[0:1], (256, 128)))


def last_kernel(scaling, got, got_before, data_grad, grad_now, grad_past, grad_mix, grad_lift):
    last = got[:, 0, :]
    turned = last.T
    for channel in range(3):
        for m in range(16):
            row = channel * 16 + m
            data_grad[channel : channel + 1, m * 256 : (m + 1) * 256] = turned[row : row + 1]
    late = pltpu.roll(last, 64, 1) * scaling
    early = pltpu.roll(got_before[:, 0, 0:128], 64, 1) * scaling
    main = got_before[:, 0, 128:256] * scaling
    main_past = pltpu.roll(main, 64, 1)
    for layer in range(2):
        grad_now[layer] = main[layer * 128 : (layer + 1) * 128, 0:64]
        grad_past[layer] = main_past[layer * 128 : (layer + 1) * 128, 0:64]
    grad_now[2] = late[0:128, 0:64]
    grad_past[2] = early[0:128, 0:64]
    grad_mix[0] = late[128:192, 0:64]
    grad_mix[1] = early[128:192, 0:64]
    grad_mix[2] = late[192:256, 0:64]
    grad_lift[...] = early[192:256, 0:3]


def weight_kernel(bins, psd, out):
    at = bins[...]
    high = at // LANES
    low = at % LANES
    second = lane_ids(256) >= 32
    total = jnp.zeros((256, LANES), F32)
    for h in range(8):
        rows = [
            jnp.take_along_axis(
                jnp.broadcast_to(psd[8 * j + h : 8 * j + h + 1, :], (256, LANES)), low, axis=1
            )
            for j in range(2)
        ]
        total = jnp.where(high == h, jnp.where(second, rows[1], rows[0]), total)
    out[...] = total


def call(kernel, outs, scratch=(), smem=0, n_in=0):
    vmem = pl.BlockSpec(memory_space=pltpu.VMEM)
    in_specs = [pl.BlockSpec(memory_space=pltpu.SMEM)] * smem + [vmem] * n_in
    out_shape = [jax.ShapeDtypeStruct(shape, F32) for shape in outs]
    return pl.pallas_call(
        kernel,
        out_shape=out_shape,
        in_specs=in_specs,
        out_specs=[vmem] * len(outs),
        scratch_shapes=list(scratch),
        compiler_params=pltpu.CompilerParams(vmem_limit_bytes=56 * 1024 * 1024),
    )


def two_parts(table):
    high = table.astype(jnp.bfloat16)
    low = (table - high.astype(np.float32)).astype(jnp.bfloat16)
    return np.stack([high, low])


def tables(rows_count, cols_count):
    n = rows_count * cols_count
    ids = np.arange(n)
    residue = rows_count * (ids % cols_count) + ids // cols_count

    def pair(product):
        angle = 2.0 * np.pi / n * (product % n)
        return two_parts(
            np.concatenate([np.cos(angle), np.sin(angle)], axis=1).astype(np.float32)
        )

    outward = pair(residue[:, None] * ids[None, :])
    plain = pair(ids[:, None] * ids[None, :])
    inward = pair(ids[:, None] * residue[None, :])
    return residue, outward, plain, inward


def exchange(x):
    return lax.all_to_all(x, BOTH, split_axis=0, concat_axis=0, tiled=True)


def local(
    rows_count, cols_count,
    whitened, cotangent, lift_weight, conv_now, conv_past, mix_weight, dilations, psd_bin, psd_weight,
):
    n = rows_count * cols_count
    total = n * SEG
    me = lax.axis_index("rows") * cols_count + lax.axis_index("cols")
    up = [(i, i + 1) for i in range(n - 1)]
    down = [(i + 1, i) for i in range(n - 1)]
    wh = jnp.pad(whitened, ((0, 5), (0, 0)))
    wh_left = lax.ppermute(wh[:, SEG - RIM :], BOTH, up)
    cot_right = lax.ppermute(cotangent[:, :RIM], BOTH, down)
    wh_right = lax.ppermute(wh[:, :RIM], BOTH, down)

    residue, outward, plain, inward = tables(rows_count, cols_count)
    m_ids = np.tile(np.arange(16), 4)
    r_ids = jnp.asarray(residue, jnp.int32)
    angle = (2.0 * math.pi / total) * (
        r_ids[:, None] * (256 * jnp.asarray(m_ids, jnp.int32)[None, :] + me)
    ).astype(F32)
    twist_cos = jnp.pad(jnp.cos(angle), ((0, 0), (0, 64)))
    twist_sin = jnp.pad(jnp.sin(angle), ((0, 0), (0, 64)))
    row = np.arange(LANES)
    same = (row[:, None] // 32 == row[None, :] // 32) & (row[:, None] < 64) & (row[None, :] < 64)
    part_in, part_out = (row // 16) % 2, (row // 16) % 2
    alike = same & (part_in[:, None] == part_out[None, :])
    sign = np.where(part_in[:, None] > part_out[None, :], 1.0, -1.0) * (same & ~alike)
    phase = (2.0 * math.pi / SEG) * (
        (jnp.asarray(row % 16, jnp.int32)[None, :]
         * (256 * jnp.asarray(row % 16, jnp.int32)[:, None] + me)) % SEG
    ).astype(F32)
    inner = jnp.cos(phase) * alike.astype(np.float32) + jnp.sin(phase) * sign.astype(np.float32)

    bins = psd_bin.reshape(256, 16)
    bins = jnp.concatenate([bins, bins, bins, bins, jnp.zeros((256, 64), jnp.int32)], axis=1)
    weights = call(weight_kernel, [(256, LANES)], n_in=2)(
        bins, (psd_weight * (1.0 / total)).reshape(16, LANES)
    )[0]

    w_cat = jnp.concatenate([conv_now, conv_past], axis=2)
    w_cat_t = jnp.swapaxes(w_cat, 1, 2)
    mix_t = jnp.swapaxes(mix_weight, 1, 2)
    lift_rows = jnp.pad(jnp.repeat(lift_weight.T, 16, axis=0), ((0, 16), (0, 0)))
    big = lambda rows, dtype: pltpu.VMEM((rows, WIDE), dtype)
    scratch = (
        [big(64, F32)] * 3 + [big(128, BF16)] * 2 + [big(64, F32)] * 4 + [big(64, BF16)] * 2
        + [big(64, F32)] * 4
        + [
            pltpu.VMEM((3, 128, 128), F32), pltpu.VMEM((3, 64, 128), F32),
            pltpu.VMEM((64, 128), F32), pltpu.VMEM((128, 256), F32),
        ]
    )
    sent, late = call(conv_kernel, [(n, 1, 256), (n, LANES)], scratch, smem=1, n_in=11)(
        dilations, wh, wh_left, wh_right, cotangent, cot_right, lift_weight, lift_rows,
        w_cat, w_cat_t, mix_weight, mix_t,
    )
    got = exchange(sent)
    sent, sums = call(first_kernel, [(n, 1, LANES), (8, 256)], n_in=6)(
        got, late, outward, twist_cos, twist_sin, inner
    )
    got = exchange(sent)
    sent, sums_late = call(middle_kernel, [(n, 1, 256), (8, LANES)], n_in=4)(
        got, sums, weights, plain
    )
    before = exchange(sent)
    sent, = call(third_kernel, [(n, 1, LANES)], n_in=6)(
        before, sums_late, inward, twist_cos, twist_sin, inner
    )
    got = exchange(sent)
    outs = [(3, SEG), (3, 128, 64), (3, 128, 64), (3, 64, 64), (64, 3)]
    return tuple(
        call(functools.partial(last_kernel, total ** -0.5), outs, n_in=2)(got, before)
    )


def solution(mesh):
    in_specs = (
        P(None, BOTH), P(None, BOTH), P(), P(), P(), P(), P(), P(None, "cols", "rows"), P(),
    )
    out_specs = (P(None, BOTH), P(), P(), P(), P())
    body = functools.partial(local, mesh.shape["rows"], mesh.shape["cols"])
    return jax.shard_map(body, mesh=mesh, in_specs=in_specs, out_specs=out_specs, check_vma=False)
```

```python
import functools
import math

import jax
import jax.numpy as jnp
import numpy as np
from jax import lax
from jax.experimental import pallas as pl
from jax.experimental.pallas import tpu as pltpu
from jax.sharding import PartitionSpec as P

F32 = jnp.float32
BF16 = jnp.bfloat16
BOTH = ("rows", "cols")
SEG = 4096
SHIFT = 768
LEFT = 640
SPAN = SEG + 640
BASE = 1024
WIDE = BASE + SEG + 1024
STEP = 1024
LANES = 128


def lane_ids(rows):
    return lax.broadcasted_iota(jnp.int32, (rows, LANES), 1)


def dot32(a, b):
    return jnp.dot(a, b, preferred_element_type=F32)


def dot_nt(a, b, precision=None):
    return lax.dot_general(
        a, b, (((1,), (1,)), ((), ())), preferred_element_type=F32, precision=precision
    )


def columns(start, width):
    if isinstance(start, int):
        return pl.ds(start, width)
    return pl.ds(pl.multiple_of(start, LANES), width)


def pack_kernel(cot, wh, out, parts):
    out[0:64] = cot[:, 256:1024]
    parts[...] = jnp.zeros_like(parts)
    for half in range(2):
        left = wh[:, 512 + half * 768 : 512 + (half + 1) * 768]
        for part in range(3):
            piece = left.astype(BF16).astype(F32)
            parts[half * 16 + part * 3 : half * 16 + part * 3 + 3] = piece
            left = left - piece
    out[64:96] = parts[...].astype(BF16)


def conv_kernel(
    dil, got, wh, cot, lift_t, now_t, past_t, mix,
    sent, late, parts, w_cat, w_cat_t, mix_t, square, whu, cotu,
    f0, f1, f2, x1, x2, fl1, fl2, sg1, sg2, gt1, gt2, ah, ah2, dp, dp2, g_conv, g_mix, x_t,
):
    lane = lane_ids(64)
    one_lane = lane_ids(1)
    at_start = (lax.axis_index("rows") == 0) & (lax.axis_index("cols") == 0)
    edge = jnp.where(at_start, SHIFT, 1 << 20)

    def shifted(ref, first, turn, keep_below, width):
        turned = [
            pltpu.roll(ref[:, columns(first + LANES * k, LANES)], turn, 1)
            for k in range(width // LANES + 1)
        ]
        keep = lane < keep_below
        return [jnp.where(keep, turned[k], turned[k + 1]) for k in range(width // LANES)]

    def cut(tiles, start, low, high):
        done = []
        for k, tile in enumerate(tiles):
            at = one_lane + (start - BASE + LANES * k)
            done.append(tile * jnp.where((at >= low) & (at < high), 0.0, 1.0))
        return jnp.concatenate(done, axis=1)

    def behind(ref, start, width, layer):
        d = dil[layer]
        whole = pl.multiple_of((d // LANES) * LANES, LANES)
        rest = d % LANES
        tiles = shifted(ref, start - whole - LANES, rest, rest, width)
        return cut(tiles, start, edge, edge + d)

    def beyond(ref, start, width, layer):
        d = dil[layer]
        whole = pl.multiple_of((d // LANES) * LANES, LANES)
        rest = d % LANES
        tiles = shifted(ref, start + whole, (LANES - rest) % LANES, LANES - rest, width)
        return cut(tiles, start, edge - d, edge)

    parts[...] = got[64:96].astype(F32)
    whu[...] = jnp.zeros_like(whu)
    for half in range(2):
        whole = (
            parts[half * 16 : half * 16 + 3] + parts[half * 16 + 3 : half * 16 + 6]
            + parts[half * 16 + 6 : half * 16 + 9]
        )
        if half == 0:
            whu[0:3, 0:640] = whole[:, 128:768]
        else:
            whu[0:3, 640:1408] = whole
    own = SPAN - SHIFT
    whu[0:3, 1408 : 1408 + own] = wh[:, 0:own]
    cotu[:, 0:SHIFT] = got[0:64]
    cotu[:, SHIFT:SPAN] = cot[:, 0:own]

    for layer in range(3):
        stacked = jnp.concatenate([now_t[layer], past_t[layer]], axis=0)
        w_cat_t[layer] = stacked
        w_cat[layer] = stacked.astype(F32).T.astype(BF16)
        square[...] = jnp.zeros_like(square)
        square[0:64, 0:64] = mix[layer].astype(F32)
        mix_t[layer] = square[...].T[0:64, 0:64].astype(BF16)
    square[...] = jnp.zeros_like(square)
    square[0:3, 0:64] = lift_t[...]
    lift_cols = square[...].T[0:64]
    lift_cols = [jnp.broadcast_to(lift_cols[:, i : i + 1], (64, LANES)) for i in range(3)]
    lift_8 = square[0:8, 0:64]
    lift_high = lift_8.astype(BF16)
    lift_16 = jnp.concatenate([lift_high.astype(F32), lift_8 - lift_high.astype(F32)], axis=0)
    lift_16 = lift_16.astype(BF16)

    zero_tile = jnp.zeros((64, LANES), F32)
    for k in range(3):
        f0[:, k * LANES : (k + 1) * LANES] = zero_tile
        f1[:, (k + 1) * LANES : (k + 2) * LANES] = zero_tile
        at = BASE + SPAN + k * LANES
        ah[:, at : at + LANES] = zero_tile
        ah2[:, at : at + LANES] = zero_tile
        ah2[:, at - LANES : at] = zero_tile
    f2[:, 384:512] = zero_tile
    f2[:, 512:640] = zero_tile

    def lift_step(i, carry):
        for k in range(6):
            at = (i * 6 + k) * LANES
            tile = whu[:, columns(at, LANES)]
            f0[:, columns(BASE - LEFT + at, LANES)] = (
                lift_cols[0] * tile[0:1] + lift_cols[1] * tile[1:2] + lift_cols[2] * tile[2:3]
            )
        return carry

    lax.fori_loop(0, 7, lift_step, 0)

    def gates(layer, field, start, width):
        now = field[:, columns(start, width)]
        both = jnp.concatenate(
            [now.astype(BF16), behind(field, start, width, layer).astype(BF16)], axis=0
        )
        pre = dot32(w_cat[layer], both)
        filt = jnp.tanh(pre[:64])
        sig = 0.5 * jnp.tanh(0.5 * pre[64:]) + 0.5
        gate = (filt * sig).astype(BF16)
        return now, both, filt, sig, gate

    def forward(layer, field, field_next, x, fl, sg, gt, start, width):
        now, both, filt, sig, gate = gates(layer, field, start, width)
        at = columns(start, width)
        x[:, at] = both
        fl[:, at] = filt
        sg[:, at] = sig
        gt[:, at] = gate
        field_next[:, at] = now + dot32(mix[layer], gate)

    def run_forward(layer, field, field_next, x, fl, sg, gt, start, rest):
        def step(i, carry):
            forward(layer, field, field_next, x, fl, sg, gt, start + i * STEP, STEP)
            return carry

        lax.fori_loop(0, 5, step, 0)
        if rest:
            forward(layer, field, field_next, x, fl, sg, gt, start + 5 * STEP, rest)

    run_forward(0, f0, f1, x1, fl1, sg1, gt1, BASE - 512, 128)
    run_forward(1, f1, f2, x2, fl2, sg2, gt2, BASE - 384, 0)

    g_conv[...] = jnp.zeros_like(g_conv)
    g_mix[...] = jnp.zeros_like(g_mix)

    def backward(layer, dfield, dfield_b, both, filt, sig, gate, ah_out, dp_out, start, width, own):
        d_gate = dot32(mix_t[layer], dfield_b)
        d_pre = jnp.concatenate(
            [d_gate * sig * (1.0 - filt * filt), d_gate * filt * sig * (1.0 - sig)], axis=0
        ).astype(BF16)
        back = dot32(w_cat_t[layer], d_pre)
        at = columns(start, width)
        dp_out[:, at] = dfield + back[:64]
        ah_out[:, at] = back[64:]
        if own:
            g_conv[layer] += dot_nt(both, d_pre)
            g_mix[layer] += dot_nt(
                dfield_b, jnp.concatenate([jnp.zeros((64, width), BF16), gate], axis=0)
            )

    def last_layer(start, width, own):
        now, both, filt, sig, gate = gates(2, f2, start, width)
        dfield_b = cotu[:, columns(start - BASE, width)]
        backward(2, dfield_b.astype(F32), dfield_b, both, filt, sig, gate, ah, dp, start, width, own)

    def step3(i, carry):
        last_layer(BASE + i * STEP, STEP, True)
        return carry

    lax.fori_loop(0, SEG // STEP, step3, 0)
    last_layer(BASE + SEG, 640, False)

    def saved_layer(layer, x, fl, sg, gt, ah_in, dp_in, ah_out, dp_out, start, width, own):
        at = columns(start, width)
        dfield = dp_in[:, at] + beyond(ah_in, start, width, layer + 1)
        backward(
            layer, dfield, dfield.astype(BF16), x[:, at], fl[:, at], sg[:, at], gt[:, at],
            ah_out, dp_out, start, width, own,
        )

    def step2(i, carry):
        saved_layer(1, x2, fl2, sg2, gt2, ah, dp, ah2, dp2, BASE + i * STEP, STEP, True)
        return carry

    lax.fori_loop(0, SEG // STEP, step2, 0)
    saved_layer(1, x2, fl2, sg2, gt2, ah, dp, ah2, dp2, BASE + SEG, 512, False)

    def step1(i, carry):
        saved_layer(0, x1, fl1, sg1, gt1, ah2, dp2, ah, dp, BASE + i * STEP, STEP, True)
        return carry

    lax.fori_loop(0, SEG // STEP, step1, 0)
    saved_layer(0, x1, fl1, sg1, gt1, ah2, dp2, ah, dp, BASE + SEG, 256, False)

    x_t[...] = jnp.zeros_like(x_t)
    g_lift = jnp.zeros((8, LANES), F32)
    blank = jnp.zeros((64, 256), BF16)
    for m in range(16):
        start = BASE + m * 256
        dfield = dp[:, start : start + 256] + beyond(ah, start, 256, 0)
        high = dfield.astype(BF16)
        low = (dfield - high.astype(F32)).astype(BF16)
        on_high = dot32(lift_16, high)
        x8 = on_high[0:8] + on_high[8:16] + dot32(lift_16, low)[0:8]
        for channel in range(3):
            x_t[channel * 16 + m : channel * 16 + m + 1] = x8[channel : channel + 1]
        seen = whu[:, LEFT + m * 256 : LEFT + (m + 1) * 256]
        seen_high = seen.astype(BF16).astype(F32)
        seen_16 = jnp.concatenate([seen_high, seen - seen_high], axis=0).astype(BF16)
        on_high = dot_nt(seen_16, jnp.concatenate([blank, high], axis=0))
        g_lift += (
            on_high[0:8] + on_high[8:16]
            + dot_nt(seen_16, jnp.concatenate([blank, low], axis=0))[0:8]
        )

    low = lane_ids(256) < 64
    early = jnp.concatenate([g_conv[2], g_mix[1], g_lift, jnp.zeros((56, LANES), F32)], axis=0)
    sent[:, 0, 0:128] = jnp.where(low, x_t[...].T, early)
    sent[:, 0, 128:256] = jnp.concatenate([g_conv[0], g_conv[1]], axis=0)
    late[...] = jnp.concatenate([pltpu.roll(g_conv[2], 64, 1), g_mix[0], g_mix[2]], axis=0)


def swap(x):
    first = (lane_ids(x.shape[0]) // 16) % 2 == 0
    return jnp.where(first, pltpu.roll(x, LANES - 16, 1), -pltpu.roll(x, 16, 1))


def wide_dot(table, x, sign):
    low = lane_ids(256) < 64
    parts = []
    for value in (x, sign * swap(x)):
        high = value.astype(BF16)
        rest = value - high.astype(F32)
        parts.append((high, jnp.where(low, high.astype(F32), pltpu.roll(rest, 64, 1)).astype(BF16)))
    mixed = dot32(table[0], jnp.concatenate([parts[0][1], parts[1][1]], axis=0))
    small = dot32(table[1], jnp.concatenate([parts[0][0], parts[1][0]], axis=0))
    return mixed + pltpu.roll(mixed, 64, 1) + small


def first_kernel(got, late, table, twist_cos, twist_sin, inner, sent, sums):
    data = got[:, 0, 0:128]
    rest = got[:, 0, 128:256]
    low = lane_ids(256) < 64
    x = jnp.where(low, data, 0.0)
    sums[:, 0:128] = jnp.broadcast_to(jnp.sum(data, axis=0, keepdims=True), (8, 128))
    sums[:, 128:256] = jnp.broadcast_to(jnp.sum(rest, axis=0, keepdims=True), (8, 128))
    y = wide_dot(table, x, 1.0)
    y = y * twist_cos[...] + swap(y) * twist_sin[...]
    y = lax.dot(y, inner[...], precision=lax.Precision.HIGHEST, preferred_element_type=F32)
    sent[:, 0, :] = jnp.where(low, y, late[...])


def middle_kernel(got, sums, weights, table, sent, sums_late):
    data = got[:, 0, :]
    low = lane_ids(256) < 64
    x = jnp.where(low, data, 0.0)
    sums_late[...] = jnp.broadcast_to(jnp.sum(data, axis=0, keepdims=True), (8, 128))
    y = wide_dot(table, x, 1.0)
    y = jnp.where(low, y * weights[...], 0.0)
    y = wide_dot(table, y, -1.0)
    sent[:, 0, 0:128] = jnp.where(low, y, jnp.broadcast_to(sums[0:1, 0:128], (256, 128)))
    sent[:, 0, 128:256] = jnp.broadcast_to(sums[0:1, 128:256], (256, 128))


def third_kernel(got, sums_late, table, twist_cos, twist_sin, inner, sent):
    low = lane_ids(256) < 64
    x = jnp.where(low, got[:, 0, 0:128], 0.0)
    y = dot_nt(x, inner[...], lax.Precision.HIGHEST)
    y = y * twist_cos[...] - swap(y) * twist_sin[...]
    y = wide_dot(table, y, -1.0)
    sent[:, 0, :] = jnp.where(low, y, jnp.broadcast_to(sums_late[0:1], (256, 128)))


def last_kernel(scaling, got, got_before, data_grad, now_t, past_t, grad_mix, lift_t):
    last = got[:, 0, :]
    turned = last.T
    for channel in range(3):
        for slot in range(16):
            row = channel * 16 + slot
            m = (slot - SHIFT // 256) % 16
            data_grad[channel : channel + 1, m * 256 : (m + 1) * 256] = turned[row : row + 1]
    late = pltpu.roll(last, 64, 1) * scaling
    early = got_before[:, 0, 0:128] * scaling
    main = got_before[:, 0, 128:256] * scaling
    third = jnp.where(lane_ids(128) < 64, late[0:128], early[0:128])
    for layer, value in enumerate((main[0:128], main[128:256], third)):
        now_t[layer] = value[0:64]
        past_t[layer] = value[64:128]
    early = pltpu.roll(early[128:256], 64, 1)
    grad_mix[0] = late[128:192, 0:64]
    grad_mix[1] = early[0:64, 0:64]
    grad_mix[2] = late[192:256, 0:64]
    lift_t[...] = early[64:67, 0:64]


def weight_kernel(bins, psd, out):
    at = bins[...]
    high = at // LANES
    low = at % LANES
    second = lane_ids(256) >= 32
    total = jnp.zeros((256, LANES), F32)
    for h in range(8):
        rows = [
            jnp.take_along_axis(
                jnp.broadcast_to(psd[8 * j + h : 8 * j + h + 1, :], (256, LANES)), low, axis=1
            )
            for j in range(2)
        ]
        total = jnp.where(high == h, jnp.where(second, rows[1], rows[0]), total)
    out[...] = total


def call(kernel, outs, scratch=(), smem=0, n_in=0, in_specs=None, grid=()):
    vmem = pl.BlockSpec(memory_space=pltpu.VMEM)
    if in_specs is None:
        in_specs = [pl.BlockSpec(memory_space=pltpu.SMEM)] * smem + [vmem] * n_in
    out_shape = [
        out if isinstance(out, jax.ShapeDtypeStruct) else jax.ShapeDtypeStruct(out, F32)
        for out in outs
    ]
    return pl.pallas_call(
        kernel,
        grid=grid,
        out_shape=out_shape,
        in_specs=in_specs,
        out_specs=[vmem] * len(outs),
        scratch_shapes=list(scratch),
        compiler_params=pltpu.CompilerParams(vmem_limit_bytes=56 * 1024 * 1024),
    )


def two_parts(table):
    high = table.astype(jnp.bfloat16)
    low = (table - high.astype(np.float32)).astype(jnp.bfloat16)
    return np.stack([high, low])


def tables(rows_count, cols_count):
    n = rows_count * cols_count
    ids = np.arange(n)
    residue = rows_count * (ids % cols_count) + ids // cols_count

    def pair(product):
        angle = 2.0 * np.pi / n * (product % n)
        return two_parts(
            np.concatenate([np.cos(angle), np.sin(angle)], axis=1).astype(np.float32)
        )

    outward = pair(residue[:, None] * ids[None, :])
    plain = pair(ids[:, None] * ids[None, :])
    inward = pair(ids[:, None] * residue[None, :])
    return residue, outward, plain, inward


def exchange(x):
    return lax.all_to_all(x, BOTH, split_axis=0, concat_axis=0, tiled=True)


def local(
    rows_count, cols_count,
    whitened, cotangent, lift_weight, conv_now, conv_past, mix_weight, dilations, psd_bin, psd_weight,
):
    n = rows_count * cols_count
    total = n * SEG
    me = lax.axis_index("rows") * cols_count + lax.axis_index("cols")
    message, = call(
        pack_kernel, [jax.ShapeDtypeStruct((96, SHIFT), BF16)], [pltpu.VMEM((32, SHIFT), F32)],
        in_specs=[
            pl.BlockSpec((64, 1024), lambda i: (0, 3)), pl.BlockSpec((3, 2048), lambda i: (0, 1)),
        ],
        grid=(1,),
    )(cotangent, whitened)
    received = lax.ppermute(message, BOTH, [(i, (i + 1) % n) for i in range(n)])

    residue, outward, plain, inward = tables(rows_count, cols_count)
    row = np.arange(LANES)
    slot = row % 16
    later = np.where(slot < SHIFT // 256, slot + 16, slot)
    inside = (row < 64).astype(np.float32)

    def twist(steps):
        fixed = jnp.asarray(residue[:, None] * (256 * steps)[None, :], jnp.int32)
        product = (fixed + jnp.asarray(residue, jnp.int32)[:, None] * me) % total
        angle = (2.0 * math.pi / total) * product.astype(F32)
        return jnp.cos(angle) * inside, jnp.sin(angle) * inside

    twist_cos, twist_sin = twist(slot)
    back_cos, back_sin = twist(later)
    same = (row[:, None] // 32 == row[None, :] // 32) & (row[:, None] < 64) & (row[None, :] < 64)
    part = (row // 16) % 2
    alike = same & (part[:, None] == part[None, :])
    sign = np.where(part[:, None] > part[None, :], 1.0, -1.0) * (same & ~alike)
    fixed = jnp.asarray(256 * slot[:, None] * slot[None, :], jnp.int32)
    product = (fixed + jnp.asarray(slot, jnp.int32)[None, :] * me) % SEG
    phase = (2.0 * math.pi / SEG) * product.astype(F32)
    inner = jnp.cos(phase) * alike.astype(np.float32) + jnp.sin(phase) * sign.astype(np.float32)

    bins = psd_bin.reshape(256, 16)
    bins = jnp.concatenate([bins, bins, bins, bins, jnp.zeros((256, 64), jnp.int32)], axis=1)
    weights = call(weight_kernel, [(256, LANES)], n_in=2)(
        bins, (psd_weight * (1.0 / total)).reshape(16, LANES)
    )[0]

    big = lambda rows, dtype: pltpu.VMEM((rows, WIDE), dtype)
    square = pltpu.VMEM((LANES, LANES), F32)
    scratch = (
        [
            pltpu.VMEM((32, SHIFT), F32), pltpu.VMEM((3, 128, 128), BF16),
            pltpu.VMEM((3, 128, 128), BF16), pltpu.VMEM((3, 64, 64), BF16), square,
            pltpu.VMEM((8, LEFT + SPAN), F32), pltpu.VMEM((64, SPAN), BF16),
        ]
        + [big(64, F32)] * 3 + [big(128, BF16)] * 2 + [big(64, F32)] * 4 + [big(64, BF16)] * 2
        + [big(64, F32)] * 4
        + [pltpu.VMEM((3, 128, 128), F32), pltpu.VMEM((3, 64, 128), F32), pltpu.VMEM((128, 256), F32)]
    )
    sent, late = call(conv_kernel, [(n, 1, 256), (n, LANES)], scratch, smem=1, n_in=7)(
        dilations, received, whitened, cotangent, lift_weight.T, jnp.swapaxes(conv_now, 1, 2),
        jnp.swapaxes(conv_past, 1, 2), mix_weight,
    )
    got = exchange(sent)
    sent, sums = call(first_kernel, [(n, 1, LANES), (8, 256)], n_in=6)(
        got, late, outward, twist_cos, twist_sin, inner
    )
    got = exchange(sent)
    sent, sums_late = call(middle_kernel, [(n, 1, 256), (8, LANES)], n_in=4)(
        got, sums, weights, plain
    )
    before = exchange(sent)
    sent, = call(third_kernel, [(n, 1, LANES)], n_in=6)(
        before, sums_late, inward, back_cos, back_sin, inner
    )
    got = exchange(sent)
    outs = [(3, SEG), (3, 64, 128), (3, 64, 128), (3, 64, 64), (3, 64)]
    data_grad, now_t, past_t, grad_mix, lift_t = call(
        functools.partial(last_kernel, total ** -0.5), outs, n_in=2
    )(got, before)
    return (
        data_grad, jnp.swapaxes(now_t, 1, 2), jnp.swapaxes(past_t, 1, 2), grad_mix, lift_t.T
    )


def solution(mesh):
    in_specs = (
        P(None, BOTH), P(None, BOTH), P(), P(), P(), P(), P(), P(None, "cols", "rows"), P(),
    )
    out_specs = (P(None, BOTH), P(), P(), P(), P())
    body = functools.partial(local, mesh.shape["rows"], mesh.shape["cols"])
    return jax.shard_map(body, mesh=mesh, in_specs=in_specs, out_specs=out_specs, check_vma=False)
```

```python
import functools
import math

import jax
import jax.numpy as jnp
import numpy as np
from jax import lax
from jax.experimental import pallas as pl
from jax.experimental.pallas import tpu as pltpu
from jax.sharding import PartitionSpec as P

F32 = jnp.float32
BF16 = jnp.bfloat16
BOTH = ("rows", "cols")
SEG = 4096
SHIFT = 768
LEFT = 640
SPAN = SEG + 640
BASE = 1024
WIDE = BASE + SEG + 1024
STEP = 1024
LANES = 128


def lane_ids(rows):
    return lax.broadcasted_iota(jnp.int32, (rows, LANES), 1)


def dot32(a, b):
    return jnp.dot(a, b, preferred_element_type=F32)


def dot_nt(a, b, precision=None):
    return lax.dot_general(
        a, b, (((1,), (1,)), ((), ())), preferred_element_type=F32, precision=precision
    )


def columns(start, width):
    if isinstance(start, int):
        return pl.ds(start, width)
    return pl.ds(pl.multiple_of(start, LANES), width)


def pack_kernel(cot, wh, out, parts):
    out[0:64] = cot[:, 256:1024]
    parts[...] = jnp.zeros_like(parts)
    for half in range(2):
        left = wh[:, 512 + half * 768 : 512 + (half + 1) * 768]
        for part in range(3):
            piece = left.astype(BF16).astype(F32)
            parts[half * 16 + part * 3 : half * 16 + part * 3 + 3] = piece
            left = left - piece
    out[64:96] = parts[...].astype(BF16)


def conv_kernel(
    dil, got, wh, cot, lift_t, now_t, past_t, mix,
    sent, parts, w_cat, w_cat_t, mix_t, square, whu, cotu,
    f0, f1, f2, x1, x2, fl1, fl2, sg1, sg2, gt1, gt2, ah, ah2, dp, dp2, g_conv, g_mix, x_t,
):
    lane = lane_ids(64)
    one_lane = lane_ids(1)
    at_start = (lax.axis_index("rows") == 0) & (lax.axis_index("cols") == 0)
    edge = jnp.where(at_start, SHIFT, 1 << 20)

    def shifted(ref, first, turn, keep_below, width):
        turned = [
            pltpu.roll(ref[:, columns(first + LANES * k, LANES)], turn, 1)
            for k in range(width // LANES + 1)
        ]
        keep = lane < keep_below
        return [jnp.where(keep, turned[k], turned[k + 1]) for k in range(width // LANES)]

    def cut(tiles, start, low, high):
        done = []
        for k, tile in enumerate(tiles):
            at = one_lane + (start - BASE + LANES * k)
            done.append(tile * jnp.where((at >= low) & (at < high), 0.0, 1.0))
        return jnp.concatenate(done, axis=1)

    def behind(ref, start, width, layer):
        d = dil[layer]
        whole = pl.multiple_of((d // LANES) * LANES, LANES)
        rest = d % LANES
        tiles = shifted(ref, start - whole - LANES, rest, rest, width)
        return cut(tiles, start, edge, edge + d)

    def beyond(ref, start, width, layer):
        d = dil[layer]
        whole = pl.multiple_of((d // LANES) * LANES, LANES)
        rest = d % LANES
        tiles = shifted(ref, start + whole, (LANES - rest) % LANES, LANES - rest, width)
        return cut(tiles, start, edge - d, edge)

    parts[...] = got[64:96].astype(F32)
    whu[...] = jnp.zeros_like(whu)
    for half in range(2):
        whole = (
            parts[half * 16 : half * 16 + 3] + parts[half * 16 + 3 : half * 16 + 6]
            + parts[half * 16 + 6 : half * 16 + 9]
        )
        if half == 0:
            whu[0:3, 0:640] = whole[:, 128:768]
        else:
            whu[0:3, 640:1408] = whole
    own = SPAN - SHIFT
    whu[0:3, 1408 : 1408 + own] = wh[:, 0:own]
    cotu[:, 0:SHIFT] = got[0:64]
    cotu[:, SHIFT:SPAN] = cot[:, 0:own]

    for layer in range(3):
        stacked = jnp.concatenate([now_t[layer], past_t[layer]], axis=0)
        w_cat_t[layer] = stacked
        w_cat[layer] = stacked.astype(F32).T.astype(BF16)
        square[...] = jnp.zeros_like(square)
        square[0:64, 0:64] = mix[layer].astype(F32)
        mix_t[layer] = square[...].T[0:64, 0:64].astype(BF16)
    square[...] = jnp.zeros_like(square)
    square[0:3, 0:64] = lift_t[...]
    lift_cols = square[...].T[0:64]
    lift_cols = [jnp.broadcast_to(lift_cols[:, i : i + 1], (64, LANES)) for i in range(3)]
    lift_8 = square[0:8, 0:64]
    lift_high = lift_8.astype(BF16)
    lift_16 = jnp.concatenate([lift_high.astype(F32), lift_8 - lift_high.astype(F32)], axis=0)
    lift_16 = lift_16.astype(BF16)

    zero_tile = jnp.zeros((64, LANES), F32)
    for k in range(3):
        f0[:, k * LANES : (k + 1) * LANES] = zero_tile
        f1[:, (k + 1) * LANES : (k + 2) * LANES] = zero_tile
        at = BASE + SPAN + k * LANES
        ah[:, at : at + LANES] = zero_tile
        ah2[:, at : at + LANES] = zero_tile
        ah2[:, at - LANES : at] = zero_tile
    f2[:, 384:512] = zero_tile
    f2[:, 512:640] = zero_tile

    def lift_step(i, carry):
        for k in range(6):
            at = (i * 6 + k) * LANES
            tile = whu[:, columns(at, LANES)]
            f0[:, columns(BASE - LEFT + at, LANES)] = (
                lift_cols[0] * tile[0:1] + lift_cols[1] * tile[1:2] + lift_cols[2] * tile[2:3]
            )
        return carry

    lax.fori_loop(0, 7, lift_step, 0)

    def gates(layer, field, start, width):
        now = field[:, columns(start, width)]
        both = jnp.concatenate(
            [now.astype(BF16), behind(field, start, width, layer).astype(BF16)], axis=0
        )
        pre = dot32(w_cat[layer], both)
        filt = jnp.tanh(pre[:64])
        sig = 0.5 * jnp.tanh(0.5 * pre[64:]) + 0.5
        gate = (filt * sig).astype(BF16)
        return now, both, filt, sig, gate

    def forward(layer, field, field_next, x, fl, sg, gt, start, width):
        now, both, filt, sig, gate = gates(layer, field, start, width)
        at = columns(start, width)
        x[:, at] = both
        fl[:, at] = filt
        sg[:, at] = sig
        gt[:, at] = gate
        field_next[:, at] = now + dot32(mix[layer], gate)

    def run_forward(layer, field, field_next, x, fl, sg, gt, start, rest):
        def step(i, carry):
            forward(layer, field, field_next, x, fl, sg, gt, start + i * STEP, STEP)
            return carry

        lax.fori_loop(0, 5, step, 0)
        if rest:
            forward(layer, field, field_next, x, fl, sg, gt, start + 5 * STEP, rest)

    run_forward(0, f0, f1, x1, fl1, sg1, gt1, BASE - 512, 128)
    run_forward(1, f1, f2, x2, fl2, sg2, gt2, BASE - 384, 0)

    g_conv[...] = jnp.zeros_like(g_conv)
    g_mix[...] = jnp.zeros_like(g_mix)

    def backward(layer, dfield, dfield_b, both, filt, sig, gate, ah_out, dp_out, start, width, own):
        d_gate = dot32(mix_t[layer], dfield_b)
        d_pre = jnp.concatenate(
            [d_gate * sig * (1.0 - filt * filt), d_gate * filt * sig * (1.0 - sig)], axis=0
        ).astype(BF16)
        back = dot32(w_cat_t[layer], d_pre)
        at = columns(start, width)
        dp_out[:, at] = dfield + back[:64]
        ah_out[:, at] = back[64:]
        if own:
            g_conv[layer] += dot_nt(both, d_pre)
            empty = jnp.zeros((64, width), BF16)
            placed = [empty, gate] if layer == 1 else [gate, empty]
            g_mix[layer] += dot_nt(dfield_b, jnp.concatenate(placed, axis=0))

    def last_layer(start, width, own):
        now, both, filt, sig, gate = gates(2, f2, start, width)
        dfield_b = cotu[:, columns(start - BASE, width)]
        backward(2, dfield_b.astype(F32), dfield_b, both, filt, sig, gate, ah, dp, start, width, own)

    def step3(i, carry):
        last_layer(BASE + i * STEP, STEP, True)
        return carry

    lax.fori_loop(0, SEG // STEP, step3, 0)
    last_layer(BASE + SEG, 640, False)

    def saved_layer(layer, x, fl, sg, gt, ah_in, dp_in, ah_out, dp_out, start, width, own):
        at = columns(start, width)
        dfield = dp_in[:, at] + beyond(ah_in, start, width, layer + 1)
        backward(
            layer, dfield, dfield.astype(BF16), x[:, at], fl[:, at], sg[:, at], gt[:, at],
            ah_out, dp_out, start, width, own,
        )

    def step2(i, carry):
        saved_layer(1, x2, fl2, sg2, gt2, ah, dp, ah2, dp2, BASE + i * STEP, STEP, True)
        return carry

    lax.fori_loop(0, SEG // STEP, step2, 0)
    saved_layer(1, x2, fl2, sg2, gt2, ah, dp, ah2, dp2, BASE + SEG, 512, False)

    def step1(i, carry):
        saved_layer(0, x1, fl1, sg1, gt1, ah2, dp2, ah, dp, BASE + i * STEP, STEP, True)
        return carry

    lax.fori_loop(0, SEG // STEP, step1, 0)
    saved_layer(0, x1, fl1, sg1, gt1, ah2, dp2, ah, dp, BASE + SEG, 256, False)

    g_lift = jnp.zeros((8, LANES), F32)
    blank = jnp.zeros((64, 256), BF16)
    for m in range(16):
        start = BASE + m * 256
        dfield = dp[:, start : start + 256] + beyond(ah, start, 256, 0)
        high = dfield.astype(BF16)
        low = (dfield - high.astype(F32)).astype(BF16)
        on_high = dot32(lift_16, high)
        x8 = on_high[0:8] + on_high[8:16] + dot32(lift_16, low)[0:8]
        for half in range(2):
            for channel in range(3):
                x_t[2 * m + half : 2 * m + half + 1, channel * LANES : (channel + 1) * LANES] = x8[
                    channel : channel + 1, half * LANES : (half + 1) * LANES
                ]
        seen = whu[:, LEFT + m * 256 : LEFT + (m + 1) * 256]
        seen_high = seen.astype(BF16).astype(F32)
        seen_16 = jnp.concatenate([seen_high, seen - seen_high], axis=0).astype(BF16)
        on_high = dot_nt(seen_16, jnp.concatenate([blank, high], axis=0))
        g_lift += (
            on_high[0:8] + on_high[8:16]
            + dot_nt(seen_16, jnp.concatenate([blank, low], axis=0))[0:8]
        )

    sent[:, 0, :] = jnp.concatenate([x_t[...].astype(BF16)] * 8, axis=0)
    corner = jnp.concatenate(
        [g_mix[0] + g_mix[1], g_mix[2, 0:8] + g_lift, g_mix[2, 8:64]], axis=0
    )
    sent[:, 1, 0:128] = jnp.concatenate([g_conv[0], g_conv[1]], axis=0).astype(BF16)
    sent[:, 1, 128:256] = jnp.concatenate([g_conv[2], corner], axis=0).astype(BF16)
    sent[:, 1, 256:384] = jnp.zeros((256, LANES), BF16)


def halves(value):
    high = value.astype(BF16)
    return high, (value - high.astype(F32)).astype(BF16)


def left_dot(table, value):
    high, low = halves(value)
    return dot32(table[...], jnp.concatenate([high, low, high], axis=0))


def right_dot(dot, table, value):
    high, low = halves(value)
    rows = value.shape[0]
    mixed = dot(jnp.concatenate([high, low], axis=0), table[0])
    return mixed[:rows] + mixed[rows:] + dot(high, table[1])


def first_kernel(got, table, twist_cos, twist_sin, sent, sums):
    grads = jnp.sum(got[:, 1, 0:256].astype(F32), axis=0, keepdims=True)
    sums[...] = jnp.broadcast_to(grads, (8, 256))
    both = dot32(table[...], got[:, 0, :])
    both = both[0:64] + both[64:128]
    cos = [both[0:32, k * LANES : (k + 1) * LANES] for k in range(3)]
    sin = [both[32:64, k * LANES : (k + 1) * LANES] for k in range(3)]
    for k, (real, imag) in enumerate(
        ((cos[0] + sin[1], cos[1] - sin[0]), (cos[2], -sin[2]))
    ):
        sent[:, 2 * k, :] = real * twist_cos[...] + imag * twist_sin[...]
        sent[:, 2 * k + 1, :] = imag * twist_cos[...] - real * twist_sin[...]


def middle_kernel(got, weights, outer, fast, outer_back, turn_cos, turn_sin, sent):
    pieces = [got[:, k, :] for k in range(4)]
    y = jnp.concatenate(
        [
            jnp.concatenate([pieces[0], pieces[2]], axis=1),
            jnp.concatenate([pieces[1], pieces[3]], axis=1),
        ],
        axis=0,
    )
    y = left_dot(outer, y)
    cos, sin = turn_cos[...], turn_sin[...]
    rows = []
    for k in range(2):
        real = y[0:32, k * LANES : (k + 1) * LANES]
        imag = y[32:64, k * LANES : (k + 1) * LANES]
        rows.append(jnp.concatenate([real * cos + imag * sin, imag * cos - real * sin], axis=1))
    y = right_dot(dot32, fast, jnp.concatenate(rows, axis=0))
    y = y * jnp.concatenate([weights[...], weights[...]], axis=1)
    y = right_dot(dot_nt, fast, y)
    reals, imags = [], []
    for k in range(2):
        real = y[k * 32 : (k + 1) * 32, 0:LANES]
        imag = y[k * 32 : (k + 1) * 32, LANES:]
        reals.append(real * cos - imag * sin)
        imags.append(imag * cos + real * sin)
    y = jnp.concatenate(
        [jnp.concatenate(reals, axis=1), jnp.concatenate(imags, axis=1)], axis=0
    )
    y = left_dot(outer_back, y)
    for k in range(2):
        sent[:, 2 * k, :] = y[0:32, k * LANES : (k + 1) * LANES]
        sent[:, 2 * k + 1, :] = y[32:64, k * LANES : (k + 1) * LANES]


def third_kernel(got, sums, table, twist_cos, twist_sin, sent):
    cos, sin = twist_cos[...], twist_sin[...]
    real = [got[:, k, :] * cos - got[:, k + 1, :] * sin for k in (0, 2)]
    imag = [got[:, k + 1, :] * cos + got[:, k, :] * sin for k in (0, 2)]
    y = jnp.concatenate(
        [
            jnp.concatenate([real[0], imag[0], real[1]], axis=1),
            jnp.concatenate([imag[0], -real[0], imag[1]], axis=1),
        ],
        axis=0,
    )
    sent[:, 0, :] = left_dot(table, y).astype(BF16)
    sent[:, 1, 0:256] = jnp.broadcast_to(sums[0:1], (256, 256)).astype(BF16)
    sent[:, 1, 256:384] = jnp.zeros((256, LANES), BF16)


def last_kernel(scaling, got, data_grad, now_t, past_t, grad_mix, lift_t):
    value = got[:, 0, :].astype(F32)
    total = value[0:32]
    for k in range(1, 8):
        total = total + value[32 * k : 32 * (k + 1)]
    for piece in range(32):
        for channel in range(3):
            data_grad[channel : channel + 1, piece * LANES : (piece + 1) * LANES] = total[
                piece : piece + 1, channel * LANES : (channel + 1) * LANES
            ]
    grads = got[:, 1, 0:256].astype(F32) * scaling
    layers = (grads[0:128, 0:128], grads[128:256, 0:128], grads[0:128, 128:256])
    for layer, value in enumerate(layers):
        now_t[layer] = value[0:64]
        past_t[layer] = value[64:128]
    corner = grads[128:256, 128:256]
    turned = pltpu.roll(corner, 64, 1)
    grad_mix[0] = corner[0:64, 0:64]
    grad_mix[1] = turned[0:64, 0:64]
    grad_mix[2] = corner[64:128, 0:64]
    lift_t[...] = turned[64:67, 0:64]


def weight_kernel(bins, psd, out):
    at = bins[...]
    high = at // LANES
    low = at % LANES
    for j in range(2):
        total = jnp.zeros((32, LANES), F32)
        for h in range(8):
            row = jnp.broadcast_to(psd[8 * j + h : 8 * j + h + 1, :], (32, LANES))
            total = jnp.where(high == h, jnp.take_along_axis(row, low, axis=1), total)
        out[32 * j : 32 * (j + 1)] = total


def call(kernel, outs, scratch=(), smem=0, n_in=0, in_specs=None, grid=()):
    vmem = pl.BlockSpec(memory_space=pltpu.VMEM)
    if in_specs is None:
        in_specs = [pl.BlockSpec(memory_space=pltpu.SMEM)] * smem + [vmem] * n_in
    out_shape = [
        out if isinstance(out, jax.ShapeDtypeStruct) else jax.ShapeDtypeStruct(out, F32)
        for out in outs
    ]
    return pl.pallas_call(
        kernel,
        grid=grid,
        out_shape=out_shape,
        in_specs=in_specs,
        out_specs=[vmem] * len(outs),
        scratch_shapes=list(scratch),
        compiler_params=pltpu.CompilerParams(vmem_limit_bytes=56 * 1024 * 1024),
    )


def two_parts(table):
    high = table.astype(np.float32).astype(jnp.bfloat16)
    low = (table - high.astype(np.float64)).astype(np.float32).astype(jnp.bfloat16)
    return high, low


def for_left(table):
    high, low = two_parts(table)
    return np.concatenate([high, high, low], axis=-1)


def tables(rows_count, cols_count):
    n = rows_count * cols_count
    residue = rows_count * np.arange(cols_count)[None, :] + np.arange(rows_count)[:, None]
    angle = 2.0 * np.pi / n * (residue[:, :, None] * np.arange(n)[None, None, :] % n)
    outward = np.concatenate([np.cos(angle), np.sin(angle)], axis=1)
    inward = np.swapaxes(np.concatenate([np.cos(angle), -np.sin(angle)], axis=1), 1, 2)
    outward = np.concatenate(two_parts(outward), axis=1)
    inward = for_left(inward)

    def mixing(product, size, sign):
        angle = 2.0 * np.pi / size * (product % size)
        cos, sin = np.cos(angle), sign * np.sin(angle)
        return np.block([[cos, sin], [-sin, cos]])

    c = np.arange(cols_count)
    l = np.arange(LANES)
    outer = for_left(mixing(c[:, None] * c[None, :], cols_count, 1.0))
    outer_back = for_left(
        mixing((c[:, None] + SHIFT // LANES) * c[None, :], cols_count, -1.0)
    )
    fast = np.stack(two_parts(mixing(l[:, None] * l[None, :], LANES, -1.0)))
    angle = 2.0 * np.pi / SEG * (c[:, None] * l[None, :])
    return (
        outward, inward, outer, outer_back, fast,
        np.cos(angle).astype(np.float32), np.sin(angle).astype(np.float32),
    )


def exchange(x, axes):
    return lax.all_to_all(x, axes, split_axis=0, concat_axis=0, tiled=True)


def local(
    rows_count, cols_count,
    whitened, cotangent, lift_weight, conv_now, conv_past, mix_weight, dilations, psd_bin, psd_weight,
):
    n = rows_count * cols_count
    total = n * SEG
    message, = call(
        pack_kernel, [jax.ShapeDtypeStruct((96, SHIFT), BF16)], [pltpu.VMEM((32, SHIFT), F32)],
        in_specs=[
            pl.BlockSpec((64, 1024), lambda i: (0, 3)), pl.BlockSpec((3, 2048), lambda i: (0, 1)),
        ],
        grid=(1,),
    )(cotangent, whitened)
    received = lax.ppermute(message, BOTH, [(i, (i + 1) % n) for i in range(n)])

    outward, inward, outer, outer_back, fast, turn_cos, turn_sin = tables(rows_count, cols_count)
    my_row, my_col = lax.axis_index("rows"), lax.axis_index("cols")
    outward = lax.dynamic_index_in_dim(jnp.asarray(outward), my_row, 0, keepdims=False)
    inward = lax.dynamic_index_in_dim(jnp.asarray(inward), my_row, 0, keepdims=False)

    def twist(ahead):
        residue = rows_count * lax.broadcasted_iota(jnp.int32, (cols_count, LANES), 0) + my_row
        sample = lax.broadcasted_iota(jnp.int32, (cols_count, LANES), 1) + LANES * (my_col + ahead)
        angle = (2.0 * math.pi / total) * ((residue * sample) % total).astype(F32)
        return jnp.cos(angle), jnp.sin(angle)

    twist_cos, twist_sin = twist(0)
    back_cos, back_sin = twist(SHIFT // LANES)

    bins = psd_bin.reshape(LANES, cols_count).T
    weights = call(weight_kernel, [(2 * cols_count, LANES)], n_in=2)(
        bins, (psd_weight * (1.0 / total)).reshape(16, LANES)
    )[0]

    big = lambda rows, dtype: pltpu.VMEM((rows, WIDE), dtype)
    square = pltpu.VMEM((LANES, LANES), F32)
    scratch = (
        [
            pltpu.VMEM((32, SHIFT), F32), pltpu.VMEM((3, 128, 128), BF16),
            pltpu.VMEM((3, 128, 128), BF16), pltpu.VMEM((3, 64, 64), BF16), square,
            pltpu.VMEM((8, LEFT + SPAN), F32), pltpu.VMEM((64, SPAN), BF16),
        ]
        + [big(64, F32)] * 3 + [big(128, BF16)] * 2 + [big(64, F32)] * 4 + [big(64, BF16)] * 2
        + [big(64, F32)] * 4
        + [pltpu.VMEM((3, 128, 128), F32), pltpu.VMEM((3, 64, 128), F32), pltpu.VMEM((32, 384), F32)]
    )
    packed = jax.ShapeDtypeStruct((n, 2, 3 * LANES), BF16)
    sent, = call(conv_kernel, [packed], scratch, smem=1, n_in=7)(
        dilations, received, whitened, cotangent, lift_weight.T, jnp.swapaxes(conv_now, 1, 2),
        jnp.swapaxes(conv_past, 1, 2), mix_weight,
    )
    got = exchange(sent, BOTH)
    pieces = (cols_count, 4, LANES)
    sent, sums = call(first_kernel, [pieces, (8, 256)], n_in=4)(got, outward, twist_cos, twist_sin)
    got = exchange(sent, "cols")
    sent, = call(middle_kernel, [pieces], n_in=7)(
        got, weights, outer, fast, outer_back, turn_cos, turn_sin
    )
    got = exchange(sent, "cols")
    sent, = call(third_kernel, [packed], n_in=5)(got, sums, inward, back_cos, back_sin)
    got = exchange(sent, BOTH)
    outs = [(3, SEG), (3, 64, 128), (3, 64, 128), (3, 64, 64), (3, 64)]
    data_grad, now_t, past_t, grad_mix, lift_t = call(
        functools.partial(last_kernel, total ** -0.5), outs, n_in=1
    )(got)
    return (
        data_grad, jnp.swapaxes(now_t, 1, 2), jnp.swapaxes(past_t, 1, 2), grad_mix, lift_t.T
    )


def solution(mesh):
    in_specs = (
        P(None, BOTH), P(None, BOTH), P(), P(), P(), P(), P(), P(None, "cols", "rows"), P(),
    )
    out_specs = (P(None, BOTH), P(), P(), P(), P())
    body = functools.partial(local, mesh.shape["rows"], mesh.shape["cols"])
    return jax.shard_map(body, mesh=mesh, in_specs=in_specs, out_specs=out_specs, check_vma=False)
```

```python
import functools
import math

import jax
import jax.numpy as jnp
import numpy as np
from jax import lax
from jax.experimental import pallas as pl
from jax.experimental.pallas import tpu as pltpu
from jax.sharding import PartitionSpec as P

F32 = jnp.float32
BF16 = jnp.bfloat16
BOTH = ("rows", "cols")
SEG = 4096
SHIFT = 768
LEFT = 640
SPAN = SEG + 640
BASE = 1024
WIDE = BASE + SEG + 1024
STEP = 2048
STRIDE = 2560
LANES = 128


def lane_ids(rows):
    return lax.broadcasted_iota(jnp.int32, (rows, LANES), 1)


def dot32(a, b):
    return jnp.dot(a, b, preferred_element_type=F32)


def dot_nt(a, b, precision=None):
    return lax.dot_general(
        a, b, (((1,), (1,)), ((), ())), preferred_element_type=F32, precision=precision
    )


def columns(start, width):
    if isinstance(start, int):
        return pl.ds(start, width)
    return pl.ds(pl.multiple_of(start, LANES), width)


def pack_kernel(cot, wh, out, parts):
    out[0:64] = cot[:, 256:1024]
    parts[...] = jnp.zeros_like(parts)
    for half in range(2):
        left = wh[:, 512 + half * 768 : 512 + (half + 1) * 768]
        for part in range(3):
            piece = left.astype(BF16).astype(F32)
            parts[half * 16 + part * 3 : half * 16 + part * 3 + 3] = piece
            left = left - piece
    out[64:96] = parts[...].astype(BF16)


def conv_kernel(
    dil, got, wh, cot, lift_t, now_t, past_t, mix,
    sent, parts, w_cat, w_cat_t, mix_t, square, whu, cotu,
    f0, f1, f2, x1, x2, fl1, fl2, sg1, sg2, gt1, gt2, ah, ah2, dp, dp2, g_conv, g_mix, x_t,
):
    lane = lane_ids(64)
    one_lane = lane_ids(1)
    at_start = (lax.axis_index("rows") == 0) & (lax.axis_index("cols") == 0)
    edge = jnp.where(at_start, SHIFT, 1 << 20)

    def shifted(ref, first, turn, keep_below, width):
        turned = [
            pltpu.roll(ref[:, columns(first + LANES * k, LANES)], turn, 1)
            for k in range(width // LANES + 1)
        ]
        keep = lane < keep_below
        return [jnp.where(keep, turned[k], turned[k + 1]) for k in range(width // LANES)]

    def cut(tiles, start, low, high):
        done = []
        for k, tile in enumerate(tiles):
            at = one_lane + (start - BASE + LANES * k)
            done.append(tile * jnp.where((at >= low) & (at < high), 0.0, 1.0))
        return jnp.concatenate(done, axis=1)

    def behind(ref, start, width, layer):
        d = dil[layer]
        whole = pl.multiple_of((d // LANES) * LANES, LANES)
        rest = d % LANES
        tiles = shifted(ref, start - whole - LANES, rest, rest, width)
        return cut(tiles, start, edge, edge + d)

    def beyond(ref, start, width, layer):
        d = dil[layer]
        whole = pl.multiple_of((d // LANES) * LANES, LANES)
        rest = d % LANES
        tiles = shifted(ref, start + whole, (LANES - rest) % LANES, LANES - rest, width)
        return cut(tiles, start, edge - d, edge)

    parts[...] = got[64:96].astype(F32)
    whu[...] = jnp.zeros_like(whu)
    for half in range(2):
        whole = (
            parts[half * 16 : half * 16 + 3] + parts[half * 16 + 3 : half * 16 + 6]
            + parts[half * 16 + 6 : half * 16 + 9]
        )
        if half == 0:
            whu[0:3, 0:640] = whole[:, 128:768]
        else:
            whu[0:3, 640:1408] = whole
    own = SPAN - SHIFT
    whu[0:3, 1408 : 1408 + own] = wh[:, 0:own]
    cotu[:, 0:SHIFT] = got[0:64]
    cotu[:, SHIFT:SPAN] = cot[:, 0:own]

    for layer in range(3):
        stacked = jnp.concatenate([now_t[layer], past_t[layer]], axis=0)
        w_cat_t[layer] = stacked
        w_cat[layer] = stacked.astype(F32).T.astype(BF16)
        square[...] = jnp.zeros_like(square)
        square[0:64, 0:64] = mix[layer].astype(F32)
        mix_t[layer] = square[...].T[0:64, 0:64].astype(BF16)
    square[...] = jnp.zeros_like(square)
    square[0:3, 0:64] = lift_t[...]
    lift_cols = square[...].T[0:64]
    lift_cols = [jnp.broadcast_to(lift_cols[:, i : i + 1], (64, LANES)) for i in range(3)]
    lift_8 = square[0:8, 0:64]
    lift_high = lift_8.astype(BF16)
    lift_16 = jnp.concatenate([lift_high.astype(F32), lift_8 - lift_high.astype(F32)], axis=0)
    lift_16 = lift_16.astype(BF16)

    zero_tile = jnp.zeros((64, LANES), F32)
    for k in range(3):
        f0[:, k * LANES : (k + 1) * LANES] = zero_tile
        f1[:, (k + 1) * LANES : (k + 2) * LANES] = zero_tile
        at = BASE + SPAN + k * LANES
        ah[:, at : at + LANES] = zero_tile
        ah2[:, at : at + LANES] = zero_tile
        ah2[:, at - LANES : at] = zero_tile
    f2[:, 384:512] = zero_tile
    f2[:, 512:640] = zero_tile

    def lift_step(i, carry):
        for k in range(6):
            at = (i * 6 + k) * LANES
            tile = whu[:, columns(at, LANES)]
            f0[:, columns(BASE - LEFT + at, LANES)] = (
                lift_cols[0] * tile[0:1] + lift_cols[1] * tile[1:2] + lift_cols[2] * tile[2:3]
            )
        return carry

    lax.fori_loop(0, 7, lift_step, 0)

    def gates(layer, field, start, width):
        now = field[:, columns(start, width)]
        both = jnp.concatenate(
            [now.astype(BF16), behind(field, start, width, layer).astype(BF16)], axis=0
        )
        pre = dot32(w_cat[layer], both)
        filt = jnp.tanh(pre[:64])
        sig = 0.5 * jnp.tanh(0.5 * pre[64:]) + 0.5
        gate = (filt * sig).astype(BF16)
        return now, both, filt, sig, gate

    def forward(layer, field, field_next, x, fl, sg, gt, start, width):
        now, both, filt, sig, gate = gates(layer, field, start, width)
        at = columns(start, width)
        x[:, at] = both
        fl[:, at] = filt
        sg[:, at] = sig
        gt[:, at] = gate
        field_next[:, at] = now + dot32(mix[layer], gate)

    def run_forward(layer, field, field_next, x, fl, sg, gt, start, rest):
        def step(i, carry):
            forward(layer, field, field_next, x, fl, sg, gt, start + i * STRIDE, STRIDE)
            return carry

        lax.fori_loop(0, 2, step, 0)
        if rest:
            forward(layer, field, field_next, x, fl, sg, gt, start + 2 * STRIDE, rest)

    run_forward(0, f0, f1, x1, fl1, sg1, gt1, BASE - 512, 128)
    run_forward(1, f1, f2, x2, fl2, sg2, gt2, BASE - 384, 0)

    g_conv[...] = jnp.zeros_like(g_conv)
    g_mix[...] = jnp.zeros_like(g_mix)

    def backward(layer, dfield, dfield_b, both, filt, sig, gate, ah_out, dp_out, start, width, own):
        d_gate = dot32(mix_t[layer], dfield_b)
        d_pre = jnp.concatenate(
            [d_gate * sig * (1.0 - filt * filt), d_gate * filt * sig * (1.0 - sig)], axis=0
        ).astype(BF16)
        back = dot32(w_cat_t[layer], d_pre)
        at = columns(start, width)
        dp_out[:, at] = dfield + back[:64]
        ah_out[:, at] = back[64:]
        if own:
            g_conv[layer] += dot_nt(both, d_pre)
            empty = jnp.zeros((64, width), BF16)
            placed = [empty, gate] if layer == 1 else [gate, empty]
            g_mix[layer] += dot_nt(dfield_b, jnp.concatenate(placed, axis=0))

    def last_layer(start, width, own):
        now, both, filt, sig, gate = gates(2, f2, start, width)
        dfield_b = cotu[:, columns(start - BASE, width)]
        backward(2, dfield_b.astype(F32), dfield_b, both, filt, sig, gate, ah, dp, start, width, own)

    def step3(i, carry):
        last_layer(BASE + i * STEP, STEP, True)
        return carry

    lax.fori_loop(0, SEG // STEP, step3, 0)
    last_layer(BASE + SEG, 640, False)

    def saved_layer(layer, x, fl, sg, gt, ah_in, dp_in, ah_out, dp_out, start, width, own):
        at = columns(start, width)
        dfield = dp_in[:, at] + beyond(ah_in, start, width, layer + 1)
        backward(
            layer, dfield, dfield.astype(BF16), x[:, at], fl[:, at], sg[:, at], gt[:, at],
            ah_out, dp_out, start, width, own,
        )

    def step2(i, carry):
        saved_layer(1, x2, fl2, sg2, gt2, ah, dp, ah2, dp2, BASE + i * STEP, STEP, True)
        return carry

    lax.fori_loop(0, SEG // STEP, step2, 0)
    saved_layer(1, x2, fl2, sg2, gt2, ah, dp, ah2, dp2, BASE + SEG, 512, False)

    def step1(i, carry):
        saved_layer(0, x1, fl1, sg1, gt1, ah2, dp2, ah, dp, BASE + i * STEP, STEP, True)
        return carry

    lax.fori_loop(0, SEG // STEP, step1, 0)
    saved_layer(0, x1, fl1, sg1, gt1, ah2, dp2, ah, dp, BASE + SEG, 256, False)

    g_lift = jnp.zeros((8, LANES), F32)
    blank = jnp.zeros((64, 256), BF16)
    for m in range(16):
        start = BASE + m * 256
        dfield = dp[:, start : start + 256] + beyond(ah, start, 256, 0)
        high = dfield.astype(BF16)
        low = (dfield - high.astype(F32)).astype(BF16)
        on_high = dot32(lift_16, high)
        x8 = on_high[0:8] + on_high[8:16] + dot32(lift_16, low)[0:8]
        for half in range(2):
            for channel in range(3):
                x_t[2 * m + half : 2 * m + half + 1, channel * LANES : (channel + 1) * LANES] = x8[
                    channel : channel + 1, half * LANES : (half + 1) * LANES
                ]
        seen = whu[:, LEFT + m * 256 : LEFT + (m + 1) * 256]
        seen_high = seen.astype(BF16).astype(F32)
        seen_16 = jnp.concatenate([seen_high, seen - seen_high], axis=0).astype(BF16)
        on_high = dot_nt(seen_16, jnp.concatenate([blank, high], axis=0))
        g_lift += (
            on_high[0:8] + on_high[8:16]
            + dot_nt(seen_16, jnp.concatenate([blank, low], axis=0))[0:8]
        )

    sent[:, 0, :] = jnp.concatenate([x_t[...].astype(BF16)] * 8, axis=0)
    corner = jnp.concatenate(
        [g_mix[0] + g_mix[1], g_mix[2, 0:8] + g_lift, g_mix[2, 8:64]], axis=0
    )
    sent[:, 1, 0:128] = jnp.concatenate([g_conv[0], g_conv[1]], axis=0).astype(BF16)
    sent[:, 1, 128:256] = jnp.concatenate([g_conv[2], corner], axis=0).astype(BF16)
    sent[:, 1, 256:384] = jnp.zeros((256, LANES), BF16)


def halves(value):
    high = value.astype(BF16)
    return high, (value - high.astype(F32)).astype(BF16)


def left_dot(table, value):
    high, low = halves(value)
    return dot32(table[...], jnp.concatenate([high, low, high], axis=0))


def right_dot(dot, table, value):
    high, low = halves(value)
    rows = value.shape[0]
    mixed = dot(jnp.concatenate([high, low], axis=0), table[0])
    return mixed[:rows] + mixed[rows:] + dot(high, table[1])


def first_kernel(got, table, twist_cos, twist_sin, sent, sums):
    grads = jnp.sum(got[:, 1, 0:256].astype(F32), axis=0, keepdims=True)
    sums[...] = jnp.broadcast_to(grads, (8, 256))
    both = dot32(table[...], got[:, 0, :])
    both = both[0:64] + both[64:128]
    cos = [both[0:32, k * LANES : (k + 1) * LANES] for k in range(3)]
    sin = [both[32:64, k * LANES : (k + 1) * LANES] for k in range(3)]
    for k, (real, imag) in enumerate(
        ((cos[0] + sin[1], cos[1] - sin[0]), (cos[2], -sin[2]))
    ):
        sent[:, 2 * k, :] = real * twist_cos[...] + imag * twist_sin[...]
        sent[:, 2 * k + 1, :] = imag * twist_cos[...] - real * twist_sin[...]


def middle_kernel(got, weights, outer, fast, outer_back, turn_cos, turn_sin, sent):
    pieces = [got[:, k, :] for k in range(4)]
    y = jnp.concatenate(
        [
            jnp.concatenate([pieces[0], pieces[2]], axis=1),
            jnp.concatenate([pieces[1], pieces[3]], axis=1),
        ],
        axis=0,
    )
    y = left_dot(outer, y)
    cos, sin = turn_cos[...], turn_sin[...]
    rows = []
    for k in range(2):
        real = y[0:32, k * LANES : (k + 1) * LANES]
        imag = y[32:64, k * LANES : (k + 1) * LANES]
        rows.append(jnp.concatenate([real * cos + imag * sin, imag * cos - real * sin], axis=1))
    y = right_dot(dot32, fast, jnp.concatenate(rows, axis=0))
    y = y * jnp.concatenate([weights[...], weights[...]], axis=1)
    y = right_dot(dot_nt, fast, y)
    reals, imags = [], []
    for k in range(2):
        real = y[k * 32 : (k + 1) * 32, 0:LANES]
        imag = y[k * 32 : (k + 1) * 32, LANES:]
        reals.append(real * cos - imag * sin)
        imags.append(imag * cos + real * sin)
    y = jnp.concatenate(
        [jnp.concatenate(reals, axis=1), jnp.concatenate(imags, axis=1)], axis=0
    )
    y = left_dot(outer_back, y)
    for k in range(2):
        sent[:, 2 * k, :] = y[0:32, k * LANES : (k + 1) * LANES]
        sent[:, 2 * k + 1, :] = y[32:64, k * LANES : (k + 1) * LANES]


def third_kernel(got, sums, table, twist_cos, twist_sin, sent):
    cos, sin = twist_cos[...], twist_sin[...]
    real = [got[:, k, :] * cos - got[:, k + 1, :] * sin for k in (0, 2)]
    imag = [got[:, k + 1, :] * cos + got[:, k, :] * sin for k in (0, 2)]
    y = jnp.concatenate(
        [
            jnp.concatenate([real[0], imag[0], real[1]], axis=1),
            jnp.concatenate([imag[0], -real[0], imag[1]], axis=1),
        ],
        axis=0,
    )
    sent[:, 0, :] = left_dot(table, y).astype(BF16)
    sent[:, 1, 0:256] = jnp.broadcast_to(sums[0:1], (256, 256)).astype(BF16)
    sent[:, 1, 256:384] = jnp.zeros((256, LANES), BF16)


def last_kernel(scaling, got, data_grad, now_t, past_t, grad_mix, lift_t):
    value = got[:, 0, :].astype(F32)
    total = value[0:32]
    for k in range(1, 8):
        total = total + value[32 * k : 32 * (k + 1)]
    for piece in range(32):
        for channel in range(3):
            data_grad[channel : channel + 1, piece * LANES : (piece + 1) * LANES] = total[
                piece : piece + 1, channel * LANES : (channel + 1) * LANES
            ]
    grads = got[:, 1, 0:256].astype(F32) * scaling
    layers = (grads[0:128, 0:128], grads[128:256, 0:128], grads[0:128, 128:256])
    for layer, value in enumerate(layers):
        now_t[layer] = value[0:64]
        past_t[layer] = value[64:128]
    corner = grads[128:256, 128:256]
    turned = pltpu.roll(corner, 64, 1)
    grad_mix[0] = corner[0:64, 0:64]
    grad_mix[1] = turned[0:64, 0:64]
    grad_mix[2] = corner[64:128, 0:64]
    lift_t[...] = turned[64:67, 0:64]


def weight_kernel(bins, psd, out):
    at = bins[...]
    high = at // LANES
    low = at % LANES
    for j in range(2):
        total = jnp.zeros((32, LANES), F32)
        for h in range(8):
            row = jnp.broadcast_to(psd[8 * j + h : 8 * j + h + 1, :], (32, LANES))
            total = jnp.where(high == h, jnp.take_along_axis(row, low, axis=1), total)
        out[32 * j : 32 * (j + 1)] = total


def call(kernel, outs, scratch=(), smem=0, n_in=0, in_specs=None, grid=()):
    vmem = pl.BlockSpec(memory_space=pltpu.VMEM)
    if in_specs is None:
        in_specs = [pl.BlockSpec(memory_space=pltpu.SMEM)] * smem + [vmem] * n_in
    out_shape = [
        out if isinstance(out, jax.ShapeDtypeStruct) else jax.ShapeDtypeStruct(out, F32)
        for out in outs
    ]
    return pl.pallas_call(
        kernel,
        grid=grid,
        out_shape=out_shape,
        in_specs=in_specs,
        out_specs=[vmem] * len(outs),
        scratch_shapes=list(scratch),
        compiler_params=pltpu.CompilerParams(vmem_limit_bytes=56 * 1024 * 1024),
    )


def two_parts(table):
    high = table.astype(np.float32).astype(jnp.bfloat16)
    low = (table - high.astype(np.float64)).astype(np.float32).astype(jnp.bfloat16)
    return high, low


def for_left(table):
    high, low = two_parts(table)
    return np.concatenate([high, high, low], axis=-1)


def tables(rows_count, cols_count):
    n = rows_count * cols_count
    residue = rows_count * np.arange(cols_count)[None, :] + np.arange(rows_count)[:, None]
    angle = 2.0 * np.pi / n * (residue[:, :, None] * np.arange(n)[None, None, :] % n)
    outward = np.concatenate([np.cos(angle), np.sin(angle)], axis=1)
    inward = np.swapaxes(np.concatenate([np.cos(angle), -np.sin(angle)], axis=1), 1, 2)
    outward = np.concatenate(two_parts(outward), axis=1)
    inward = for_left(inward)

    def mixing(product, size, sign):
        angle = 2.0 * np.pi / size * (product % size)
        cos, sin = np.cos(angle), sign * np.sin(angle)
        return np.block([[cos, sin], [-sin, cos]])

    c = np.arange(cols_count)
    l = np.arange(LANES)
    outer = for_left(mixing(c[:, None] * c[None, :], cols_count, 1.0))
    outer_back = for_left(
        mixing((c[:, None] + SHIFT // LANES) * c[None, :], cols_count, -1.0)
    )
    fast = np.stack(two_parts(mixing(l[:, None] * l[None, :], LANES, -1.0)))
    angle = 2.0 * np.pi / SEG * (c[:, None] * l[None, :])
    return (
        outward, inward, outer, outer_back, fast,
        np.cos(angle).astype(np.float32), np.sin(angle).astype(np.float32),
    )


def near(x):
    return pltpu.with_memory_space_constraint(x, pltpu.VMEM)


def exchange(x, axes):
    return near(lax.all_to_all(x, axes, split_axis=0, concat_axis=0, tiled=True))


def local(
    rows_count, cols_count,
    whitened, cotangent, lift_weight, conv_now, conv_past, mix_weight, dilations, psd_bin, psd_weight,
):
    n = rows_count * cols_count
    total = n * SEG
    message, = call(
        pack_kernel, [jax.ShapeDtypeStruct((96, SHIFT), BF16)], [pltpu.VMEM((32, SHIFT), F32)],
        in_specs=[
            pl.BlockSpec((64, 1024), lambda i: (0, 3)), pl.BlockSpec((3, 2048), lambda i: (0, 1)),
        ],
        grid=(1,),
    )(cotangent, whitened)
    received = near(lax.ppermute(message, BOTH, [(i, (i + 1) % n) for i in range(n)]))

    outward, inward, outer, outer_back, fast, turn_cos, turn_sin = tables(rows_count, cols_count)
    my_row, my_col = lax.axis_index("rows"), lax.axis_index("cols")
    outward = lax.dynamic_index_in_dim(jnp.asarray(outward), my_row, 0, keepdims=False)
    inward = lax.dynamic_index_in_dim(jnp.asarray(inward), my_row, 0, keepdims=False)

    def twist(ahead):
        residue = rows_count * lax.broadcasted_iota(jnp.int32, (cols_count, LANES), 0) + my_row
        sample = lax.broadcasted_iota(jnp.int32, (cols_count, LANES), 1) + LANES * (my_col + ahead)
        angle = (2.0 * math.pi / total) * ((residue * sample) % total).astype(F32)
        return jnp.cos(angle), jnp.sin(angle)

    twist_cos, twist_sin = twist(0)
    back_cos, back_sin = twist(SHIFT // LANES)

    bins = psd_bin.reshape(LANES, cols_count).T
    weights = call(weight_kernel, [(2 * cols_count, LANES)], n_in=2)(
        bins, (psd_weight * (1.0 / total)).reshape(16, LANES)
    )[0]

    big = lambda rows, dtype: pltpu.VMEM((rows, WIDE), dtype)
    square = pltpu.VMEM((LANES, LANES), F32)
    scratch = (
        [
            pltpu.VMEM((32, SHIFT), F32), pltpu.VMEM((3, 128, 128), BF16),
            pltpu.VMEM((3, 128, 128), BF16), pltpu.VMEM((3, 64, 64), BF16), square,
            pltpu.VMEM((8, LEFT + SPAN), F32), pltpu.VMEM((64, SPAN), BF16),
        ]
        + [big(64, F32)] * 3 + [big(128, BF16)] * 2 + [big(64, F32)] * 4 + [big(64, BF16)] * 2
        + [big(64, F32)] * 4
        + [pltpu.VMEM((3, 128, 128), F32), pltpu.VMEM((3, 64, 128), F32), pltpu.VMEM((32, 384), F32)]
    )
    packed = jax.ShapeDtypeStruct((n, 2, 3 * LANES), BF16)
    sent, = call(conv_kernel, [packed], scratch, smem=1, n_in=7)(
        dilations, received, whitened, cotangent, lift_weight.T, jnp.swapaxes(conv_now, 1, 2),
        jnp.swapaxes(conv_past, 1, 2), mix_weight,
    )
    got = exchange(sent, BOTH)
    pieces = (cols_count, 4, LANES)
    sent, sums = call(first_kernel, [pieces, (8, 256)], n_in=4)(got, near(outward), near(twist_cos), near(twist_sin))
    got = exchange(sent, "cols")
    sent, = call(middle_kernel, [pieces], n_in=7)(
        got, near(weights), near(outer), near(fast), near(outer_back), near(turn_cos), near(turn_sin)
    )
    got = exchange(sent, "cols")
    sent, = call(third_kernel, [packed], n_in=5)(got, near(sums), near(inward), near(back_cos), near(back_sin))
    got = exchange(sent, BOTH)
    outs = [(3, SEG), (3, 64, 128), (3, 64, 128), (3, 64, 64), (3, 64)]
    data_grad, now_t, past_t, grad_mix, lift_t = call(
        functools.partial(last_kernel, total ** -0.5), outs, n_in=1
    )(got)
    return (
        data_grad, jnp.swapaxes(now_t, 1, 2), jnp.swapaxes(past_t, 1, 2), grad_mix, lift_t.T
    )


def solution(mesh):
    in_specs = (
        P(None, BOTH), P(None, BOTH), P(), P(), P(), P(), P(), P(None, "cols", "rows"), P(),
    )
    out_specs = (P(None, BOTH), P(), P(), P(), P())
    body = functools.partial(local, mesh.shape["rows"], mesh.shape["cols"])
    return jax.shard_map(body, mesh=mesh, in_specs=in_specs, out_specs=out_specs, check_vma=False)
```

```python
import functools
import math

import jax
import jax.numpy as jnp
import numpy as np
from jax import lax
from jax.experimental import pallas as pl
from jax.experimental.pallas import tpu as pltpu
from jax.sharding import PartitionSpec as P

F32 = jnp.float32
BF16 = jnp.bfloat16
BOTH = ("rows", "cols")
SEG = 4096
SHIFT = 768
LEFT = 640
SPAN = SEG + 640
BASE = 1024
WIDE = BASE + SEG + 1024
STEP = 2048
STRIDE = 2560
LANES = 128


def lane_ids(rows):
    return lax.broadcasted_iota(jnp.int32, (rows, LANES), 1)


def dot32(a, b):
    return jnp.dot(a, b, preferred_element_type=F32)


def dot_nt(a, b, precision=None):
    return lax.dot_general(
        a, b, (((1,), (1,)), ((), ())), preferred_element_type=F32, precision=precision
    )


def columns(start, width):
    if isinstance(start, int):
        return pl.ds(start, width)
    return pl.ds(pl.multiple_of(start, LANES), width)


def pack_kernel(cot, wh, out, parts):
    out[0:64] = cot[:, 256:1024]
    parts[...] = jnp.zeros_like(parts)
    for half in range(2):
        left = wh[:, 512 + half * 768 : 512 + (half + 1) * 768]
        for part in range(3):
            piece = left.astype(BF16).astype(F32)
            parts[half * 16 + part * 3 : half * 16 + part * 3 + 3] = piece
            left = left - piece
    out[64:96] = parts[...].astype(BF16)


def conv_kernel(
    dil, got, wh, cot, lift_t, now_t, past_t, mix,
    sent, parts, w_cat, w_cat_t, mix_t, square, whu, cotu,
    f0, f1, f2, x1, x2, fl1, fl2, sg1, sg2, gt1, gt2, ah, ah2, dp, dp2, g_conv, g_mix, x_t,
):
    lane = lane_ids(64)
    one_lane = lane_ids(1)
    at_start = (lax.axis_index("rows") == 0) & (lax.axis_index("cols") == 0)
    edge = jnp.where(at_start, SHIFT, 1 << 20)

    def shifted(ref, first, turn, keep_below, width):
        turned = [
            pltpu.roll(ref[:, columns(first + LANES * k, LANES)], turn, 1)
            for k in range(width // LANES + 1)
        ]
        keep = lane < keep_below
        return [jnp.where(keep, turned[k], turned[k + 1]) for k in range(width // LANES)]

    def cut(tiles, start, low, high):
        done = []
        for k, tile in enumerate(tiles):
            at = one_lane + (start - BASE + LANES * k)
            done.append(tile * jnp.where((at >= low) & (at < high), 0.0, 1.0))
        return jnp.concatenate(done, axis=1)

    def behind(ref, start, width, layer):
        d = dil[layer]
        whole = pl.multiple_of((d // LANES) * LANES, LANES)
        rest = d % LANES
        tiles = shifted(ref, start - whole - LANES, rest, rest, width)
        return cut(tiles, start, edge, edge + d)

    def beyond(ref, start, width, layer):
        d = dil[layer]
        whole = pl.multiple_of((d // LANES) * LANES, LANES)
        rest = d % LANES
        tiles = shifted(ref, start + whole, (LANES - rest) % LANES, LANES - rest, width)
        return cut(tiles, start, edge - d, edge)

    parts[...] = got[64:96].astype(F32)
    whu[...] = jnp.zeros_like(whu)
    for half in range(2):
        whole = (
            parts[half * 16 : half * 16 + 3] + parts[half * 16 + 3 : half * 16 + 6]
            + parts[half * 16 + 6 : half * 16 + 9]
        )
        if half == 0:
            whu[0:3, 0:640] = whole[:, 128:768]
        else:
            whu[0:3, 640:1408] = whole
    own = SPAN - SHIFT
    whu[0:3, 1408 : 1408 + own] = wh[:, 0:own]
    cotu[:, 0:SHIFT] = got[0:64]
    cotu[:, SHIFT:SPAN] = cot[:, 0:own]

    for layer in range(3):
        stacked = jnp.concatenate([now_t[layer], past_t[layer]], axis=0)
        w_cat_t[layer] = stacked
        w_cat[layer] = stacked.astype(F32).T.astype(BF16)
        square[...] = jnp.zeros_like(square)
        square[0:64, 0:64] = mix[layer].astype(F32)
        mix_t[layer] = square[...].T[0:64, 0:64].astype(BF16)
    square[...] = jnp.zeros_like(square)
    square[0:3, 0:64] = lift_t[...]
    lift_cols = square[...].T[0:64]
    lift_cols = [jnp.broadcast_to(lift_cols[:, i : i + 1], (64, LANES)) for i in range(3)]
    lift_8 = square[0:8, 0:64]
    lift_high = lift_8.astype(BF16)
    lift_16 = jnp.concatenate([lift_high.astype(F32), lift_8 - lift_high.astype(F32)], axis=0)
    lift_16 = lift_16.astype(BF16)

    zero_tile = jnp.zeros((64, LANES), F32)
    for k in range(3):
        f0[:, k * LANES : (k + 1) * LANES] = zero_tile
        f1[:, (k + 1) * LANES : (k + 2) * LANES] = zero_tile
        at = BASE + SPAN + k * LANES
        ah[:, at : at + LANES] = zero_tile
        ah2[:, at : at + LANES] = zero_tile
        ah2[:, at - LANES : at] = zero_tile
    f2[:, 384:512] = zero_tile
    f2[:, 512:640] = zero_tile

    def lift_step(i, carry):
        for k in range(6):
            at = (i * 6 + k) * LANES
            tile = whu[:, columns(at, LANES)]
            f0[:, columns(BASE - LEFT + at, LANES)] = (
                lift_cols[0] * tile[0:1] + lift_cols[1] * tile[1:2] + lift_cols[2] * tile[2:3]
            )
        return carry

    lax.fori_loop(0, 7, lift_step, 0)

    def gates(layer, field, start, width):
        now = field[:, columns(start, width)]
        both = jnp.concatenate(
            [now.astype(BF16), behind(field, start, width, layer).astype(BF16)], axis=0
        )
        pre = dot32(w_cat[layer], both)
        filt = jnp.tanh(pre[:64])
        sig = 0.5 * jnp.tanh(0.5 * pre[64:]) + 0.5
        gate = (filt * sig).astype(BF16)
        return now, both, filt, sig, gate

    def forward(layer, field, field_next, x, fl, sg, gt, start, width):
        now, both, filt, sig, gate = gates(layer, field, start, width)
        at = columns(start, width)
        x[:, at] = both
        fl[:, at] = filt
        sg[:, at] = sig
        gt[:, at] = gate
        field_next[:, at] = now + dot32(mix[layer], gate)

    def run_forward(layer, field, field_next, x, fl, sg, gt, start, rest):
        def step(i, carry):
            forward(layer, field, field_next, x, fl, sg, gt, start + i * STRIDE, STRIDE)
            return carry

        lax.fori_loop(0, 2, step, 0)
        if rest:
            forward(layer, field, field_next, x, fl, sg, gt, start + 2 * STRIDE, rest)

    run_forward(0, f0, f1, x1, fl1, sg1, gt1, BASE - 512, 128)
    run_forward(1, f1, f2, x2, fl2, sg2, gt2, BASE - 384, 0)

    g_conv[...] = jnp.zeros_like(g_conv)
    g_mix[...] = jnp.zeros_like(g_mix)

    def backward(layer, dfield, dfield_b, both, filt, sig, gate, ah_out, dp_out, start, width, own):
        d_gate = dot32(mix_t[layer], dfield_b)
        d_pre = jnp.concatenate(
            [d_gate * sig * (1.0 - filt * filt), d_gate * filt * sig * (1.0 - sig)], axis=0
        ).astype(BF16)
        back = dot32(w_cat_t[layer], d_pre)
        at = columns(start, width)
        dp_out[:, at] = dfield + back[:64]
        ah_out[:, at] = back[64:]
        if own:
            g_conv[layer] += dot_nt(both, d_pre)
            empty = jnp.zeros((64, width), BF16)
            placed = [empty, gate] if layer == 1 else [gate, empty]
            g_mix[layer] += dot_nt(dfield_b, jnp.concatenate(placed, axis=0))

    def last_layer(start, width, own):
        now, both, filt, sig, gate = gates(2, f2, start, width)
        dfield_b = cotu[:, columns(start - BASE, width)]
        backward(2, dfield_b.astype(F32), dfield_b, both, filt, sig, gate, ah, dp, start, width, own)

    def step3(i, carry):
        last_layer(BASE + i * STEP, STEP, True)
        return carry

    lax.fori_loop(0, SEG // STEP, step3, 0)
    last_layer(BASE + SEG, 640, False)

    def saved_layer(layer, x, fl, sg, gt, ah_in, dp_in, ah_out, dp_out, start, width, own):
        at = columns(start, width)
        dfield = dp_in[:, at] + beyond(ah_in, start, width, layer + 1)
        backward(
            layer, dfield, dfield.astype(BF16), x[:, at], fl[:, at], sg[:, at], gt[:, at],
            ah_out, dp_out, start, width, own,
        )

    def step2(i, carry):
        saved_layer(1, x2, fl2, sg2, gt2, ah, dp, ah2, dp2, BASE + i * STEP, STEP, True)
        return carry

    lax.fori_loop(0, SEG // STEP, step2, 0)
    saved_layer(1, x2, fl2, sg2, gt2, ah, dp, ah2, dp2, BASE + SEG, 512, False)

    def step1(i, carry):
        saved_layer(0, x1, fl1, sg1, gt1, ah2, dp2, ah, dp, BASE + i * STEP, STEP, True)
        return carry

    lax.fori_loop(0, SEG // STEP, step1, 0)
    saved_layer(0, x1, fl1, sg1, gt1, ah2, dp2, ah, dp, BASE + SEG, 256, False)

    g_lift = jnp.zeros((8, LANES), F32)
    blank = jnp.zeros((64, 256), BF16)
    for m in range(16):
        start = BASE + m * 256
        dfield = dp[:, start : start + 256] + beyond(ah, start, 256, 0)
        high = dfield.astype(BF16)
        low = (dfield - high.astype(F32)).astype(BF16)
        on_high = dot32(lift_16, high)
        x8 = on_high[0:8] + on_high[8:16] + dot32(lift_16, low)[0:8]
        for half in range(2):
            for channel in range(3):
                x_t[2 * m + half : 2 * m + half + 1, channel * LANES : (channel + 1) * LANES] = x8[
                    channel : channel + 1, half * LANES : (half + 1) * LANES
                ]
        seen = whu[:, LEFT + m * 256 : LEFT + (m + 1) * 256]
        seen_high = seen.astype(BF16).astype(F32)
        seen_16 = jnp.concatenate([seen_high, seen - seen_high], axis=0).astype(BF16)
        on_high = dot_nt(seen_16, jnp.concatenate([blank, high], axis=0))
        g_lift += (
            on_high[0:8] + on_high[8:16]
            + dot_nt(seen_16, jnp.concatenate([blank, low], axis=0))[0:8]
        )

    pair = x_t[:, 0:256].astype(BF16)
    single = jnp.concatenate([x_t[:, 256:384], jnp.zeros((32, LANES), F32)], axis=1).astype(BF16)
    sent[:, 0, :] = jnp.concatenate([pair] * 4 + [single] * 4, axis=0)
    corner = jnp.concatenate(
        [g_mix[0] + g_mix[1], g_mix[2, 0:8] + g_lift, g_mix[2, 8:64]], axis=0
    )
    sent[:, 1, 0:128] = jnp.concatenate([g_conv[0], g_conv[1]], axis=0).astype(BF16)
    sent[:, 1, 128:256] = jnp.concatenate([g_conv[2], corner], axis=0).astype(BF16)


def halves(value):
    high = value.astype(BF16)
    return high, (value - high.astype(F32)).astype(BF16)


def left_dot(table, value):
    high, low = halves(value)
    return dot32(table[...], jnp.concatenate([high, low, high], axis=0))


def right_dot(dot, table, value):
    high, low = halves(value)
    rows = value.shape[0]
    mixed = dot(jnp.concatenate([high, low], axis=0), table[0])
    return mixed[:rows] + mixed[rows:] + dot(high, table[1])


def first_kernel(got, table, twist_cos, twist_sin, sent, sums):
    grads = jnp.sum(got[:, 1, :].astype(F32), axis=0, keepdims=True)
    sums[...] = jnp.broadcast_to(grads, (8, 256))
    both = dot32(table[...], got[:, 0, :])
    both = both[0:128] + both[128:256]
    real = both[0:64, 0:LANES] + both[64:128, LANES:]
    imag = both[0:64, LANES:] - both[64:128, 0:LANES]
    turned_real = real * twist_cos[...] + imag * twist_sin[...]
    turned_imag = imag * twist_cos[...] - real * twist_sin[...]
    for k in range(2):
        sent[:, 2 * k, :] = turned_real[32 * k : 32 * (k + 1)]
        sent[:, 2 * k + 1, :] = turned_imag[32 * k : 32 * (k + 1)]


def middle_kernel(got, weights, outer, fast, outer_back, turn_cos, turn_sin, sent):
    pieces = [got[:, k, :] for k in range(4)]
    y = jnp.concatenate(
        [
            jnp.concatenate([pieces[0], pieces[2]], axis=1),
            jnp.concatenate([pieces[1], pieces[3]], axis=1),
        ],
        axis=0,
    )
    y = left_dot(outer, y)
    cos, sin = turn_cos[...], turn_sin[...]
    rows = []
    for k in range(2):
        real = y[0:32, k * LANES : (k + 1) * LANES]
        imag = y[32:64, k * LANES : (k + 1) * LANES]
        rows.append(jnp.concatenate([real * cos + imag * sin, imag * cos - real * sin], axis=1))
    y = right_dot(dot32, fast, jnp.concatenate(rows, axis=0))
    y = y * jnp.concatenate([weights[...], weights[...]], axis=1)
    y = right_dot(dot_nt, fast, y)
    reals, imags = [], []
    for k in range(2):
        real = y[k * 32 : (k + 1) * 32, 0:LANES]
        imag = y[k * 32 : (k + 1) * 32, LANES:]
        reals.append(real * cos - imag * sin)
        imags.append(imag * cos + real * sin)
    y = jnp.concatenate(
        [jnp.concatenate(reals, axis=1), jnp.concatenate(imags, axis=1)], axis=0
    )
    y = left_dot(outer_back, y)
    for k in range(2):
        sent[:, 2 * k, :] = y[0:32, k * LANES : (k + 1) * LANES]
        sent[:, 2 * k + 1, :] = y[32:64, k * LANES : (k + 1) * LANES]


def third_kernel(got, sums, table, twist_cos, twist_sin, sent):
    cos, sin = twist_cos[...], twist_sin[...]
    real = jnp.concatenate([got[:, 0, :], got[:, 2, :]], axis=0)
    imag = jnp.concatenate([got[:, 1, :], got[:, 3, :]], axis=0)
    real, imag = real * cos - imag * sin, imag * cos + real * sin
    y = jnp.concatenate(
        [jnp.concatenate([real, imag], axis=1), jnp.concatenate([imag, -real], axis=1)], axis=0
    )
    sent[:, 0, :] = left_dot(table, y).astype(BF16)
    sent[:, 1, :] = jnp.broadcast_to(sums[0:1], (256, 256)).astype(BF16)


def last_kernel(scaling, got, data_grad, now_t, past_t, grad_mix, lift_t):
    value = got[:, 0, :].astype(F32)
    pair, single = value[0:32], value[128:160, 0:LANES]
    for k in range(1, 4):
        pair = pair + value[32 * k : 32 * (k + 1)]
        single = single + value[128 + 32 * k : 128 + 32 * (k + 1), 0:LANES]
    for channel, part in enumerate((pair[:, 0:LANES], pair[:, LANES:], single)):
        for piece in range(32):
            data_grad[channel : channel + 1, piece * LANES : (piece + 1) * LANES] = part[
                piece : piece + 1
            ]
    grads = got[:, 1, :].astype(F32) * scaling
    layers = (grads[0:128, 0:128], grads[128:256, 0:128], grads[0:128, 128:256])
    for layer, value in enumerate(layers):
        now_t[layer] = value[0:64]
        past_t[layer] = value[64:128]
    corner = grads[128:256, 128:256]
    turned = pltpu.roll(corner, 64, 1)
    grad_mix[0] = corner[0:64, 0:64]
    grad_mix[1] = turned[0:64, 0:64]
    grad_mix[2] = corner[64:128, 0:64]
    lift_t[...] = turned[64:67, 0:64]


def weight_kernel(bins, psd, out):
    at = bins[...]
    high = at // LANES
    low = at % LANES
    total = jnp.zeros((64, LANES), F32)
    for h in range(8):
        row = jnp.broadcast_to(psd[h : h + 1, :], (64, LANES))
        total = jnp.where(high == h, jnp.take_along_axis(row, low, axis=1), total)
    out[...] = total


def call(kernel, outs, scratch=(), smem=0, n_in=0, in_specs=None, grid=()):
    vmem = pl.BlockSpec(memory_space=pltpu.VMEM)
    if in_specs is None:
        in_specs = [pl.BlockSpec(memory_space=pltpu.SMEM)] * smem + [vmem] * n_in
    out_shape = [
        out if isinstance(out, jax.ShapeDtypeStruct) else jax.ShapeDtypeStruct(out, F32)
        for out in outs
    ]
    return pl.pallas_call(
        kernel,
        grid=grid,
        out_shape=out_shape,
        in_specs=in_specs,
        out_specs=[vmem] * len(outs),
        scratch_shapes=list(scratch),
        compiler_params=pltpu.CompilerParams(vmem_limit_bytes=56 * 1024 * 1024),
    )


def two_parts(table):
    high = table.astype(np.float32).astype(jnp.bfloat16)
    low = (table - high.astype(np.float64)).astype(np.float32).astype(jnp.bfloat16)
    return high, low


def for_left(table):
    high, low = two_parts(table)
    return np.concatenate([high, high, low], axis=-1)


def tables(rows_count, cols_count):
    n = rows_count * cols_count
    half = rows_count // 2
    h = np.arange(2 * cols_count)
    residue = rows_count * (h % cols_count) + half * (h // cols_count)
    residue = residue[None, :] + np.arange(half)[:, None]
    angle = 2.0 * np.pi / n * (residue[:, :, None] * np.arange(n)[None, None, :] % n)
    outward = np.concatenate([np.cos(angle), np.sin(angle)], axis=1)
    inward = np.swapaxes(np.concatenate([np.cos(angle), -np.sin(angle)], axis=1), 1, 2)
    outward = np.concatenate(two_parts(outward), axis=1)
    inward = for_left(inward)

    def mixing(product, size, sign):
        angle = 2.0 * np.pi / size * (product % size)
        cos, sin = np.cos(angle), sign * np.sin(angle)
        return np.block([[cos, sin], [-sin, cos]])

    c = np.arange(cols_count)
    l = np.arange(LANES)
    outer = for_left(mixing(c[:, None] * c[None, :], cols_count, 1.0))
    outer_back = for_left(
        mixing((c[:, None] + SHIFT // LANES) * c[None, :], cols_count, -1.0)
    )
    fast = np.stack(two_parts(mixing(l[:, None] * l[None, :], LANES, -1.0)))
    angle = 2.0 * np.pi / SEG * (c[:, None] * l[None, :])
    return (
        outward, inward, outer, outer_back, fast,
        np.cos(angle).astype(np.float32), np.sin(angle).astype(np.float32),
    )


def near(x):
    return pltpu.with_memory_space_constraint(x, pltpu.VMEM)


def exchange(x, axes):
    return near(lax.all_to_all(x, axes, split_axis=0, concat_axis=0, tiled=True))


def local(
    rows_count, cols_count,
    whitened, cotangent, lift_weight, conv_now, conv_past, mix_weight, dilations, psd_bin, psd_weight,
):
    n = rows_count * cols_count
    total = n * SEG
    message, = call(
        pack_kernel, [jax.ShapeDtypeStruct((96, SHIFT), BF16)], [pltpu.VMEM((32, SHIFT), F32)],
        in_specs=[
            pl.BlockSpec((64, 1024), lambda i: (0, 3)), pl.BlockSpec((3, 2048), lambda i: (0, 1)),
        ],
        grid=(1,),
    )(cotangent, whitened)
    received = near(lax.ppermute(message, BOTH, [(i, (i + 1) % n) for i in range(n)]))

    big = lambda rows, dtype: pltpu.VMEM((rows, WIDE), dtype)
    square = pltpu.VMEM((LANES, LANES), F32)
    scratch = (
        [
            pltpu.VMEM((32, SHIFT), F32), pltpu.VMEM((3, 128, 128), BF16),
            pltpu.VMEM((3, 128, 128), BF16), pltpu.VMEM((3, 64, 64), BF16), square,
            pltpu.VMEM((8, LEFT + SPAN), F32), pltpu.VMEM((64, SPAN), BF16),
        ]
        + [big(64, F32)] * 3 + [big(128, BF16)] * 2 + [big(64, F32)] * 4 + [big(64, BF16)] * 2
        + [big(64, F32)] * 4
        + [pltpu.VMEM((3, 128, 128), F32), pltpu.VMEM((3, 64, 128), F32), pltpu.VMEM((32, 384), F32)]
    )
    packed = jax.ShapeDtypeStruct((n, 2, 2 * LANES), BF16)
    sent, = call(conv_kernel, [packed], scratch, smem=1, n_in=7)(
        dilations, received, whitened, cotangent, lift_weight.T, jnp.swapaxes(conv_now, 1, 2),
        jnp.swapaxes(conv_past, 1, 2), mix_weight,
    )
    outward, inward, outer, outer_back, fast, turn_cos, turn_sin = tables(rows_count, cols_count)
    my_row, my_col, psd_bin, sent = lax.optimization_barrier(
        (lax.axis_index("rows"), lax.axis_index("cols"), psd_bin, sent)
    )
    half = rows_count // 2
    my_low, second = my_row % half, my_row >= half
    outward = lax.dynamic_index_in_dim(jnp.asarray(outward), my_low, 0, keepdims=False)
    inward = lax.dynamic_index_in_dim(jnp.asarray(inward), my_low, 0, keepdims=False)

    def twist(ahead):
        h = lax.broadcasted_iota(jnp.int32, (2 * cols_count, LANES), 0)
        residue = rows_count * (h % cols_count) + half * (h // cols_count) + my_low
        sample = lax.broadcasted_iota(jnp.int32, h.shape, 1) + LANES * (my_col + ahead)
        angle = (2.0 * math.pi / total) * ((residue * sample) % total).astype(F32)
        return jnp.cos(angle), jnp.sin(angle)

    twist_cos, twist_sin = twist(0)
    back_cos, back_sin = twist(SHIFT // LANES)

    bins = psd_bin.reshape(LANES, cols_count).T
    other = lax.ppermute(bins, "rows", [(i, (i + half) % rows_count) for i in range(rows_count)])
    bins = jnp.concatenate(
        [jnp.where(second, other, bins), jnp.where(second, bins, other)], axis=0
    )
    psd = jnp.where(second, psd_weight[1], psd_weight[0]) * (1.0 / total)
    weights = call(weight_kernel, [(2 * cols_count, LANES)], n_in=2)(bins, psd.reshape(8, LANES))[0]

    got = exchange(sent, BOTH)
    pieces = (cols_count, 4, LANES)
    sent, sums = call(first_kernel, [pieces, (8, 256)], n_in=4)(got, near(outward), near(twist_cos), near(twist_sin))
    got = exchange(sent, "cols")
    sent, = call(middle_kernel, [pieces], n_in=7)(
        got, weights, near(outer), near(fast), near(outer_back), near(turn_cos), near(turn_sin)
    )
    got = exchange(sent, "cols")
    sent, = call(third_kernel, [packed], n_in=5)(got, near(sums), near(inward), near(back_cos), near(back_sin))
    got = exchange(sent, BOTH)
    outs = [(3, SEG), (3, 64, 128), (3, 64, 128), (3, 64, 64), (3, 64)]
    data_grad, now_t, past_t, grad_mix, lift_t = call(
        functools.partial(last_kernel, total ** -0.5), outs, n_in=1
    )(got)
    return (
        data_grad, jnp.swapaxes(now_t, 1, 2), jnp.swapaxes(past_t, 1, 2), grad_mix, lift_t.T
    )


def solution(mesh):
    in_specs = (
        P(None, BOTH), P(None, BOTH), P(), P(), P(), P(), P(), P(None, "cols", "rows"), P(),
    )
    out_specs = (P(None, BOTH), P(), P(), P(), P())
    body = functools.partial(local, mesh.shape["rows"], mesh.shape["cols"])
    return jax.shard_map(body, mesh=mesh, in_specs=in_specs, out_specs=out_specs, check_vma=False)
```

```python
import functools
import math

import jax
import jax.numpy as jnp
import numpy as np
from jax import lax
from jax.experimental import pallas as pl
from jax.experimental.pallas import tpu as pltpu
from jax.sharding import PartitionSpec as P

F32 = jnp.float32
BF16 = jnp.bfloat16
BOTH = ("rows", "cols")
SEG = 4096
SHIFT = 768
LEFT = 640
SPAN = SEG + 640
BASE = 1024
WIDE = BASE + SEG + 1024
STEP = 2048
STRIDE = 2560
LANES = 128


def lane_ids(rows):
    return lax.broadcasted_iota(jnp.int32, (rows, LANES), 1)


def dot32(a, b):
    return jnp.dot(a, b, preferred_element_type=F32)


def dot_nt(a, b, precision=None):
    return lax.dot_general(
        a, b, (((1,), (1,)), ((), ())), preferred_element_type=F32, precision=precision
    )


def columns(start, width):
    if isinstance(start, int):
        return pl.ds(start, width)
    return pl.ds(pl.multiple_of(start, LANES), width)


def pack_kernel(cot, wh, out, parts):
    out[0:64] = cot[:, 256:1024]
    parts[...] = jnp.zeros_like(parts)
    for half in range(2):
        left = wh[:, 512 + half * 768 : 512 + (half + 1) * 768]
        for part in range(3):
            piece = left.astype(BF16).astype(F32)
            parts[half * 16 + part * 3 : half * 16 + part * 3 + 3] = piece
            left = left - piece
    out[64:96] = parts[...].astype(BF16)


def conv_kernel(
    dil, got, wh, cot, lift_t, now_t, past_t, mix,
    sent, parts, w_cat, w_cat_t, mix_t, square, whu, cotu,
    f0, f1, f2, x1, x2, fl1, fl2, sg1, sg2, gt1, gt2, ah, ah2, dp, dp2, g_conv, g_mix, x_t,
):
    lane = lane_ids(64)
    one_lane = lane_ids(1)
    at_start = (lax.axis_index("rows") == 0) & (lax.axis_index("cols") == 0)
    edge = jnp.where(at_start, SHIFT, 1 << 20)

    def shifted(ref, first, turn, keep_below, width):
        turned = [
            pltpu.roll(ref[:, columns(first + LANES * k, LANES)], turn, 1)
            for k in range(width // LANES + 1)
        ]
        keep = lane < keep_below
        return [jnp.where(keep, turned[k], turned[k + 1]) for k in range(width // LANES)]

    def cut(tiles, start, low, high):
        done = []
        for k, tile in enumerate(tiles):
            at = one_lane + (start - BASE + LANES * k)
            done.append(tile * jnp.where((at >= low) & (at < high), 0.0, 1.0))
        return jnp.concatenate(done, axis=1)

    def behind(ref, start, width, layer):
        d = dil[layer]
        whole = pl.multiple_of((d // LANES) * LANES, LANES)
        rest = d % LANES
        tiles = shifted(ref, start - whole - LANES, rest, rest, width)
        return cut(tiles, start, edge, edge + d)

    def beyond(ref, start, width, layer):
        d = dil[layer]
        whole = pl.multiple_of((d // LANES) * LANES, LANES)
        rest = d % LANES
        tiles = shifted(ref, start + whole, (LANES - rest) % LANES, LANES - rest, width)
        return cut(tiles, start, edge - d, edge)

    parts[...] = got[64:96].astype(F32)
    whu[...] = jnp.zeros_like(whu)
    for half in range(2):
        whole = (
            parts[half * 16 : half * 16 + 3] + parts[half * 16 + 3 : half * 16 + 6]
            + parts[half * 16 + 6 : half * 16 + 9]
        )
        if half == 0:
            whu[0:3, 0:640] = whole[:, 128:768]
        else:
            whu[0:3, 640:1408] = whole
    own = SPAN - SHIFT
    whu[0:3, 1408 : 1408 + own] = wh[:, 0:own]
    cotu[:, 0:SHIFT] = got[0:64]
    cotu[:, SHIFT:SPAN] = cot[:, 0:own]

    for layer in range(3):
        stacked = jnp.concatenate([now_t[layer], past_t[layer]], axis=0)
        w_cat_t[layer] = stacked
        w_cat[layer] = stacked.astype(F32).T.astype(BF16)
        square[...] = jnp.zeros_like(square)
        square[0:64, 0:64] = mix[layer].astype(F32)
        mix_t[layer] = square[...].T[0:64, 0:64].astype(BF16)
    square[...] = jnp.zeros_like(square)
    square[0:3, 0:64] = lift_t[...]
    lift_cols = square[...].T[0:64]
    lift_cols = [jnp.broadcast_to(lift_cols[:, i : i + 1], (64, LANES)) for i in range(3)]
    lift_8 = square[0:8, 0:64]
    lift_high = lift_8.astype(BF16)
    lift_16 = jnp.concatenate([lift_high.astype(F32), lift_8 - lift_high.astype(F32)], axis=0)
    lift_16 = lift_16.astype(BF16)

    zero_tile = jnp.zeros((64, LANES), F32)
    for k in range(3):
        f0[:, k * LANES : (k + 1) * LANES] = zero_tile
        f1[:, (k + 1) * LANES : (k + 2) * LANES] = zero_tile
        at = BASE + SPAN + k * LANES
        ah[:, at : at + LANES] = zero_tile
        ah2[:, at : at + LANES] = zero_tile
        ah2[:, at - LANES : at] = zero_tile
    f2[:, 384:512] = zero_tile
    f2[:, 512:640] = zero_tile

    def lift_step(i, carry):
        for k in range(6):
            at = (i * 6 + k) * LANES
            tile = whu[:, columns(at, LANES)]
            f0[:, columns(BASE - LEFT + at, LANES)] = (
                lift_cols[0] * tile[0:1] + lift_cols[1] * tile[1:2] + lift_cols[2] * tile[2:3]
            )
        return carry

    lax.fori_loop(0, 7, lift_step, 0)

    def gates(layer, field, start, width):
        now = field[:, columns(start, width)]
        both = jnp.concatenate(
            [now.astype(BF16), behind(field, start, width, layer).astype(BF16)], axis=0
        )
        pre = dot32(w_cat[layer], both)
        filt = jnp.tanh(pre[:64])
        sig = 0.5 * jnp.tanh(0.5 * pre[64:]) + 0.5
        gate = (filt * sig).astype(BF16)
        return now, both, filt, sig, gate

    def forward(layer, field, field_next, x, fl, sg, gt, start, width):
        now, both, filt, sig, gate = gates(layer, field, start, width)
        at = columns(start, width)
        x[:, at] = both
        fl[:, at] = filt
        sg[:, at] = sig
        gt[:, at] = gate
        field_next[:, at] = now + dot32(mix[layer], gate)

    def run_forward(layer, field, field_next, x, fl, sg, gt, start, rest):
        def step(i, carry):
            forward(layer, field, field_next, x, fl, sg, gt, start + i * STRIDE, STRIDE)
            return carry

        lax.fori_loop(0, 2, step, 0)
        if rest:
            forward(layer, field, field_next, x, fl, sg, gt, start + 2 * STRIDE, rest)

    run_forward(0, f0, f1, x1, fl1, sg1, gt1, BASE - 512, 128)
    run_forward(1, f1, f2, x2, fl2, sg2, gt2, BASE - 384, 0)

    g_conv[...] = jnp.zeros_like(g_conv)
    g_mix[...] = jnp.zeros_like(g_mix)

    def backward(layer, dfield, dfield_b, both, filt, sig, gate, ah_out, dp_out, start, width, own):
        d_gate = dot32(mix_t[layer], dfield_b)
        d_pre = jnp.concatenate(
            [d_gate * sig * (1.0 - filt * filt), d_gate * filt * sig * (1.0 - sig)], axis=0
        ).astype(BF16)
        back = dot32(w_cat_t[layer], d_pre)
        at = columns(start, width)
        dp_out[:, at] = dfield + back[:64]
        ah_out[:, at] = back[64:]
        if own:
            g_conv[layer] += dot_nt(both, d_pre)
            empty = jnp.zeros((64, width), BF16)
            placed = [empty, gate] if layer == 1 else [gate, empty]
            g_mix[layer] += dot_nt(dfield_b, jnp.concatenate(placed, axis=0))

    def last_layer(start, width, own):
        now, both, filt, sig, gate = gates(2, f2, start, width)
        dfield_b = cotu[:, columns(start - BASE, width)]
        backward(2, dfield_b.astype(F32), dfield_b, both, filt, sig, gate, ah, dp, start, width, own)

    def step3(i, carry):
        last_layer(BASE + i * STEP, STEP, True)
        return carry

    lax.fori_loop(0, SEG // STEP, step3, 0)
    last_layer(BASE + SEG, 640, False)

    def saved_layer(layer, x, fl, sg, gt, ah_in, dp_in, ah_out, dp_out, start, width, own):
        at = columns(start, width)
        dfield = dp_in[:, at] + beyond(ah_in, start, width, layer + 1)
        backward(
            layer, dfield, dfield.astype(BF16), x[:, at], fl[:, at], sg[:, at], gt[:, at],
            ah_out, dp_out, start, width, own,
        )

    def step2(i, carry):
        saved_layer(1, x2, fl2, sg2, gt2, ah, dp, ah2, dp2, BASE + i * STEP, STEP, True)
        return carry

    lax.fori_loop(0, SEG // STEP, step2, 0)
    saved_layer(1, x2, fl2, sg2, gt2, ah, dp, ah2, dp2, BASE + SEG, 512, False)

    def step1(i, carry):
        saved_layer(0, x1, fl1, sg1, gt1, ah2, dp2, ah, dp, BASE + i * STEP, STEP, True)
        return carry

    lax.fori_loop(0, SEG // STEP, step1, 0)
    saved_layer(0, x1, fl1, sg1, gt1, ah2, dp2, ah, dp, BASE + SEG, 256, False)

    g_lift = jnp.zeros((8, LANES), F32)
    blank = jnp.zeros((64, 256), BF16)
    for m in range(16):
        start = BASE + m * 256
        dfield = dp[:, start : start + 256] + beyond(ah, start, 256, 0)
        high = dfield.astype(BF16)
        low = (dfield - high.astype(F32)).astype(BF16)
        on_high = dot32(lift_16, high)
        x8 = on_high[0:8] + on_high[8:16] + dot32(lift_16, low)[0:8]
        for half in range(2):
            for channel in range(3):
                x_t[2 * m + half : 2 * m + half + 1, channel * LANES : (channel + 1) * LANES] = x8[
                    channel : channel + 1, half * LANES : (half + 1) * LANES
                ]
        seen = whu[:, LEFT + m * 256 : LEFT + (m + 1) * 256]
        seen_high = seen.astype(BF16).astype(F32)
        seen_16 = jnp.concatenate([seen_high, seen - seen_high], axis=0).astype(BF16)
        on_high = dot_nt(seen_16, jnp.concatenate([blank, high], axis=0))
        g_lift += (
            on_high[0:8] + on_high[8:16]
            + dot_nt(seen_16, jnp.concatenate([blank, low], axis=0))[0:8]
        )

    pair = x_t[:, 0:256].astype(BF16)
    single = jnp.concatenate([x_t[:, 256:384], jnp.zeros((32, LANES), F32)], axis=1).astype(BF16)
    sent[:, 0, :] = jnp.concatenate([pair] * 4 + [single] * 4, axis=0)
    corner = jnp.concatenate(
        [g_mix[0] + g_mix[1], g_mix[2, 0:8] + g_lift, g_mix[2, 8:64]], axis=0
    )
    sent[:, 1, 0:128] = jnp.concatenate([g_conv[0], g_conv[1]], axis=0).astype(BF16)
    sent[:, 1, 128:256] = jnp.concatenate([g_conv[2], corner], axis=0).astype(BF16)


def halves(value):
    high = value.astype(BF16)
    return high, (value - high.astype(F32)).astype(BF16)


def left_dot(table, value):
    high, low = halves(value)
    return dot32(table[...], jnp.concatenate([high, low, high], axis=0))


def right_dot(dot, table, value):
    high, low = halves(value)
    rows = value.shape[0]
    mixed = dot(jnp.concatenate([high, low], axis=0), table[0])
    return mixed[:rows] + mixed[rows:] + dot(high, table[1])


def first_kernel(got, table, twist_cos, twist_sin, sent, sums):
    grads = jnp.sum(got[:, 1, :].astype(F32), axis=0, keepdims=True)
    sums[...] = jnp.broadcast_to(grads, (8, 256))
    both = dot32(table[...], got[:, 0, :])
    both = both[0:128] + both[128:256]
    real = both[0:64, 0:LANES] + both[64:128, LANES:]
    imag = both[0:64, LANES:] - both[64:128, 0:LANES]
    turned_real = real * twist_cos[...] + imag * twist_sin[...]
    turned_imag = imag * twist_cos[...] - real * twist_sin[...]
    for k in range(2):
        sent[:, 2 * k, :] = turned_real[32 * k : 32 * (k + 1)]
        sent[:, 2 * k + 1, :] = turned_imag[32 * k : 32 * (k + 1)]


def middle_kernel(got, weights, outer, fast, outer_back, turn_cos, turn_sin, sent):
    pieces = [got[:, k, :] for k in range(4)]
    y = jnp.concatenate(
        [
            jnp.concatenate([pieces[0], pieces[2]], axis=1),
            jnp.concatenate([pieces[1], pieces[3]], axis=1),
        ],
        axis=0,
    )
    y = left_dot(outer, y)
    cos, sin = turn_cos[...], turn_sin[...]
    rows = []
    for k in range(2):
        real = y[0:32, k * LANES : (k + 1) * LANES]
        imag = y[32:64, k * LANES : (k + 1) * LANES]
        rows.append(jnp.concatenate([real * cos + imag * sin, imag * cos - real * sin], axis=1))
    y = right_dot(dot32, fast, jnp.concatenate(rows, axis=0))
    y = y * jnp.concatenate([weights[...], weights[...]], axis=1)
    y = right_dot(dot_nt, fast, y)
    reals, imags = [], []
    for k in range(2):
        real = y[k * 32 : (k + 1) * 32, 0:LANES]
        imag = y[k * 32 : (k + 1) * 32, LANES:]
        reals.append(real * cos - imag * sin)
        imags.append(imag * cos + real * sin)
    y = jnp.concatenate(
        [jnp.concatenate(reals, axis=1), jnp.concatenate(imags, axis=1)], axis=0
    )
    y = left_dot(outer_back, y)
    for k in range(2):
        sent[:, 2 * k, :] = y[0:32, k * LANES : (k + 1) * LANES]
        sent[:, 2 * k + 1, :] = y[32:64, k * LANES : (k + 1) * LANES]


def third_kernel(got, sums, table, twist_cos, twist_sin, sent):
    cos, sin = twist_cos[...], twist_sin[...]
    real = jnp.concatenate([got[:, 0, :], got[:, 2, :]], axis=0)
    imag = jnp.concatenate([got[:, 1, :], got[:, 3, :]], axis=0)
    real, imag = real * cos - imag * sin, imag * cos + real * sin
    y = jnp.concatenate(
        [jnp.concatenate([real, imag], axis=1), jnp.concatenate([imag, -real], axis=1)], axis=0
    )
    sent[:, 0, :] = left_dot(table, y).astype(BF16)
    sent[:, 1, :] = jnp.broadcast_to(sums[0:1], (256, 256)).astype(BF16)


def last_kernel(scaling, got, data_grad, now_t, past_t, grad_mix, lift_t):
    value = got[:, 0, :].astype(F32)
    pair, single = value[0:32], value[128:160, 0:LANES]
    for k in range(1, 4):
        pair = pair + value[32 * k : 32 * (k + 1)]
        single = single + value[128 + 32 * k : 128 + 32 * (k + 1), 0:LANES]
    for channel, part in enumerate((pair[:, 0:LANES], pair[:, LANES:], single)):
        for piece in range(32):
            data_grad[channel : channel + 1, piece * LANES : (piece + 1) * LANES] = part[
                piece : piece + 1
            ]
    grads = got[:, 1, :].astype(F32) * scaling
    layers = (grads[0:128, 0:128], grads[128:256, 0:128], grads[0:128, 128:256])
    for layer, value in enumerate(layers):
        now_t[layer] = value[0:64]
        past_t[layer] = value[64:128]
    corner = grads[128:256, 128:256]
    turned = pltpu.roll(corner, 64, 1)
    grad_mix[0] = corner[0:64, 0:64]
    grad_mix[1] = turned[0:64, 0:64]
    grad_mix[2] = corner[64:128, 0:64]
    lift_t[...] = turned[64:67, 0:64]


def weight_kernel(bins, psd, out):
    at = bins[...]
    high = at // LANES
    low = at % LANES
    total = jnp.zeros((64, LANES), F32)
    for h in range(8):
        row = jnp.broadcast_to(psd[h : h + 1, :], (64, LANES))
        total = jnp.where(high == h, jnp.take_along_axis(row, low, axis=1), total)
    out[...] = total


def call(kernel, outs, scratch=(), smem=0, n_in=0, in_specs=None, grid=()):
    vmem = pl.BlockSpec(memory_space=pltpu.VMEM)
    if in_specs is None:
        in_specs = [pl.BlockSpec(memory_space=pltpu.SMEM)] * smem + [vmem] * n_in
    out_shape = [
        jax.ShapeDtypeStruct(out, F32) if isinstance(out, tuple) else out for out in outs
    ]
    return pl.pallas_call(
        kernel,
        grid=grid,
        out_shape=out_shape,
        in_specs=in_specs,
        out_specs=[vmem] * len(outs),
        scratch_shapes=list(scratch),
        compiler_params=pltpu.CompilerParams(vmem_limit_bytes=56 * 1024 * 1024),
    )


def two_parts(table):
    high = table.astype(np.float32).astype(jnp.bfloat16)
    low = (table - high.astype(np.float64)).astype(np.float32).astype(jnp.bfloat16)
    return high, low


def for_left(table):
    high, low = two_parts(table)
    return np.concatenate([high, high, low], axis=-1)


def tables(rows_count, cols_count):
    n = rows_count * cols_count
    half = rows_count // 2
    h = np.arange(2 * cols_count)
    residue = rows_count * (h % cols_count) + half * (h // cols_count)
    residue = residue[None, :] + np.arange(half)[:, None]
    angle = 2.0 * np.pi / n * (residue[:, :, None] * np.arange(n)[None, None, :] % n)
    outward = np.concatenate([np.cos(angle), np.sin(angle)], axis=1)
    inward = np.swapaxes(np.concatenate([np.cos(angle), -np.sin(angle)], axis=1), 1, 2)
    outward = np.concatenate(two_parts(outward), axis=1)
    inward = for_left(inward)

    def mixing(product, size, sign):
        angle = 2.0 * np.pi / size * (product % size)
        cos, sin = np.cos(angle), sign * np.sin(angle)
        return np.block([[cos, sin], [-sin, cos]])

    c = np.arange(cols_count)
    l = np.arange(LANES)
    outer = for_left(mixing(c[:, None] * c[None, :], cols_count, 1.0))
    outer_back = for_left(
        mixing((c[:, None] + SHIFT // LANES) * c[None, :], cols_count, -1.0)
    )
    fast = np.stack(two_parts(mixing(l[:, None] * l[None, :], LANES, -1.0)))
    angle = 2.0 * np.pi / SEG * (c[:, None] * l[None, :])
    return (
        outward, inward, outer, outer_back, fast,
        np.cos(angle).astype(np.float32), np.sin(angle).astype(np.float32),
    )


def near(x):
    return pltpu.with_memory_space_constraint(x, pltpu.VMEM)


def exchange(x, axes):
    return near(lax.all_to_all(x, axes, split_axis=0, concat_axis=0, tiled=True))


def local(
    rows_count, cols_count,
    whitened, cotangent, lift_weight, conv_now, conv_past, mix_weight, dilations, psd_bin, psd_weight,
):
    n = rows_count * cols_count
    total = n * SEG
    message, = call(
        pack_kernel, [pltpu.VMEM((96, SHIFT), BF16)], [pltpu.VMEM((32, SHIFT), F32)],
        in_specs=[
            pl.BlockSpec((64, 1024), lambda i: (0, 3)), pl.BlockSpec((3, 2048), lambda i: (0, 1)),
        ],
        grid=(1,),
    )(cotangent, whitened)
    received = near(lax.ppermute(message, BOTH, [(i, (i + 1) % n) for i in range(n)]))

    big = lambda rows, dtype: pltpu.VMEM((rows, WIDE), dtype)
    square = pltpu.VMEM((LANES, LANES), F32)
    scratch = (
        [
            pltpu.VMEM((32, SHIFT), F32), pltpu.VMEM((3, 128, 128), BF16),
            pltpu.VMEM((3, 128, 128), BF16), pltpu.VMEM((3, 64, 64), BF16), square,
            pltpu.VMEM((8, LEFT + SPAN), F32), pltpu.VMEM((64, SPAN), BF16),
        ]
        + [big(64, F32)] * 3 + [big(128, BF16)] * 2 + [big(64, F32)] * 4 + [big(64, BF16)] * 2
        + [big(64, F32)] * 4
        + [pltpu.VMEM((3, 128, 128), F32), pltpu.VMEM((3, 64, 128), F32), pltpu.VMEM((32, 384), F32)]
    )
    packed = pltpu.VMEM((n, 2, 2 * LANES), BF16)
    sent, = call(conv_kernel, [packed], scratch, smem=1, n_in=7)(
        dilations, received, whitened, cotangent, lift_weight.T, jnp.swapaxes(conv_now, 1, 2),
        jnp.swapaxes(conv_past, 1, 2), mix_weight,
    )
    outward, inward, outer, outer_back, fast, turn_cos, turn_sin = tables(rows_count, cols_count)
    my_row, my_col, psd_bin, sent = lax.optimization_barrier(
        (lax.axis_index("rows"), lax.axis_index("cols"), psd_bin, sent)
    )
    half = rows_count // 2
    my_low, second = my_row % half, my_row >= half
    outward = lax.dynamic_index_in_dim(jnp.asarray(outward), my_low, 0, keepdims=False)
    inward = lax.dynamic_index_in_dim(jnp.asarray(inward), my_low, 0, keepdims=False)

    def twist(ahead):
        h = lax.broadcasted_iota(jnp.int32, (2 * cols_count, LANES), 0)
        residue = rows_count * (h % cols_count) + half * (h // cols_count) + my_low
        sample = lax.broadcasted_iota(jnp.int32, h.shape, 1) + LANES * (my_col + ahead)
        angle = (2.0 * math.pi / total) * ((residue * sample) % total).astype(F32)
        return jnp.cos(angle), jnp.sin(angle)

    twist_cos, twist_sin = twist(0)
    back_cos, back_sin = twist(SHIFT // LANES)

    bins = psd_bin.reshape(LANES, cols_count).T
    other = lax.ppermute(bins, "rows", [(i, (i + half) % rows_count) for i in range(rows_count)])
    bins = jnp.concatenate(
        [jnp.where(second, other, bins), jnp.where(second, bins, other)], axis=0
    )
    psd = jnp.where(second, psd_weight[1], psd_weight[0]) * (1.0 / total)
    weights = call(weight_kernel, [pltpu.VMEM((2 * cols_count, LANES), F32)], n_in=2)(bins, psd.reshape(8, LANES))[0]

    got = exchange(sent, BOTH)
    pieces = pltpu.VMEM((cols_count, 4, LANES), F32)
    sent, sums = call(first_kernel, [pieces, pltpu.VMEM((8, 256), F32)], n_in=4)(got, near(outward), near(twist_cos), near(twist_sin))
    got = exchange(sent, "cols")
    sent, = call(middle_kernel, [pieces], n_in=7)(
        got, near(weights), near(outer), near(fast), near(outer_back), near(turn_cos), near(turn_sin)
    )
    got = exchange(sent, "cols")
    sent, = call(third_kernel, [packed], n_in=5)(got, near(sums), near(inward), near(back_cos), near(back_sin))
    got = exchange(sent, BOTH)
    outs = [(3, SEG), (3, 64, 128), (3, 64, 128), (3, 64, 64), (3, 64)]
    data_grad, now_t, past_t, grad_mix, lift_t = call(
        functools.partial(last_kernel, total ** -0.5), outs, n_in=1
    )(got)
    return (
        data_grad, jnp.swapaxes(now_t, 1, 2), jnp.swapaxes(past_t, 1, 2), grad_mix, lift_t.T
    )


def solution(mesh):
    in_specs = (
        P(None, BOTH), P(None, BOTH), P(), P(), P(), P(), P(), P(None, "cols", "rows"), P(),
    )
    out_specs = (P(None, BOTH), P(), P(), P(), P())
    body = functools.partial(local, mesh.shape["rows"], mesh.shape["cols"])
    return jax.shard_map(body, mesh=mesh, in_specs=in_specs, out_specs=out_specs, check_vma=False)
```

```python
import functools
import math

import jax
import jax.numpy as jnp
import numpy as np
from jax import lax
from jax.experimental import pallas as pl
from jax.experimental.pallas import tpu as pltpu
from jax.sharding import PartitionSpec as P

F32 = jnp.float32
BF16 = jnp.bfloat16
BOTH = ("rows", "cols")
SEG = 4096
SHIFT = 768
LEFT = 640
SPAN = SEG + 640
BASE = 1024
WIDE = BASE + SEG + 1024
STEP = 2048
STRIDE = 2560
LANES = 128


def lane_ids(rows):
    return lax.broadcasted_iota(jnp.int32, (rows, LANES), 1)


def dot32(a, b):
    return jnp.dot(a, b, preferred_element_type=F32)


def dot_nt(a, b, precision=None):
    return lax.dot_general(
        a, b, (((1,), (1,)), ((), ())), preferred_element_type=F32, precision=precision
    )


def columns(start, width):
    if isinstance(start, int):
        return pl.ds(start, width)
    return pl.ds(pl.multiple_of(start, LANES), width)


def pack_kernel(cot, wh, out, parts):
    out[0:64] = cot[:, 256:1024]
    parts[...] = jnp.zeros_like(parts)
    for half in range(2):
        left = wh[:, 512 + half * 768 : 512 + (half + 1) * 768]
        for part in range(3):
            piece = left.astype(BF16).astype(F32)
            parts[half * 16 + part * 3 : half * 16 + part * 3 + 3] = piece
            left = left - piece
    out[64:96] = parts[...].astype(BF16)


def conv_kernel(
    dil, got, wh, cot, lift_t, now_t, past_t, mix,
    sent, parts, w_cat, w_cat_t, mix_t, square, whu, cotu,
    f0, f1, f2, x1, x2, fl1, fl2, sg1, sg2, gt1, gt2, ah, ah2, dp, dp2, g_conv, g_mix, x_t,
):
    lane = lane_ids(64)
    one_lane = lane_ids(1)
    at_start = (lax.axis_index("rows") == 0) & (lax.axis_index("cols") == 0)
    edge = jnp.where(at_start, SHIFT, 1 << 20)

    def shifted(ref, first, turn, keep_below, width):
        turned = [
            pltpu.roll(ref[:, columns(first + LANES * k, LANES)], turn, 1)
            for k in range(width // LANES + 1)
        ]
        keep = lane < keep_below
        return [jnp.where(keep, turned[k], turned[k + 1]) for k in range(width // LANES)]

    def cut(tiles, start, low, high):
        done = []
        for k, tile in enumerate(tiles):
            at = one_lane + (start - BASE + LANES * k)
            done.append(tile * jnp.where((at >= low) & (at < high), 0.0, 1.0))
        return jnp.concatenate(done, axis=1)

    def behind(ref, start, width, layer):
        d = dil[layer]
        whole = pl.multiple_of((d // LANES) * LANES, LANES)
        rest = d % LANES
        tiles = shifted(ref, start - whole - LANES, rest, rest, width)
        return cut(tiles, start, edge, edge + d)

    def beyond(ref, start, width, layer):
        d = dil[layer]
        whole = pl.multiple_of((d // LANES) * LANES, LANES)
        rest = d % LANES
        tiles = shifted(ref, start + whole, (LANES - rest) % LANES, LANES - rest, width)
        return cut(tiles, start, edge - d, edge)

    parts[...] = got[64:96].astype(F32)
    whu[...] = jnp.zeros_like(whu)
    for half in range(2):
        whole = (
            parts[half * 16 : half * 16 + 3] + parts[half * 16 + 3 : half * 16 + 6]
            + parts[half * 16 + 6 : half * 16 + 9]
        )
        if half == 0:
            whu[0:3, 0:640] = whole[:, 128:768]
        else:
            whu[0:3, 640:1408] = whole
    own = SPAN - SHIFT
    whu[0:3, 1408 : 1408 + own] = wh[:, 0:own]
    cotu[:, 0:SHIFT] = got[0:64]
    cotu[:, SHIFT:SPAN] = cot[:, 0:own]

    for layer in range(3):
        stacked = jnp.concatenate([now_t[layer], past_t[layer]], axis=0)
        w_cat_t[layer] = stacked
        w_cat[layer] = stacked.astype(F32).T.astype(BF16)
        square[...] = jnp.zeros_like(square)
        square[0:64, 0:64] = mix[layer].astype(F32)
        mix_t[layer] = square[...].T[0:64, 0:64].astype(BF16)
    square[...] = jnp.zeros_like(square)
    square[0:3, 0:64] = lift_t[...]
    lift_cols = square[...].T[0:64]
    lift_cols = [jnp.broadcast_to(lift_cols[:, i : i + 1], (64, LANES)) for i in range(3)]
    lift_8 = square[0:8, 0:64]
    lift_high = lift_8.astype(BF16)
    lift_16 = jnp.concatenate([lift_high.astype(F32), lift_8 - lift_high.astype(F32)], axis=0)
    lift_16 = lift_16.astype(BF16)

    zero_tile = jnp.zeros((64, LANES), F32)
    for k in range(3):
        f0[:, k * LANES : (k + 1) * LANES] = zero_tile
        f1[:, (k + 1) * LANES : (k + 2) * LANES] = zero_tile
        at = BASE + SPAN + k * LANES
        ah[:, at : at + LANES] = zero_tile
        ah2[:, at : at + LANES] = zero_tile
        ah2[:, at - LANES : at] = zero_tile
    f2[:, 384:512] = zero_tile
    f2[:, 512:640] = zero_tile

    def lift_step(i, carry):
        for k in range(6):
            at = (i * 6 + k) * LANES
            tile = whu[:, columns(at, LANES)]
            f0[:, columns(BASE - LEFT + at, LANES)] = (
                lift_cols[0] * tile[0:1] + lift_cols[1] * tile[1:2] + lift_cols[2] * tile[2:3]
            )
        return carry

    lax.fori_loop(0, 7, lift_step, 0)

    def gates(layer, field, start, width):
        now = field[:, columns(start, width)]
        both = jnp.concatenate(
            [now.astype(BF16), behind(field, start, width, layer).astype(BF16)], axis=0
        )
        pre = dot32(w_cat[layer], both)
        filt = jnp.tanh(pre[:64])
        sig = 0.5 * jnp.tanh(0.5 * pre[64:]) + 0.5
        gate = (filt * sig).astype(BF16)
        return now, both, filt, sig, gate

    def forward(layer, field, field_next, x, fl, sg, gt, start, width):
        now, both, filt, sig, gate = gates(layer, field, start, width)
        at = columns(start, width)
        x[:, at] = both
        fl[:, at] = filt
        sg[:, at] = sig
        gt[:, at] = gate
        field_next[:, at] = now + dot32(mix[layer], gate)

    def run_forward(layer, field, field_next, x, fl, sg, gt, start, rest):
        def step(i, carry):
            forward(layer, field, field_next, x, fl, sg, gt, start + i * STRIDE, STRIDE)
            return carry

        lax.fori_loop(0, 2, step, 0)
        if rest:
            forward(layer, field, field_next, x, fl, sg, gt, start + 2 * STRIDE, rest)

    run_forward(0, f0, f1, x1, fl1, sg1, gt1, BASE - 512, 128)
    run_forward(1, f1, f2, x2, fl2, sg2, gt2, BASE - 384, 0)

    g_conv[...] = jnp.zeros_like(g_conv)
    g_mix[...] = jnp.zeros_like(g_mix)

    def backward(layer, dfield, dfield_b, both, filt, sig, gate, ah_out, dp_out, start, width, own):
        d_gate = dot32(mix_t[layer], dfield_b)
        d_pre = jnp.concatenate(
            [d_gate * sig * (1.0 - filt * filt), d_gate * filt * sig * (1.0 - sig)], axis=0
        ).astype(BF16)
        back = dot32(w_cat_t[layer], d_pre)
        at = columns(start, width)
        dp_out[:, at] = dfield + back[:64]
        ah_out[:, at] = back[64:]
        if own:
            g_conv[layer] += dot_nt(both, d_pre)
            empty = jnp.zeros((64, width), BF16)
            placed = [empty, gate] if layer == 1 else [gate, empty]
            g_mix[layer] += dot_nt(dfield_b, jnp.concatenate(placed, axis=0))

    def last_layer(start, width, own):
        now, both, filt, sig, gate = gates(2, f2, start, width)
        dfield_b = cotu[:, columns(start - BASE, width)]
        backward(2, dfield_b.astype(F32), dfield_b, both, filt, sig, gate, ah, dp, start, width, own)

    def step3(i, carry):
        last_layer(BASE + i * STEP, STEP, True)
        return carry

    lax.fori_loop(0, SEG // STEP, step3, 0)
    last_layer(BASE + SEG, 640, False)

    def saved_layer(layer, x, fl, sg, gt, ah_in, dp_in, ah_out, dp_out, start, width, own):
        at = columns(start, width)
        dfield = dp_in[:, at] + beyond(ah_in, start, width, layer + 1)
        backward(
            layer, dfield, dfield.astype(BF16), x[:, at], fl[:, at], sg[:, at], gt[:, at],
            ah_out, dp_out, start, width, own,
        )

    def step2(i, carry):
        saved_layer(1, x2, fl2, sg2, gt2, ah, dp, ah2, dp2, BASE + i * STEP, STEP, True)
        return carry

    lax.fori_loop(0, SEG // STEP, step2, 0)
    saved_layer(1, x2, fl2, sg2, gt2, ah, dp, ah2, dp2, BASE + SEG, 512, False)

    def step1(i, carry):
        saved_layer(0, x1, fl1, sg1, gt1, ah2, dp2, ah, dp, BASE + i * STEP, STEP, True)
        return carry

    lax.fori_loop(0, SEG // STEP, step1, 0)
    saved_layer(0, x1, fl1, sg1, gt1, ah2, dp2, ah, dp, BASE + SEG, 256, False)

    on_high_sum = jnp.zeros((64, 16), F32)
    on_low_sum = jnp.zeros((64, 16), F32)
    for m in range(16):
        start = BASE + m * 256
        dfield = dp[:, start : start + 256] + beyond(ah, start, 256, 0)
        high = dfield.astype(BF16)
        low = (dfield - high.astype(F32)).astype(BF16)
        on_high = dot32(lift_16, high)
        x8 = on_high[0:8] + on_high[8:16] + dot32(lift_16, low)[0:8]
        for half in range(2):
            for channel in range(3):
                x_t[2 * m + half : 2 * m + half + 1, channel * LANES : (channel + 1) * LANES] = x8[
                    channel : channel + 1, half * LANES : (half + 1) * LANES
                ]
        seen = whu[:, LEFT + m * 256 : LEFT + (m + 1) * 256]
        seen_high = seen.astype(BF16).astype(F32)
        seen_16 = jnp.concatenate([seen_high, seen - seen_high], axis=0).astype(BF16)
        on_high_sum += dot_nt(high, seen_16)
        on_low_sum += dot_nt(low, seen_16)
    square[...] = jnp.zeros_like(square)
    square[64:128, 0:16] = on_high_sum
    square[64:128, 16:32] = on_low_sum
    g_lift = square[...].T
    g_lift = g_lift[0:8] + g_lift[8:16] + g_lift[16:24]

    pair = x_t[:, 0:256].astype(BF16)
    single = jnp.concatenate([x_t[:, 256:384], jnp.zeros((32, LANES), F32)], axis=1).astype(BF16)
    sent[:, 0, :] = jnp.concatenate([pair] * 4 + [single] * 4, axis=0)
    corner = jnp.concatenate(
        [g_mix[0] + g_mix[1], g_mix[2, 0:8] + g_lift, g_mix[2, 8:64]], axis=0
    )
    sent[:, 1, 0:128] = jnp.concatenate([g_conv[0], g_conv[1]], axis=0).astype(BF16)
    sent[:, 1, 128:256] = jnp.concatenate([g_conv[2], corner], axis=0).astype(BF16)


def halves(value):
    high = value.astype(BF16)
    return high, (value - high.astype(F32)).astype(BF16)


def left_dot(table, value):
    high, low = halves(value)
    return dot32(table[...], jnp.concatenate([high, low, high], axis=0))


def right_dot(dot, table, value):
    high, low = halves(value)
    rows = value.shape[0]
    mixed = dot(jnp.concatenate([high, low], axis=0), table[0])
    return mixed[:rows] + mixed[rows:] + dot(high, table[1])


def first_kernel(got, table, twist_cos, twist_sin, sent, sums):
    both = dot32(table[...], got[...].reshape(512, 256))
    sums[...] = both[256:264]
    both = both[0:128] + both[128:256]
    real = both[0:64, 0:LANES] + both[64:128, LANES:]
    imag = both[0:64, LANES:] - both[64:128, 0:LANES]
    turned_real = real * twist_cos[...] + imag * twist_sin[...]
    turned_imag = imag * twist_cos[...] - real * twist_sin[...]
    for k in range(2):
        sent[:, 2 * k, :] = turned_real[32 * k : 32 * (k + 1)]
        sent[:, 2 * k + 1, :] = turned_imag[32 * k : 32 * (k + 1)]


def middle_kernel(got, weights, outer, fast, outer_back, turn_cos, turn_sin, sent):
    pieces = [got[:, k, :] for k in range(4)]
    y = jnp.concatenate(
        [
            jnp.concatenate([pieces[0], pieces[2]], axis=1),
            jnp.concatenate([pieces[1], pieces[3]], axis=1),
        ],
        axis=0,
    )
    y = left_dot(outer, y)
    cos, sin = turn_cos[...], turn_sin[...]
    rows = []
    for k in range(2):
        real = y[0:32, k * LANES : (k + 1) * LANES]
        imag = y[32:64, k * LANES : (k + 1) * LANES]
        rows.append(jnp.concatenate([real * cos + imag * sin, imag * cos - real * sin], axis=1))
    y = right_dot(dot32, fast, jnp.concatenate(rows, axis=0))
    y = y * jnp.concatenate([weights[...], weights[...]], axis=1)
    y = right_dot(dot_nt, fast, y)
    reals, imags = [], []
    for k in range(2):
        real = y[k * 32 : (k + 1) * 32, 0:LANES]
        imag = y[k * 32 : (k + 1) * 32, LANES:]
        reals.append(real * cos - imag * sin)
        imags.append(imag * cos + real * sin)
    y = jnp.concatenate(
        [jnp.concatenate(reals, axis=1), jnp.concatenate(imags, axis=1)], axis=0
    )
    y = left_dot(outer_back, y)
    for k in range(2):
        sent[:, 2 * k, :] = y[0:32, k * LANES : (k + 1) * LANES]
        sent[:, 2 * k + 1, :] = y[32:64, k * LANES : (k + 1) * LANES]


def third_kernel(got, sums, table, twist_cos, twist_sin, sent):
    cos, sin = twist_cos[...], twist_sin[...]
    real = jnp.concatenate([got[:, 0, :], got[:, 2, :]], axis=0)
    imag = jnp.concatenate([got[:, 1, :], got[:, 3, :]], axis=0)
    real, imag = real * cos - imag * sin, imag * cos + real * sin
    y = jnp.concatenate(
        [jnp.concatenate([real, imag], axis=1), jnp.concatenate([imag, -real], axis=1)], axis=0
    )
    sent[:, 0, :] = left_dot(table, y).astype(BF16)
    sent[:, 1, :] = jnp.broadcast_to(sums[0:1], (256, 256)).astype(BF16)


def last_kernel(scaling, got, data_grad, now_t, past_t, grad_mix, lift_t):
    value = got[:, 0, :].astype(F32)
    pair, single = value[0:32], value[128:160, 0:LANES]
    for k in range(1, 4):
        pair = pair + value[32 * k : 32 * (k + 1)]
        single = single + value[128 + 32 * k : 128 + 32 * (k + 1), 0:LANES]
    for channel, part in enumerate((pair[:, 0:LANES], pair[:, LANES:], single)):
        for piece in range(32):
            data_grad[channel : channel + 1, piece * LANES : (piece + 1) * LANES] = part[
                piece : piece + 1
            ]
    grads = got[:, 1, :].astype(F32) * scaling
    layers = (grads[0:128, 0:128], grads[128:256, 0:128], grads[0:128, 128:256])
    for layer, value in enumerate(layers):
        now_t[layer] = value[0:64]
        past_t[layer] = value[64:128]
    corner = grads[128:256, 128:256]
    turned = pltpu.roll(corner, 64, 1)
    grad_mix[0] = corner[0:64, 0:64]
    grad_mix[1] = turned[0:64, 0:64]
    grad_mix[2] = corner[64:128, 0:64]
    lift_t[...] = turned[64:67, 0:64]


def weight_kernel(bins, psd, out):
    at = bins[...]
    high = at // LANES
    low = at % LANES
    total = jnp.zeros((64, LANES), F32)
    for h in range(8):
        row = jnp.broadcast_to(psd[h : h + 1, :], (64, LANES))
        total = jnp.where(high == h, jnp.take_along_axis(row, low, axis=1), total)
    out[...] = total


def call(kernel, outs, scratch=(), smem=0, n_in=0, in_specs=None, grid=()):
    vmem = pl.BlockSpec(memory_space=pltpu.VMEM)
    if in_specs is None:
        in_specs = [pl.BlockSpec(memory_space=pltpu.SMEM)] * smem + [vmem] * n_in
    out_shape = [
        jax.ShapeDtypeStruct(out, F32) if isinstance(out, tuple) else out for out in outs
    ]
    return pl.pallas_call(
        kernel,
        grid=grid,
        out_shape=out_shape,
        in_specs=in_specs,
        out_specs=[vmem] * len(outs),
        scratch_shapes=list(scratch),
        compiler_params=pltpu.CompilerParams(vmem_limit_bytes=56 * 1024 * 1024),
    )


def two_parts(table):
    high = table.astype(np.float32).astype(jnp.bfloat16)
    low = (table - high.astype(np.float64)).astype(np.float32).astype(jnp.bfloat16)
    return high, low


def for_left(table):
    high, low = two_parts(table)
    return np.concatenate([high, high, low], axis=-1)


def tables(rows_count, cols_count):
    n = rows_count * cols_count
    half = rows_count // 2
    h = np.arange(2 * cols_count)
    residue = rows_count * (h % cols_count) + half * (h // cols_count)
    residue = residue[None, :] + np.arange(half)[:, None]
    angle = 2.0 * np.pi / n * (residue[:, :, None] * np.arange(n)[None, None, :] % n)
    outward = np.concatenate([np.cos(angle), np.sin(angle)], axis=1)
    inward = np.swapaxes(np.concatenate([np.cos(angle), -np.sin(angle)], axis=1), 1, 2)
    outward = np.concatenate(two_parts(outward), axis=1)
    spread = np.zeros((half, 272, 2 * n), outward.dtype)
    spread[:, 0:256, 0::2] = outward
    spread[:, 256:264, 1::2] = 1
    inward = for_left(inward)

    def mixing(product, size, sign):
        angle = 2.0 * np.pi / size * (product % size)
        cos, sin = np.cos(angle), sign * np.sin(angle)
        return np.block([[cos, sin], [-sin, cos]])

    c = np.arange(cols_count)
    l = np.arange(LANES)
    outer = for_left(mixing(c[:, None] * c[None, :], cols_count, 1.0))
    outer_back = for_left(
        mixing((c[:, None] + SHIFT // LANES) * c[None, :], cols_count, -1.0)
    )
    fast = np.stack(two_parts(mixing(l[:, None] * l[None, :], LANES, -1.0)))
    angle = 2.0 * np.pi / SEG * (c[:, None] * l[None, :])
    return (
        spread, inward, outer, outer_back, fast,
        np.cos(angle).astype(np.float32), np.sin(angle).astype(np.float32),
    )


def near(x):
    return pltpu.with_memory_space_constraint(x, pltpu.VMEM)


def exchange(x, axes):
    return near(lax.all_to_all(x, axes, split_axis=0, concat_axis=0, tiled=True))


def local(
    rows_count, cols_count,
    whitened, cotangent, lift_weight, conv_now, conv_past, mix_weight, dilations, psd_bin, psd_weight,
):
    n = rows_count * cols_count
    total = n * SEG
    message, = call(
        pack_kernel, [pltpu.VMEM((96, SHIFT), BF16)], [pltpu.VMEM((32, SHIFT), F32)],
        in_specs=[
            pl.BlockSpec((64, 1024), lambda i: (0, 3)), pl.BlockSpec((3, 2048), lambda i: (0, 1)),
        ],
        grid=(1,),
    )(cotangent, whitened)
    received = near(lax.ppermute(message, BOTH, [(i, (i + 1) % n) for i in range(n)]))

    big = lambda rows, dtype: pltpu.VMEM((rows, WIDE), dtype)
    square = pltpu.VMEM((LANES, LANES), F32)
    scratch = (
        [
            pltpu.VMEM((32, SHIFT), F32), pltpu.VMEM((3, 128, 128), BF16),
            pltpu.VMEM((3, 128, 128), BF16), pltpu.VMEM((3, 64, 64), BF16), square,
            pltpu.VMEM((8, LEFT + SPAN), F32), pltpu.VMEM((64, SPAN), BF16),
        ]
        + [big(64, F32)] * 3 + [big(128, BF16)] * 2 + [big(64, F32)] * 4 + [big(64, BF16)] * 2
        + [big(64, F32)] * 4
        + [pltpu.VMEM((3, 128, 128), F32), pltpu.VMEM((3, 64, 128), F32), pltpu.VMEM((32, 384), F32)]
    )
    packed = pltpu.VMEM((n, 2, 2 * LANES), BF16)
    sent, = call(conv_kernel, [packed], scratch, smem=1, n_in=7)(
        dilations, received, whitened, cotangent, lift_weight.T, jnp.swapaxes(conv_now, 1, 2),
        jnp.swapaxes(conv_past, 1, 2), mix_weight,
    )
    outward, inward, outer, outer_back, fast, turn_cos, turn_sin = tables(rows_count, cols_count)
    my_row, my_col = lax.axis_index("rows"), lax.axis_index("cols")
    psd_bin, sent = lax.optimization_barrier((psd_bin, sent))
    half = rows_count // 2
    my_low, second = my_row % half, my_row >= half
    outward = lax.dynamic_index_in_dim(jnp.asarray(outward), my_low, 0, keepdims=False)
    inward = lax.dynamic_index_in_dim(jnp.asarray(inward), my_low, 0, keepdims=False)

    def twist(ahead):
        h = lax.broadcasted_iota(jnp.int32, (2 * cols_count, LANES), 0)
        residue = rows_count * (h % cols_count) + half * (h // cols_count) + my_low
        sample = lax.broadcasted_iota(jnp.int32, h.shape, 1) + LANES * (my_col + ahead)
        angle = (2.0 * math.pi / total) * ((residue * sample) % total).astype(F32)
        return jnp.cos(angle), jnp.sin(angle)

    twist_cos, twist_sin = twist(0)
    back_cos, back_sin = twist(SHIFT // LANES)

    bins = psd_bin.reshape(LANES, cols_count).T
    other = lax.ppermute(bins, "rows", [(i, (i + half) % rows_count) for i in range(rows_count)])
    bins = jnp.concatenate(
        [jnp.where(second, other, bins), jnp.where(second, bins, other)], axis=0
    )
    psd = jnp.where(second, psd_weight[1], psd_weight[0]) * (1.0 / total)
    weights = call(weight_kernel, [pltpu.VMEM((2 * cols_count, LANES), F32)], n_in=2)(bins, psd.reshape(8, LANES))[0]

    got = exchange(sent, BOTH)
    pieces = pltpu.VMEM((cols_count, 4, LANES), F32)
    sent, sums = call(first_kernel, [pieces, pltpu.VMEM((8, 256), F32)], n_in=4)(got, near(outward), near(twist_cos), near(twist_sin))
    got = exchange(sent, "cols")
    sent, = call(middle_kernel, [pieces], n_in=7)(
        got, near(weights), near(outer), near(fast), near(outer_back), near(turn_cos), near(turn_sin)
    )
    got = exchange(sent, "cols")
    sent, = call(third_kernel, [packed], n_in=5)(got, near(sums), near(inward), near(back_cos), near(back_sin))
    got = exchange(sent, BOTH)
    outs = [(3, SEG), (3, 64, 128), (3, 64, 128), (3, 64, 64), (3, 64)]
    data_grad, now_t, past_t, grad_mix, lift_t = call(
        functools.partial(last_kernel, total ** -0.5), outs, n_in=1
    )(got)
    return (
        data_grad, jnp.swapaxes(now_t, 1, 2), jnp.swapaxes(past_t, 1, 2), grad_mix, lift_t.T
    )


def solution(mesh):
    in_specs = (
        P(None, BOTH), P(None, BOTH), P(), P(), P(), P(), P(), P(None, "cols", "rows"), P(),
    )
    out_specs = (P(None, BOTH), P(), P(), P(), P())
    body = functools.partial(local, mesh.shape["rows"], mesh.shape["cols"])
    return jax.shard_map(body, mesh=mesh, in_specs=in_specs, out_specs=out_specs, check_vma=False)
```

```python
import functools
import math

import jax
import jax.numpy as jnp
import numpy as np
from jax import lax
from jax.experimental import pallas as pl
from jax.experimental.pallas import tpu as pltpu
from jax.sharding import PartitionSpec as P

F32 = jnp.float32
BF16 = jnp.bfloat16
BOTH = ("rows", "cols")
SEG = 4096
SHIFT = 768
LEFT = 640
SPAN = SEG + 640
BASE = 1024
WIDE = BASE + SEG + 1024
STEP = 2048
STRIDE = 2560
LANES = 128


def lane_ids(rows):
    return lax.broadcasted_iota(jnp.int32, (rows, LANES), 1)


def dot32(a, b):
    return jnp.dot(a, b, preferred_element_type=F32)


def dot_nt(a, b, precision=None):
    return lax.dot_general(
        a, b, (((1,), (1,)), ((), ())), preferred_element_type=F32, precision=precision
    )


def columns(start, width):
    if isinstance(start, int):
        return pl.ds(start, width)
    return pl.ds(pl.multiple_of(start, LANES), width)


def pack_kernel(cot, wh, out, parts):
    out[0:64] = cot[:, 256:1024]
    parts[...] = jnp.zeros_like(parts)
    for half in range(2):
        left = wh[:, 512 + half * 768 : 512 + (half + 1) * 768]
        for part in range(3):
            piece = left.astype(BF16).astype(F32)
            parts[half * 16 + part * 3 : half * 16 + part * 3 + 3] = piece
            left = left - piece
    out[64:96] = parts[...].astype(BF16)


def conv_kernel(
    dil, got, wh, cot, lift_t, now_t, past_t, mix,
    sent, parts, w_cat, w_cat_t, mix_t, square, whu, cotu,
    f0, f1, f2, x1, x2, fl1, fl2, sg1, sg2, gt1, gt2, ah, ah2, dp, dp2, g_conv, g_mix, x_t,
):
    lane = lane_ids(64)
    one_lane = lane_ids(1)
    at_start = (lax.axis_index("rows") == 0) & (lax.axis_index("cols") == 0)
    edge = jnp.where(at_start, SHIFT, 1 << 20)

    def shifted(ref, first, turn, keep_below, width):
        turned = [
            pltpu.roll(ref[:, columns(first + LANES * k, LANES)], turn, 1)
            for k in range(width // LANES + 1)
        ]
        keep = lane < keep_below
        return [jnp.where(keep, turned[k], turned[k + 1]) for k in range(width // LANES)]

    def cut(tiles, start, low, high):
        done = []
        for k, tile in enumerate(tiles):
            at = one_lane + (start - BASE + LANES * k)
            done.append(tile * jnp.where((at >= low) & (at < high), 0.0, 1.0))
        return jnp.concatenate(done, axis=1)

    def behind(ref, start, width, layer):
        d = dil[layer]
        whole = pl.multiple_of((d // LANES) * LANES, LANES)
        rest = d % LANES
        tiles = shifted(ref, start - whole - LANES, rest, rest, width)
        return cut(tiles, start, edge, edge + d)

    def beyond(ref, start, width, layer):
        d = dil[layer]
        whole = pl.multiple_of((d // LANES) * LANES, LANES)
        rest = d % LANES
        tiles = shifted(ref, start + whole, (LANES - rest) % LANES, LANES - rest, width)
        return cut(tiles, start, edge - d, edge)

    parts[...] = got[64:96].astype(F32)
    whu[...] = jnp.zeros_like(whu)
    for half in range(2):
        whole = (
            parts[half * 16 : half * 16 + 3] + parts[half * 16 + 3 : half * 16 + 6]
            + parts[half * 16 + 6 : half * 16 + 9]
        )
        if half == 0:
            whu[0:3, 0:640] = whole[:, 128:768]
        else:
            whu[0:3, 640:1408] = whole
    own = SPAN - SHIFT
    whu[0:3, 1408 : 1408 + own] = wh[:, 0:own]
    cotu[:, 0:SHIFT] = got[0:64]
    cotu[:, SHIFT:SPAN] = cot[:, 0:own]

    for layer in range(3):
        stacked = jnp.concatenate([now_t[layer], past_t[layer]], axis=0)
        w_cat_t[layer] = stacked
        w_cat[layer] = stacked.astype(F32).T.astype(BF16)
        square[...] = jnp.zeros_like(square)
        square[0:64, 0:64] = mix[layer].astype(F32)
        mix_t[layer] = square[...].T[0:64, 0:64].astype(BF16)
    square[...] = jnp.zeros_like(square)
    square[0:3, 0:64] = lift_t[...]
    lift_cols = square[...].T[0:64]
    lift_cols = [jnp.broadcast_to(lift_cols[:, i : i + 1], (64, LANES)) for i in range(3)]
    lift_8 = square[0:8, 0:64]
    lift_high = lift_8.astype(BF16)
    lift_16 = jnp.concatenate([lift_high.astype(F32), lift_8 - lift_high.astype(F32)], axis=0)
    lift_16 = lift_16.astype(BF16)

    zero_tile = jnp.zeros((64, LANES), F32)
    for k in range(3):
        f0[:, k * LANES : (k + 1) * LANES] = zero_tile
        f1[:, (k + 1) * LANES : (k + 2) * LANES] = zero_tile
        at = BASE + SPAN + k * LANES
        ah[:, at : at + LANES] = zero_tile
        ah2[:, at : at + LANES] = zero_tile
        ah2[:, at - LANES : at] = zero_tile
    f2[:, 384:512] = zero_tile
    f2[:, 512:640] = zero_tile

    def lift_step(i, carry):
        for k in range(6):
            at = (i * 6 + k) * LANES
            tile = whu[:, columns(at, LANES)]
            f0[:, columns(BASE - LEFT + at, LANES)] = (
                lift_cols[0] * tile[0:1] + lift_cols[1] * tile[1:2] + lift_cols[2] * tile[2:3]
            )
        return carry

    lax.fori_loop(0, 7, lift_step, 0)

    def gates(layer, field, start, width):
        now = field[:, columns(start, width)]
        both = jnp.concatenate(
            [now.astype(BF16), behind(field, start, width, layer).astype(BF16)], axis=0
        )
        pre = dot32(w_cat[layer], both)
        filt = jnp.tanh(pre[:64])
        sig = 0.5 * jnp.tanh(0.5 * pre[64:]) + 0.5
        gate = (filt * sig).astype(BF16)
        return now, both, filt, sig, gate

    def forward(layer, field, field_next, x, fl, sg, gt, start, width):
        now, both, filt, sig, gate = gates(layer, field, start, width)
        at = columns(start, width)
        x[:, at] = both
        fl[:, at] = filt
        sg[:, at] = sig
        gt[:, at] = gate
        field_next[:, at] = now + dot32(mix[layer], gate)

    def run_forward(layer, field, field_next, x, fl, sg, gt, start, rest):
        def step(i, carry):
            forward(layer, field, field_next, x, fl, sg, gt, start + i * STRIDE, STRIDE)
            return carry

        lax.fori_loop(0, 2, step, 0)
        if rest:
            forward(layer, field, field_next, x, fl, sg, gt, start + 2 * STRIDE, rest)

    run_forward(0, f0, f1, x1, fl1, sg1, gt1, BASE - 512, 128)
    run_forward(1, f1, f2, x2, fl2, sg2, gt2, BASE - 384, 0)

    g_conv[...] = jnp.zeros_like(g_conv)
    g_mix[...] = jnp.zeros_like(g_mix)

    def backward(layer, dfield, dfield_b, both, filt, sig, gate, ah_out, dp_out, start, width, own):
        d_gate = dot32(mix_t[layer], dfield_b)
        d_pre = jnp.concatenate(
            [d_gate * sig * (1.0 - filt * filt), d_gate * filt * sig * (1.0 - sig)], axis=0
        ).astype(BF16)
        back = dot32(w_cat_t[layer], d_pre)
        at = columns(start, width)
        dp_out[:, at] = dfield + back[:64]
        ah_out[:, at] = back[64:]
        if own:
            g_conv[layer] += dot_nt(both, d_pre)
            empty = jnp.zeros((64, width), BF16)
            placed = [empty, gate] if layer == 1 else [gate, empty]
            g_mix[layer] += dot_nt(dfield_b, jnp.concatenate(placed, axis=0))

    def last_layer(start, width, own):
        now, both, filt, sig, gate = gates(2, f2, start, width)
        dfield_b = cotu[:, columns(start - BASE, width)]
        backward(2, dfield_b.astype(F32), dfield_b, both, filt, sig, gate, ah, dp, start, width, own)

    def step3(i, carry):
        last_layer(BASE + i * STEP, STEP, True)
        return carry

    lax.fori_loop(0, SEG // STEP, step3, 0)
    last_layer(BASE + SEG, 640, False)

    def saved_layer(layer, x, fl, sg, gt, ah_in, dp_in, ah_out, dp_out, start, width, own):
        at = columns(start, width)
        dfield = dp_in[:, at] + beyond(ah_in, start, width, layer + 1)
        backward(
            layer, dfield, dfield.astype(BF16), x[:, at], fl[:, at], sg[:, at], gt[:, at],
            ah_out, dp_out, start, width, own,
        )

    def step2(i, carry):
        saved_layer(1, x2, fl2, sg2, gt2, ah, dp, ah2, dp2, BASE + i * STEP, STEP, True)
        return carry

    lax.fori_loop(0, SEG // STEP, step2, 0)
    saved_layer(1, x2, fl2, sg2, gt2, ah, dp, ah2, dp2, BASE + SEG, 512, False)

    def step1(i, carry):
        saved_layer(0, x1, fl1, sg1, gt1, ah2, dp2, ah, dp, BASE + i * STEP, STEP, True)
        return carry

    lax.fori_loop(0, SEG // STEP, step1, 0)
    saved_layer(0, x1, fl1, sg1, gt1, ah2, dp2, ah, dp, BASE + SEG, 256, False)

    on_high_sum = jnp.zeros((64, 16), F32)
    on_low_sum = jnp.zeros((64, 16), F32)
    for m in range(16):
        start = BASE + m * 256
        dfield = dp[:, start : start + 256] + beyond(ah, start, 256, 0)
        high = dfield.astype(BF16)
        low = (dfield - high.astype(F32)).astype(BF16)
        on_high = dot32(lift_16, high)
        x8 = on_high[0:8] + on_high[8:16] + dot32(lift_16, low)[0:8]
        for half in range(2):
            for channel in range(3):
                x_t[2 * m + half : 2 * m + half + 1, channel * LANES : (channel + 1) * LANES] = x8[
                    channel : channel + 1, half * LANES : (half + 1) * LANES
                ]
        seen = whu[:, LEFT + m * 256 : LEFT + (m + 1) * 256]
        seen_high = seen.astype(BF16).astype(F32)
        seen_16 = jnp.concatenate([seen_high, seen - seen_high], axis=0).astype(BF16)
        on_high_sum += dot_nt(high, seen_16)
        on_low_sum += dot_nt(low, seen_16)
    square[...] = jnp.zeros_like(square)
    square[64:128, 0:16] = on_high_sum
    square[64:128, 16:32] = on_low_sum
    g_lift = square[...].T
    g_lift = g_lift[0:8] + g_lift[8:16] + g_lift[16:24]

    pair = x_t[:, 0:256].astype(BF16)
    single = jnp.concatenate([x_t[:, 256:384], jnp.zeros((32, LANES), F32)], axis=1).astype(BF16)
    sent[:, 0, :] = jnp.concatenate([pair] * 4 + [single] * 4, axis=0)
    corner = jnp.concatenate(
        [g_mix[0] + g_mix[1], g_mix[2, 0:8] + g_lift, g_mix[2, 8:64]], axis=0
    )
    sent[:, 1, 0:128] = jnp.concatenate([g_conv[0], g_conv[1]], axis=0).astype(BF16)
    sent[:, 1, 128:256] = jnp.concatenate([g_conv[2], corner], axis=0).astype(BF16)


def halves(value):
    high = value.astype(BF16)
    return high, (value - high.astype(F32)).astype(BF16)


def left_dot(table, value):
    high, low = halves(value)
    return dot32(table[...], jnp.concatenate([high, low, high], axis=0))


def right_dot(dot, table, value):
    high, low = halves(value)
    rows = value.shape[0]
    mixed = dot(jnp.concatenate([high, low], axis=0), table[0])
    return mixed[:rows] + mixed[rows:] + dot(high, table[1])


def first_kernel(got, table, twist_cos, twist_sin, sent, sums):
    both = dot32(table[...], got[...].reshape(512, 256))
    sums[...] = both[256:264]
    both = both[0:128] + both[128:256]
    real = both[0:64, 0:LANES] + both[64:128, LANES:]
    imag = both[0:64, LANES:] - both[64:128, 0:LANES]
    turned_real = real * twist_cos[...] + imag * twist_sin[...]
    turned_imag = imag * twist_cos[...] - real * twist_sin[...]
    for k in range(2):
        sent[:, 2 * k, :] = turned_real[32 * k : 32 * (k + 1)]
        sent[:, 2 * k + 1, :] = turned_imag[32 * k : 32 * (k + 1)]


def middle_kernel(got, weights, outer, fast, outer_back, turn_cos, turn_sin, sent):
    pieces = [got[:, k, :] for k in range(4)]
    y = jnp.concatenate(
        [
            jnp.concatenate([pieces[0], pieces[2]], axis=1),
            jnp.concatenate([pieces[1], pieces[3]], axis=1),
        ],
        axis=0,
    )
    y = left_dot(outer, y)
    cos, sin = turn_cos[...], turn_sin[...]
    rows = []
    for k in range(2):
        real = y[0:32, k * LANES : (k + 1) * LANES]
        imag = y[32:64, k * LANES : (k + 1) * LANES]
        rows.append(jnp.concatenate([real * cos + imag * sin, imag * cos - real * sin], axis=1))
    y = right_dot(dot32, fast, jnp.concatenate(rows, axis=0))
    y = y * jnp.concatenate([weights[...], weights[...]], axis=1)
    y = right_dot(dot_nt, fast, y)
    reals, imags = [], []
    for k in range(2):
        real = y[k * 32 : (k + 1) * 32, 0:LANES]
        imag = y[k * 32 : (k + 1) * 32, LANES:]
        reals.append(real * cos - imag * sin)
        imags.append(imag * cos + real * sin)
    y = jnp.concatenate(
        [jnp.concatenate(reals, axis=1), jnp.concatenate(imags, axis=1)], axis=0
    )
    y = left_dot(outer_back, y)
    for k in range(2):
        sent[:, 2 * k, :] = y[0:32, k * LANES : (k + 1) * LANES]
        sent[:, 2 * k + 1, :] = y[32:64, k * LANES : (k + 1) * LANES]


def third_kernel(got, sums, table, twist_cos, twist_sin, sent):
    cos, sin = twist_cos[...], twist_sin[...]
    real = jnp.concatenate([got[:, 0, :], got[:, 2, :]], axis=0)
    imag = jnp.concatenate([got[:, 1, :], got[:, 3, :]], axis=0)
    real, imag = real * cos - imag * sin, imag * cos + real * sin
    y = jnp.concatenate(
        [jnp.concatenate([real, imag], axis=1), jnp.concatenate([imag, -real], axis=1)], axis=0
    )
    sent[:, 0, :] = left_dot(table, y).astype(BF16)
    sent[:, 1, :] = jnp.broadcast_to(sums[0:1], (256, 256)).astype(BF16)


def last_kernel(scaling, got, data_grad, now_t, past_t, grad_mix, lift_t):
    value = got[:, 0, :].astype(F32)
    pair, single = value[0:32], value[128:160, 0:LANES]
    for k in range(1, 4):
        pair = pair + value[32 * k : 32 * (k + 1)]
        single = single + value[128 + 32 * k : 128 + 32 * (k + 1), 0:LANES]
    for channel, part in enumerate((pair[:, 0:LANES], pair[:, LANES:], single)):
        for piece in range(32):
            data_grad[channel : channel + 1, piece * LANES : (piece + 1) * LANES] = part[
                piece : piece + 1
            ]
    grads = got[:, 1, :].astype(F32) * scaling
    layers = (grads[0:128, 0:128], grads[128:256, 0:128], grads[0:128, 128:256])
    for layer, value in enumerate(layers):
        now_t[layer] = value[0:64]
        past_t[layer] = value[64:128]
    corner = grads[128:256, 128:256]
    turned = pltpu.roll(corner, 64, 1)
    grad_mix[0] = corner[0:64, 0:64]
    grad_mix[1] = turned[0:64, 0:64]
    grad_mix[2] = corner[64:128, 0:64]
    lift_t[...] = turned[64:67, 0:64]


def weight_kernel(bins, psd, out):
    at = bins[...]
    high = at // LANES
    low = at % LANES
    total = jnp.zeros((64, LANES), F32)
    for h in range(8):
        row = jnp.broadcast_to(psd[h : h + 1, :], (64, LANES))
        total = jnp.where(high == h, jnp.take_along_axis(row, low, axis=1), total)
    out[...] = total


def call(kernel, outs, scratch=(), smem=0, n_in=0, in_specs=None, grid=()):
    vmem = pl.BlockSpec(memory_space=pltpu.VMEM)
    if in_specs is None:
        in_specs = [pl.BlockSpec(memory_space=pltpu.SMEM)] * smem + [vmem] * n_in
    out_shape = [
        jax.ShapeDtypeStruct(out, F32) if isinstance(out, tuple) else out for out in outs
    ]
    return pl.pallas_call(
        kernel,
        grid=grid,
        out_shape=out_shape,
        in_specs=in_specs,
        out_specs=[vmem] * len(outs),
        scratch_shapes=list(scratch),
        compiler_params=pltpu.CompilerParams(vmem_limit_bytes=56 * 1024 * 1024),
    )


def two_parts(table):
    high = table.astype(np.float32).astype(jnp.bfloat16)
    low = (table - high.astype(np.float64)).astype(np.float32).astype(jnp.bfloat16)
    return high, low


def for_left(table):
    high, low = two_parts(table)
    return np.concatenate([high, high, low], axis=-1)


def tables(rows_count, cols_count):
    n = rows_count * cols_count
    half = rows_count // 2
    h = np.arange(2 * cols_count)
    residue = rows_count * (h % cols_count) + half * (h // cols_count)
    residue = residue[None, :] + np.arange(half)[:, None]
    angle = 2.0 * np.pi / n * (residue[:, :, None] * np.arange(n)[None, None, :] % n)
    outward = np.concatenate([np.cos(angle), np.sin(angle)], axis=1)
    inward = np.swapaxes(np.concatenate([np.cos(angle), -np.sin(angle)], axis=1), 1, 2)
    outward = np.concatenate(two_parts(outward), axis=1)
    spread = np.zeros((half, 272, 2 * n), outward.dtype)
    spread[:, 0:256, 0::2] = outward
    spread[:, 256:264, 1::2] = 1
    inward = for_left(inward)

    def mixing(product, size, sign):
        angle = 2.0 * np.pi / size * (product % size)
        cos, sin = np.cos(angle), sign * np.sin(angle)
        return np.block([[cos, sin], [-sin, cos]])

    c = np.arange(cols_count)
    l = np.arange(LANES)
    outer = for_left(mixing(c[:, None] * c[None, :], cols_count, 1.0))
    outer_back = for_left(
        mixing((c[:, None] + SHIFT // LANES) * c[None, :], cols_count, -1.0)
    )
    fast = np.stack(two_parts(mixing(l[:, None] * l[None, :], LANES, -1.0)))
    angle = 2.0 * np.pi / SEG * (c[:, None] * l[None, :])
    return (
        spread, inward, outer, outer_back, fast,
        np.cos(angle).astype(np.float32), np.sin(angle).astype(np.float32),
    )


def near(x):
    return pltpu.with_memory_space_constraint(x, pltpu.VMEM)


def exchange(x, axes):
    return near(lax.all_to_all(x, axes, split_axis=0, concat_axis=0, tiled=True))


def local(
    rows_count, cols_count,
    whitened, cotangent, lift_weight, conv_now, conv_past, mix_weight, dilations, psd_bin, psd_weight,
):
    n = rows_count * cols_count
    total = n * SEG
    message, = call(
        pack_kernel, [pltpu.VMEM((96, SHIFT), BF16)], [pltpu.VMEM((32, SHIFT), F32)],
        in_specs=[
            pl.BlockSpec((64, 1024), lambda i: (0, 3)), pl.BlockSpec((3, 2048), lambda i: (0, 1)),
        ],
        grid=(1,),
    )(cotangent, whitened)
    received = near(lax.ppermute(message, BOTH, [(i, (i + 1) % n) for i in range(n)]))

    big = lambda rows, dtype: pltpu.VMEM((rows, WIDE), dtype)
    square = pltpu.VMEM((LANES, LANES), F32)
    scratch = (
        [
            pltpu.VMEM((32, SHIFT), F32), pltpu.VMEM((3, 128, 128), BF16),
            pltpu.VMEM((3, 128, 128), BF16), pltpu.VMEM((3, 64, 64), BF16), square,
            pltpu.VMEM((8, LEFT + SPAN), F32), pltpu.VMEM((64, SPAN), BF16),
        ]
        + [big(64, F32)] * 3 + [big(128, BF16)] * 2 + [big(64, F32)] * 4 + [big(64, BF16)] * 2
        + [big(64, F32)] * 4
        + [pltpu.VMEM((3, 128, 128), F32), pltpu.VMEM((3, 64, 128), F32), pltpu.VMEM((32, 384), F32)]
    )
    packed = pltpu.VMEM((n, 2, 2 * LANES), BF16)
    sent, = call(conv_kernel, [packed], scratch, smem=1, n_in=7)(
        dilations, received, whitened, cotangent, lift_weight.T, jnp.swapaxes(conv_now, 1, 2),
        jnp.swapaxes(conv_past, 1, 2), mix_weight,
    )
    outward, inward, outer, outer_back, fast, turn_cos, turn_sin = tables(rows_count, cols_count)
    my_row, my_col = lax.axis_index("rows"), lax.axis_index("cols")
    psd_bin, sent = lax.optimization_barrier((psd_bin, sent))
    half = rows_count // 2
    my_low, second = my_row % half, my_row >= half
    outward = lax.dynamic_index_in_dim(jnp.asarray(outward), my_low, 0, keepdims=False)
    inward = lax.dynamic_index_in_dim(jnp.asarray(inward), my_low, 0, keepdims=False)

    def twist(ahead):
        h = lax.broadcasted_iota(jnp.int32, (2 * cols_count, LANES), 0)
        residue = rows_count * (h % cols_count) + half * (h // cols_count) + my_low
        sample = lax.broadcasted_iota(jnp.int32, h.shape, 1) + LANES * (my_col + ahead)
        angle = (2.0 * math.pi / total) * ((residue * sample) % total).astype(F32)
        return jnp.cos(angle), jnp.sin(angle)

    twist_cos, twist_sin = twist(0)
    back_cos, back_sin = twist(SHIFT // LANES)

    bins = psd_bin.reshape(LANES, cols_count).T
    other = lax.ppermute(bins, "rows", [(i, (i + half) % rows_count) for i in range(rows_count)])
    got = exchange(sent, BOTH)
    pieces = pltpu.VMEM((cols_count, 4, LANES), F32)
    sent, sums = call(first_kernel, [pieces, pltpu.VMEM((8, 256), F32)], n_in=4)(got, near(outward), near(twist_cos), near(twist_sin))
    second, sent = lax.optimization_barrier((second, sent))
    bins = jnp.concatenate(
        [jnp.where(second, other, bins), jnp.where(second, bins, other)], axis=0
    )
    psd = jnp.where(second, psd_weight[1], psd_weight[0]) * (1.0 / total)
    weights = call(weight_kernel, [pltpu.VMEM((2 * cols_count, LANES), F32)], n_in=2)(bins, psd.reshape(8, LANES))[0]
    got = exchange(sent, "cols")
    sent, = call(middle_kernel, [pieces], n_in=7)(
        got, near(weights), near(outer), near(fast), near(outer_back), near(turn_cos), near(turn_sin)
    )
    got = exchange(sent, "cols")
    sent, = call(third_kernel, [packed], n_in=5)(got, near(sums), near(inward), near(back_cos), near(back_sin))
    got = exchange(sent, BOTH)
    outs = [(3, SEG), (3, 64, 128), (3, 64, 128), (3, 64, 64), (3, 64)]
    data_grad, now_t, past_t, grad_mix, lift_t = call(
        functools.partial(last_kernel, total ** -0.5), outs, n_in=1
    )(got)
    return (
        data_grad, jnp.swapaxes(now_t, 1, 2), jnp.swapaxes(past_t, 1, 2), grad_mix, lift_t.T
    )


def solution(mesh):
    in_specs = (
        P(None, BOTH), P(None, BOTH), P(), P(), P(), P(), P(), P(None, "cols", "rows"), P(),
    )
    out_specs = (P(None, BOTH), P(), P(), P(), P())
    body = functools.partial(local, mesh.shape["rows"], mesh.shape["cols"])
    return jax.shard_map(body, mesh=mesh, in_specs=in_specs, out_specs=out_specs, check_vma=False)
```

```python
import functools
import math

import jax
import jax.numpy as jnp
import numpy as np
from jax import lax
from jax.experimental import pallas as pl
from jax.experimental.pallas import tpu as pltpu
from jax.sharding import PartitionSpec as P

F32 = jnp.float32
BF16 = jnp.bfloat16
BOTH = ("rows", "cols")
SEG = 4096
SHIFT = 768
LEFT = 640
SPAN = SEG + 640
BASE = 1024
WIDE = BASE + SEG + 1024
STEP = 2048
STRIDE = 2560
LANES = 128


def lane_ids(rows):
    return lax.broadcasted_iota(jnp.int32, (rows, LANES), 1)


def dot32(a, b):
    return jnp.dot(a, b, preferred_element_type=F32)


def dot_nt(a, b, precision=None):
    return lax.dot_general(
        a, b, (((1,), (1,)), ((), ())), preferred_element_type=F32, precision=precision
    )


def columns(start, width):
    if isinstance(start, int):
        return pl.ds(start, width)
    return pl.ds(pl.multiple_of(start, LANES), width)


def pack_kernel(cot, wh, out, parts):
    out[0:64] = cot[:, 256:1024]
    parts[...] = jnp.zeros_like(parts)
    for half in range(2):
        left = wh[:, 512 + half * 768 : 512 + (half + 1) * 768]
        for part in range(3):
            piece = left.astype(BF16).astype(F32)
            parts[half * 16 + part * 3 : half * 16 + part * 3 + 3] = piece
            left = left - piece
    out[64:96] = parts[...].astype(BF16)


def conv_kernel(
    dil, got, wh, cot, lift_t, now_t, past_t, mix,
    sent, parts, w_cat, w_cat_t, mix_t, square, whu, cotu,
    f0, f1, f2, x1, x2, fl1, fl2, sg1, sg2, gt1, gt2, ah, ah2, dp, dp2, g_conv, g_mix, x_t,
):
    lane = lane_ids(64)
    one_lane = lane_ids(1)
    at_start = (lax.axis_index("rows") == 0) & (lax.axis_index("cols") == 0)
    edge = jnp.where(at_start, SHIFT, 1 << 20)

    def shifted(ref, first, turn, keep_below, width):
        turned = [
            pltpu.roll(ref[:, columns(first + LANES * k, LANES)], turn, 1)
            for k in range(width // LANES + 1)
        ]
        keep = lane < keep_below
        return [jnp.where(keep, turned[k], turned[k + 1]) for k in range(width // LANES)]

    def cut(tiles, start, low, high):
        done = []
        for k, tile in enumerate(tiles):
            at = one_lane + (start - BASE + LANES * k)
            done.append(tile * jnp.where((at >= low) & (at < high), 0.0, 1.0))
        return jnp.concatenate(done, axis=1)

    def behind(ref, start, width, layer):
        d = dil[layer]
        whole = pl.multiple_of((d // LANES) * LANES, LANES)
        rest = d % LANES
        tiles = shifted(ref, start - whole - LANES, rest, rest, width)
        return cut(tiles, start, edge, edge + d)

    def beyond(ref, start, width, layer):
        d = dil[layer]
        whole = pl.multiple_of((d // LANES) * LANES, LANES)
        rest = d % LANES
        tiles = shifted(ref, start + whole, (LANES - rest) % LANES, LANES - rest, width)
        return cut(tiles, start, edge - d, edge)

    parts[...] = got[64:96].astype(F32)
    whu[...] = jnp.zeros_like(whu)
    for half in range(2):
        whole = (
            parts[half * 16 : half * 16 + 3] + parts[half * 16 + 3 : half * 16 + 6]
            + parts[half * 16 + 6 : half * 16 + 9]
        )
        if half == 0:
            whu[0:3, 0:640] = whole[:, 128:768]
        else:
            whu[0:3, 640:1408] = whole
    own = SPAN - SHIFT
    whu[0:3, 1408 : 1408 + own] = wh[:, 0:own]
    cotu[:, 0:SHIFT] = got[0:64]
    cotu[:, SHIFT:SPAN] = cot[:, 0:own]

    for layer in range(3):
        stacked = jnp.concatenate([now_t[layer], past_t[layer]], axis=0)
        w_cat_t[layer] = stacked
        w_cat[layer] = stacked.astype(F32).T.astype(BF16)
        square[...] = jnp.zeros_like(square)
        square[0:64, 0:64] = mix[layer].astype(F32)
        mix_t[layer] = square[...].T[0:64, 0:64].astype(BF16)
    square[...] = jnp.zeros_like(square)
    square[0:3, 0:64] = lift_t[...]
    lift_cols = square[...].T[0:64]
    lift_cols = [jnp.broadcast_to(lift_cols[:, i : i + 1], (64, LANES)) for i in range(3)]
    lift_8 = square[0:8, 0:64]
    lift_high = lift_8.astype(BF16)
    lift_16 = jnp.concatenate([lift_high.astype(F32), lift_8 - lift_high.astype(F32)], axis=0)
    lift_16 = lift_16.astype(BF16)

    zero_tile = jnp.zeros((64, LANES), F32)
    for k in range(3):
        f0[:, k * LANES : (k + 1) * LANES] = zero_tile
        f1[:, (k + 1) * LANES : (k + 2) * LANES] = zero_tile
        at = BASE + SPAN + k * LANES
        ah[:, at : at + LANES] = zero_tile
        ah2[:, at : at + LANES] = zero_tile
        ah2[:, at - LANES : at] = zero_tile
    f2[:, 384:512] = zero_tile
    f2[:, 512:640] = zero_tile

    def lift_step(i, carry):
        for k in range(6):
            at = (i * 6 + k) * LANES
            tile = whu[:, columns(at, LANES)]
            f0[:, columns(BASE - LEFT + at, LANES)] = (
                lift_cols[0] * tile[0:1] + lift_cols[1] * tile[1:2] + lift_cols[2] * tile[2:3]
            )
        return carry

    lax.fori_loop(0, 7, lift_step, 0)

    def gates(layer, field, start, width):
        now = field[:, columns(start, width)]
        both = jnp.concatenate(
            [now.astype(BF16), behind(field, start, width, layer).astype(BF16)], axis=0
        )
        pre = dot32(w_cat[layer], both)
        filt = jnp.tanh(pre[:64])
        sig = 0.5 * jnp.tanh(0.5 * pre[64:]) + 0.5
        gate = (filt * sig).astype(BF16)
        return now, both, filt, sig, gate

    def forward(layer, field, field_next, x, fl, sg, gt, start, width):
        now, both, filt, sig, gate = gates(layer, field, start, width)
        at = columns(start, width)
        x[:, at] = both
        fl[:, at] = filt
        sg[:, at] = sig
        gt[:, at] = gate
        field_next[:, at] = now + dot32(mix[layer], gate)

    def run_forward(layer, field, field_next, x, fl, sg, gt, start, rest):
        def step(i, carry):
            forward(layer, field, field_next, x, fl, sg, gt, start + i * STRIDE, STRIDE)
            return carry

        lax.fori_loop(0, 2, step, 0)
        if rest:
            forward(layer, field, field_next, x, fl, sg, gt, start + 2 * STRIDE, rest)

    run_forward(0, f0, f1, x1, fl1, sg1, gt1, BASE - 512, 128)
    run_forward(1, f1, f2, x2, fl2, sg2, gt2, BASE - 384, 0)

    g_conv[...] = jnp.zeros_like(g_conv)
    g_mix[...] = jnp.zeros_like(g_mix)

    def backward(layer, dfield, dfield_b, both, filt, sig, gate, ah_out, dp_out, start, width, own):
        d_gate = dot32(mix_t[layer], dfield_b)
        d_pre = jnp.concatenate(
            [d_gate * sig * (1.0 - filt * filt), d_gate * filt * sig * (1.0 - sig)], axis=0
        ).astype(BF16)
        back = dot32(w_cat_t[layer], d_pre)
        at = columns(start, width)
        dp_out[:, at] = dfield + back[:64]
        ah_out[:, at] = back[64:]
        if own:
            g_conv[layer] += dot_nt(both, d_pre)
            empty = jnp.zeros((64, width), BF16)
            placed = [empty, gate] if layer == 1 else [gate, empty]
            g_mix[layer] += dot_nt(dfield_b, jnp.concatenate(placed, axis=0))

    def last_layer(start, width, own):
        now, both, filt, sig, gate = gates(2, f2, start, width)
        dfield_b = cotu[:, columns(start - BASE, width)]
        backward(2, dfield_b.astype(F32), dfield_b, both, filt, sig, gate, ah, dp, start, width, own)

    def step3(i, carry):
        last_layer(BASE + i * STEP, STEP, True)
        return carry

    lax.fori_loop(0, SEG // STEP, step3, 0)
    last_layer(BASE + SEG, 640, False)

    def saved_layer(layer, x, fl, sg, gt, ah_in, dp_in, ah_out, dp_out, start, width, own):
        at = columns(start, width)
        dfield = dp_in[:, at] + beyond(ah_in, start, width, layer + 1)
        backward(
            layer, dfield, dfield.astype(BF16), x[:, at], fl[:, at], sg[:, at], gt[:, at],
            ah_out, dp_out, start, width, own,
        )

    def step2(i, carry):
        saved_layer(1, x2, fl2, sg2, gt2, ah, dp, ah2, dp2, BASE + i * STEP, STEP, True)
        return carry

    lax.fori_loop(0, SEG // STEP, step2, 0)
    saved_layer(1, x2, fl2, sg2, gt2, ah, dp, ah2, dp2, BASE + SEG, 512, False)

    def step1(i, carry):
        saved_layer(0, x1, fl1, sg1, gt1, ah2, dp2, ah, dp, BASE + i * STEP, STEP, True)
        return carry

    lax.fori_loop(0, SEG // STEP, step1, 0)
    saved_layer(0, x1, fl1, sg1, gt1, ah2, dp2, ah, dp, BASE + SEG, 256, False)

    on_high_sum = jnp.zeros((64, 16), F32)
    on_low_sum = jnp.zeros((64, 16), F32)
    for m in range(16):
        start = BASE + m * 256
        dfield = dp[:, start : start + 256] + beyond(ah, start, 256, 0)
        high = dfield.astype(BF16)
        low = (dfield - high.astype(F32)).astype(BF16)
        on_high = dot32(lift_16, high)
        x8 = on_high[0:8] + on_high[8:16] + dot32(lift_16, low)[0:8]
        for half in range(2):
            for channel in range(3):
                x_t[2 * m + half : 2 * m + half + 1, channel * LANES : (channel + 1) * LANES] = x8[
                    channel : channel + 1, half * LANES : (half + 1) * LANES
                ]
        seen = whu[:, LEFT + m * 256 : LEFT + (m + 1) * 256]
        seen_high = seen.astype(BF16).astype(F32)
        seen_16 = jnp.concatenate([seen_high, seen - seen_high], axis=0).astype(BF16)
        on_high_sum += dot_nt(high, seen_16)
        on_low_sum += dot_nt(low, seen_16)
    square[...] = jnp.zeros_like(square)
    square[64:128, 0:16] = on_high_sum
    square[64:128, 16:32] = on_low_sum
    g_lift = square[...].T
    g_lift = g_lift[0:8] + g_lift[8:16] + g_lift[16:24]

    pair = x_t[:, 0:256].astype(BF16)
    single = jnp.concatenate([x_t[:, 256:384], jnp.zeros((32, LANES), F32)], axis=1).astype(BF16)
    sent[:, 0, :] = jnp.concatenate([pair] * 4 + [single] * 4, axis=0)
    corner = jnp.concatenate(
        [g_mix[0] + g_mix[1], g_mix[2, 0:8] + g_lift, g_mix[2, 8:64]], axis=0
    )
    sent[:, 1, 0:128] = jnp.concatenate([g_conv[0], g_conv[1]], axis=0).astype(BF16)
    sent[:, 1, 128:256] = jnp.concatenate([g_conv[2], corner], axis=0).astype(BF16)


def halves(value):
    high = value.astype(BF16)
    return high, (value - high.astype(F32)).astype(BF16)


def left_dot(table, value):
    high, low = halves(value)
    return dot32(table[...], jnp.concatenate([high, low, high], axis=0))


def right_dot(dot, table, value):
    high, low = halves(value)
    rows = value.shape[0]
    mixed = dot(jnp.concatenate([high, low], axis=0), table[0])
    return mixed[:rows] + mixed[rows:] + dot(high, table[1])


def first_kernel(got, table, twist_cos, twist_sin, sent, sums):
    both = dot32(table[...], got[...].reshape(512, 256))
    sums[...] = both[256:264]
    both = both[0:128] + both[128:256]
    real = both[0:64, 0:LANES] + both[64:128, LANES:]
    imag = both[0:64, LANES:] - both[64:128, 0:LANES]
    turned_real = real * twist_cos[...] + imag * twist_sin[...]
    turned_imag = imag * twist_cos[...] - real * twist_sin[...]
    for k in range(2):
        sent[:, 2 * k, :] = turned_real[32 * k : 32 * (k + 1)]
        sent[:, 2 * k + 1, :] = turned_imag[32 * k : 32 * (k + 1)]


def middle_kernel(got, weights, outer, fast, outer_back, turn_cos, turn_sin, sent):
    pieces = [got[:, k, :] for k in range(4)]
    y = jnp.concatenate(
        [
            jnp.concatenate([pieces[0], pieces[2]], axis=1),
            jnp.concatenate([pieces[1], pieces[3]], axis=1),
        ],
        axis=0,
    )
    y = left_dot(outer, y)
    cos, sin = turn_cos[...], turn_sin[...]
    rows = []
    for k in range(2):
        real = y[0:32, k * LANES : (k + 1) * LANES]
        imag = y[32:64, k * LANES : (k + 1) * LANES]
        rows.append(jnp.concatenate([real * cos + imag * sin, imag * cos - real * sin], axis=1))
    y = right_dot(dot32, fast, jnp.concatenate(rows, axis=0))
    y = y * jnp.concatenate([weights[...], weights[...]], axis=1)
    y = right_dot(dot_nt, fast, y)
    reals, imags = [], []
    for k in range(2):
        real = y[k * 32 : (k + 1) * 32, 0:LANES]
        imag = y[k * 32 : (k + 1) * 32, LANES:]
        reals.append(real * cos - imag * sin)
        imags.append(imag * cos + real * sin)
    y = jnp.concatenate(
        [jnp.concatenate(reals, axis=1), jnp.concatenate(imags, axis=1)], axis=0
    )
    y = left_dot(outer_back, y)
    for k in range(2):
        sent[:, 2 * k, :] = y[0:32, k * LANES : (k + 1) * LANES]
        sent[:, 2 * k + 1, :] = y[32:64, k * LANES : (k + 1) * LANES]


def third_kernel(got, sums, table, twist_cos, twist_sin, sent):
    cos, sin = twist_cos[...], twist_sin[...]
    real = jnp.concatenate([got[:, 0, :], got[:, 2, :]], axis=0)
    imag = jnp.concatenate([got[:, 1, :], got[:, 3, :]], axis=0)
    real, imag = real * cos - imag * sin, imag * cos + real * sin
    y = jnp.concatenate(
        [jnp.concatenate([real, imag], axis=1), jnp.concatenate([imag, -real], axis=1)], axis=0
    )
    sent[:, 0, :] = left_dot(table, y).astype(BF16)
    sent[:, 1, :] = jnp.broadcast_to(sums[0:1], (256, 256)).astype(BF16)


def last_kernel(scaling, got, data_grad, now_t, past_t, grad_mix, lift_t):
    value = got[:, 0, :].astype(F32)
    pair, single = value[0:32], value[128:160, 0:LANES]
    for k in range(1, 4):
        pair = pair + value[32 * k : 32 * (k + 1)]
        single = single + value[128 + 32 * k : 128 + 32 * (k + 1), 0:LANES]
    for channel, part in enumerate((pair[:, 0:LANES], pair[:, LANES:], single)):
        for piece in range(32):
            data_grad[channel : channel + 1, piece * LANES : (piece + 1) * LANES] = part[
                piece : piece + 1
            ]
    grads = got[:, 1, :].astype(F32) * scaling
    layers = (grads[0:128, 0:128], grads[128:256, 0:128], grads[0:128, 128:256])
    for layer, value in enumerate(layers):
        now_t[layer] = value[0:64]
        past_t[layer] = value[64:128]
    corner = grads[128:256, 128:256]
    turned = pltpu.roll(corner, 64, 1)
    grad_mix[0] = corner[0:64, 0:64]
    grad_mix[1] = turned[0:64, 0:64]
    grad_mix[2] = corner[64:128, 0:64]
    lift_t[...] = turned[64:67, 0:64]


def weight_kernel(bins, psd, out):
    at = bins[...]
    high = at // LANES
    low = at % LANES
    total = jnp.zeros((64, LANES), F32)
    for h in range(8):
        row = jnp.broadcast_to(psd[h : h + 1, :], (64, LANES))
        total = jnp.where(high == h, jnp.take_along_axis(row, low, axis=1), total)
    out[...] = total


def call(kernel, outs, scratch=(), smem=0, n_in=0, in_specs=None, grid=()):
    vmem = pl.BlockSpec(memory_space=pltpu.VMEM)
    if in_specs is None:
        in_specs = [pl.BlockSpec(memory_space=pltpu.SMEM)] * smem + [vmem] * n_in
    out_shape = [
        jax.ShapeDtypeStruct(out, F32) if isinstance(out, tuple) else out for out in outs
    ]
    return pl.pallas_call(
        kernel,
        grid=grid,
        out_shape=out_shape,
        in_specs=in_specs,
        out_specs=[vmem] * len(outs),
        scratch_shapes=list(scratch),
        compiler_params=pltpu.CompilerParams(vmem_limit_bytes=56 * 1024 * 1024),
    )


def two_parts(table):
    high = table.astype(np.float32).astype(jnp.bfloat16)
    low = (table - high.astype(np.float64)).astype(np.float32).astype(jnp.bfloat16)
    return high, low


def for_left(table):
    high, low = two_parts(table)
    return np.concatenate([high, high, low], axis=-1)


def tables(rows_count, cols_count):
    n = rows_count * cols_count
    half = rows_count // 2
    h = np.arange(2 * cols_count)
    residue = rows_count * (h % cols_count) + half * (h // cols_count)
    residue = residue[None, :] + np.arange(half)[:, None]
    angle = 2.0 * np.pi / n * (residue[:, :, None] * np.arange(n)[None, None, :] % n)
    outward = np.concatenate([np.cos(angle), np.sin(angle)], axis=1)
    inward = np.swapaxes(np.concatenate([np.cos(angle), -np.sin(angle)], axis=1), 1, 2)
    outward = np.concatenate(two_parts(outward), axis=1)
    spread = np.zeros((half, 272, 2 * n), outward.dtype)
    spread[:, 0:256, 0::2] = outward
    spread[:, 256:264, 1::2] = 1
    inward = for_left(inward)

    def mixing(product, size, sign):
        angle = 2.0 * np.pi / size * (product % size)
        cos, sin = np.cos(angle), sign * np.sin(angle)
        return np.block([[cos, sin], [-sin, cos]])

    c = np.arange(cols_count)
    l = np.arange(LANES)
    outer = for_left(mixing(c[:, None] * c[None, :], cols_count, 1.0))
    outer_back = for_left(
        mixing((c[:, None] + SHIFT // LANES) * c[None, :], cols_count, -1.0)
    )
    fast = np.stack(two_parts(mixing(l[:, None] * l[None, :], LANES, -1.0)))
    angle = 2.0 * np.pi / SEG * (c[:, None] * l[None, :])
    return (
        spread, inward, outer, outer_back, fast,
        np.cos(angle).astype(np.float32), np.sin(angle).astype(np.float32),
    )


def near(x):
    return pltpu.with_memory_space_constraint(x, pltpu.VMEM)


def exchange(x, axes):
    return near(lax.all_to_all(x, axes, split_axis=0, concat_axis=0, tiled=True))


def local(
    rows_count, cols_count,
    whitened, cotangent, lift_weight, conv_now, conv_past, mix_weight, dilations, psd_bin, psd_weight,
):
    n = rows_count * cols_count
    total = n * SEG
    message, = call(
        pack_kernel, [pltpu.VMEM((96, SHIFT), BF16)], [pltpu.VMEM((32, SHIFT), F32)],
        in_specs=[
            pl.BlockSpec((64, 1024), lambda i: (0, 3)), pl.BlockSpec((3, 2048), lambda i: (0, 1)),
        ],
        grid=(1,),
    )(cotangent, whitened)
    received = near(lax.ppermute(message, BOTH, [(i, (i + 1) % n) for i in range(n)]))

    big = lambda rows, dtype: pltpu.VMEM((rows, WIDE), dtype)
    square = pltpu.VMEM((LANES, LANES), F32)
    scratch = (
        [
            pltpu.VMEM((32, SHIFT), F32), pltpu.VMEM((3, 128, 128), BF16),
            pltpu.VMEM((3, 128, 128), BF16), pltpu.VMEM((3, 64, 64), BF16), square,
            pltpu.VMEM((8, LEFT + SPAN), F32), pltpu.VMEM((64, SPAN), BF16),
        ]
        + [big(64, F32)] * 3 + [big(128, BF16)] * 2 + [big(64, F32)] * 4 + [big(64, BF16)] * 2
        + [big(64, F32)] * 4
        + [pltpu.VMEM((3, 128, 128), F32), pltpu.VMEM((3, 64, 128), F32), pltpu.VMEM((32, 384), F32)]
    )
    packed = pltpu.VMEM((n, 2, 2 * LANES), BF16)
    sent, = call(conv_kernel, [packed], scratch, smem=1, n_in=7)(
        dilations, received, near(whitened), near(cotangent), near(lift_weight.T),
        near(jnp.swapaxes(conv_now, 1, 2)), near(jnp.swapaxes(conv_past, 1, 2)), near(mix_weight),
    )
    outward, inward, outer, outer_back, fast, turn_cos, turn_sin = tables(rows_count, cols_count)
    my_row, my_col = lax.axis_index("rows"), lax.axis_index("cols")
    psd_bin, sent = lax.optimization_barrier((psd_bin, sent))
    half = rows_count // 2
    my_low, second = my_row % half, my_row >= half
    outward = lax.dynamic_index_in_dim(jnp.asarray(outward), my_low, 0, keepdims=False)
    inward = lax.dynamic_index_in_dim(jnp.asarray(inward), my_low, 0, keepdims=False)

    def twist(ahead):
        h = lax.broadcasted_iota(jnp.int32, (2 * cols_count, LANES), 0)
        residue = rows_count * (h % cols_count) + half * (h // cols_count) + my_low
        sample = lax.broadcasted_iota(jnp.int32, h.shape, 1) + LANES * (my_col + ahead)
        angle = (2.0 * math.pi / total) * ((residue * sample) % total).astype(F32)
        return jnp.cos(angle), jnp.sin(angle)

    twist_cos, twist_sin = twist(0)
    back_cos, back_sin = twist(SHIFT // LANES)

    bins = psd_bin.reshape(LANES, cols_count).T
    other = lax.ppermute(bins, "rows", [(i, (i + half) % rows_count) for i in range(rows_count)])
    got = exchange(sent, BOTH)
    pieces = pltpu.VMEM((cols_count, 4, LANES), F32)
    sent, sums = call(first_kernel, [pieces, pltpu.VMEM((8, 256), F32)], n_in=4)(got, near(outward), near(twist_cos), near(twist_sin))
    second, sent = lax.optimization_barrier((second, sent))
    bins = jnp.concatenate(
        [jnp.where(second, other, bins), jnp.where(second, bins, other)], axis=0
    )
    psd = jnp.where(second, psd_weight[1], psd_weight[0]) * (1.0 / total)
    weights = call(weight_kernel, [pltpu.VMEM((2 * cols_count, LANES), F32)], n_in=2)(bins, psd.reshape(8, LANES))[0]
    got = exchange(sent, "cols")
    sent, = call(middle_kernel, [pieces], n_in=7)(
        got, near(weights), near(outer), near(fast), near(outer_back), near(turn_cos), near(turn_sin)
    )
    got = exchange(sent, "cols")
    sent, = call(third_kernel, [packed], n_in=5)(got, near(sums), near(inward), near(back_cos), near(back_sin))
    got = exchange(sent, BOTH)
    outs = [(3, SEG), (3, 64, 128), (3, 64, 128), (3, 64, 64), (3, 64)]
    data_grad, now_t, past_t, grad_mix, lift_t = call(
        functools.partial(last_kernel, total ** -0.5), outs, n_in=1
    )(got)
    return (
        data_grad, jnp.swapaxes(now_t, 1, 2), jnp.swapaxes(past_t, 1, 2), grad_mix, lift_t.T
    )


def solution(mesh):
    in_specs = (
        P(None, BOTH), P(None, BOTH), P(), P(), P(), P(), P(), P(None, "cols", "rows"), P(),
    )
    out_specs = (P(None, BOTH), P(), P(), P(), P())
    body = functools.partial(local, mesh.shape["rows"], mesh.shape["cols"])
    return jax.shard_map(body, mesh=mesh, in_specs=in_specs, out_specs=out_specs, check_vma=False)
```
